32 devices in a mesh: batch: 8 (over z, y), wide: 4 (over x, core).
Axes of the slice: x: 2, y: 2, z: 4, core: 2. Of those that a mesh axis runs over, the one named last changes fastest.
Arguments:
- tokens: bfloat16 [16384, 768], P(('batch', 'wide')), may hold values from -6 to 6
- block_row: int32 [128], P(('batch', 'wide')), may hold values from 0 to 3, as said below
- block_live: int32 [128], P(('batch', 'wide')), may hold values from 0 to 128, as said below
- query_weight: float32 [768, 768], P(('batch', 'wide')), may hold values from -0.21875 to 0.21875
- key_weight: float32 [768, 768], P(('batch', 'wide')), may hold values from -0.21875 to 0.21875
- value_weight: float32 [768, 768], P(('batch', 'wide')), may hold values from -0.21875 to 0.21875
- out_weight: float32 [768, 768], P(('batch', 'wide')), may hold values from -2.5 to 2.5
- position_bias: float32 [12, 1024], replicated, may hold values from -3 to 3
- features: float32 [64, 64], replicated, may hold values from -5 to 5
- up_weight: float32 [768, 3072], P('batch', 'wide'), may hold values from -0.21875 to 0.21875
- up_bias: float32 [3072], replicated, may hold values from -1.5 to 1.5
- down_weight: float32 [768, 3072], P('batch', 'wide'), may hold values from -0.109375 to 0.109375
- down_bias: float32 [768], replicated, may hold values from -1.5 to 1.5
- gain_one: float32 [768], replicated, may hold values from 0.5 to 1.5
- shift_one: float32 [768], replicated, may hold values from -1 to 1
- gain_two: float32 [768], replicated, may hold values from 0.5 to 1.5
- shift_two: float32 [768], replicated, may hold values from -1 to 1
- cotangent: bfloat16 [16384, 768], P(('batch', 'wide')), may hold values from -6 to 6
Outputs:
- out_tokens: bfloat16 [16384, 768], P(('batch', 'wide'))
- grad_tokens: float32 [16384, 768], P(('batch', 'wide'))
- grad_query_weight: float32 [768, 768], P(('batch', 'wide'))
- grad_key_weight: float32 [768, 768], P(('batch', 'wide'))
- grad_value_weight: float32 [768, 768], P(('batch', 'wide'))
- grad_out_weight: float32 [768, 768], P(('batch', 'wide'))
- grad_position_bias: float32 [12, 1024], replicated
- grad_up_weight: float32 [768, 3072], P('batch', 'wide')
- grad_up_bias: float32 [3072], replicated
- grad_down_weight: float32 [768, 3072], P('batch', 'wide')
- grad_down_bias: float32 [768], replicated
- grad_gain_one: float32 [768], replicated
- grad_shift_one: float32 [768], replicated
- grad_gain_two: float32 [768], replicated
- grad_shift_two: float32 [768], replicated
The draws below stay inside these ranges and needn't reach their ends.
Inputs may be any that keep to these rules, and one draw needn't show every extreme that they name: `block_row`: in each device's 512 // 128 entries the row numbers start at 0 and rise by one at the first block of each row; a row covers an aligned run of a power of two blocks, from one block to all of a device's blocks. `block_live`: the live tokens of a row are its first ones and more than half of its blocks' slots; a one-block row is full.
All inputs are finite; a program needn't handle non-finite values.
Results may differ from the reference program's by a relative error of at most 0.018.
Values may be sent and summed in bfloat16 or wider, within the bound.
No kernel may reach another device: no remote copies, remote signals or barrier semaphores. Data moves between devices by JAX's collectives and lax.ppermute only.
A program may use at most 192 MiB of HBM per device.

```python
from functools import partial
import jax
import jax.numpy as jnp
from jax import lax

D = 768
H = 12
DH = 64
F = 64
FF = 3072
CAP = 512
BLK = 128
TOKENS = 16384
RELS = 1024


def bucket_layout(key):
    per_device = CAP // BLK
    levels = per_device.bit_length() - 1
    device_count = TOKENS // CAP
    split_key = jax.random.fold_in(key, 11)
    length_key = jax.random.fold_in(key, 23)
    block_index = jnp.arange(per_device, dtype=jnp.int32)
    splits = (jax.random.randint(split_key, (device_count, levels, per_device), 0, 10) < 7).astype(jnp.int32)
    split_depth = jnp.zeros((device_count, per_device), jnp.int32)
    still_split = jnp.ones((device_count, per_device), jnp.int32)
    for level_index in range(levels):
        node_index = jnp.right_shift(block_index, levels - level_index)
        chosen = jnp.take(splits[:, level_index, :], node_index, axis=1)
        still_split = still_split * chosen
        split_depth = split_depth + still_split
    split_depth = split_depth.at[0].set(0).at[1].set(0).at[2].set(levels)
    span_blocks = jnp.left_shift(jnp.ones_like(split_depth), levels - split_depth)
    first_block = block_index[None, :] // span_blocks * span_blocks
    is_first = (first_block == block_index[None, :]).astype(jnp.int32)
    row_number = jnp.cumsum(is_first, axis=1) - 1
    bucket_tokens = span_blocks * BLK
    lower_bound = jnp.where(span_blocks == 1, BLK, bucket_tokens // 2 + 1)
    drawn_length = jax.random.randint(length_key, (device_count, per_device), lower_bound, bucket_tokens + 1)
    drawn_length = drawn_length.at[0].set(CAP).at[1].set(CAP // 2 + 1)
    row_length = jnp.take_along_axis(drawn_length, first_block, axis=1)
    live_count = jnp.clip(row_length - (block_index[None, :] - first_block) * BLK, 0, BLK)
    return (row_number.reshape(-1).astype(jnp.int32), live_count.reshape(-1).astype(jnp.int32))


def draw_block_row(key, part):
    return bucket_layout(key)[0]


def draw_block_live(key, part):
    return bucket_layout(key)[1]


def block_scale(key, shape, shards, least, high):
    level, own = 1.0, jax.random.fold_in(key, 6)
    for position, parts in shards:
        heights = jnp.exp(jax.random.uniform(jax.random.fold_in(own, position), (parts,), jnp.float32, least / len(shards), high / len(shards)))
        level = level * jnp.repeat(heights, shape[position] // parts).reshape([-1 if axis == position else 1 for axis in range(len(shape))])
    return level


def centred(rng, dims, deviation, reach, shards=(), held_as=jnp.bfloat16):
    drawn = deviation * jax.random.normal(rng, dims, jnp.float32)
    if shards:
        drawn = drawn * block_scale(rng, dims, shards, -0.22, 0.18)
    return jnp.clip(drawn, -reach, reach).astype(held_as)


def setup_inputs(seed: int = 0) -> dict:
    keys = jax.random.split(jax.random.key(seed), 19)
    tokens = centred(keys[0], (TOKENS, D), 1.0, 6.0, ((0, 32),))
    block_row = draw_block_row(jax.random.fold_in(keys[18], 71), 0)
    block_live = draw_block_live(jax.random.fold_in(keys[18], 71), 0)
    query_weight = centred(keys[3], (D, D), D ** -0.5, 0.21875, ((0, 32),), jnp.float32)
    key_weight = centred(keys[4], (D, D), D ** -0.5, 0.21875, ((0, 32),), jnp.float32)
    value_weight = centred(keys[5], (D, D), D ** -0.5, 0.21875, ((0, 32),), jnp.float32)
    out_weight = centred(keys[6], (D, D), (D // 128) ** -0.5, 2.5, ((0, 32),), jnp.float32)
    position_bias = centred(keys[7], (H, RELS), 0.5, 3.0, (), jnp.float32)
    features = centred(keys[8], (DH, F), 1.0, 5.0, (), jnp.float32)
    up_weight = centred(keys[9], (D, FF), D ** -0.5, 0.21875, ((0, 8), (1, 4)), jnp.float32)
    up_bias = centred(keys[10], (FF,), 0.3, 1.5, (), jnp.float32)
    down_weight = centred(keys[11], (D, FF), FF ** -0.5, 0.109375, ((0, 8), (1, 4)), jnp.float32)
    down_bias = centred(keys[12], (D,), 0.3, 1.5, (), jnp.float32)
    gain_one = jnp.clip(1.0 + 0.1 * jax.random.normal(keys[13], (D,), jnp.float32), 0.5, 1.5)
    shift_one = centred(keys[14], (D,), 0.2, 1.0, (), jnp.float32)
    gain_two = jnp.clip(1.0 + 0.1 * jax.random.normal(keys[15], (D,), jnp.float32), 0.5, 1.5)
    shift_two = centred(keys[16], (D,), 0.2, 1.0, (), jnp.float32)
    cotangent = centred(keys[17], (TOKENS, D), 1.0, 6.0, ((0, 32),))
    return dict(tokens=tokens, block_row=block_row, block_live=block_live, query_weight=query_weight, key_weight=key_weight, value_weight=value_weight, out_weight=out_weight, position_bias=position_bias, features=features, up_weight=up_weight, up_bias=up_bias, down_weight=down_weight, down_bias=down_bias, gain_one=gain_one, shift_one=shift_one, gain_two=gain_two, shift_two=shift_two, cotangent=cotangent)


@jax.custom_vjp
def low(v):
    return lax.optimization_barrier(v.astype(jnp.bfloat16)).astype(jnp.float32)

@jax.custom_vjp
def low_back(v):
    return v

def low_keep(v):
    return (low(v), None)

def low_pass(kept, grad):
    return (grad,)

def back_keep(v):
    return (v, None)

def back_low(kept, grad):
    return (low(grad),)
low.defvjp(low_keep, low_pass)
low_back.defvjp(back_keep, back_low)
eps = 1e-05
highest = lax.Precision.HIGHEST

def token_masks(block_row, block_live, width):
    blocks = block_row.shape[0]
    offsets = jnp.broadcast_to(jnp.arange(width, dtype=jnp.int32)[None, :], (blocks, width))
    row_ids = jnp.broadcast_to(block_row[:, None], (blocks, width)).reshape(-1)
    live_tok = (offsets < block_live[:, None]).astype(jnp.float32).reshape(-1)
    return (row_ids, live_tok)

def toeplitz_from(vector, length):
    flipped = vector[::-1]
    tiled_flat = jnp.broadcast_to(flipped[None, :], (length, 2 * length)).reshape(-1)
    return tiled_flat[:length * (2 * length - 1)].reshape(length, 2 * length - 1)[:, length - 1:]

def feature_map(head_part, features):
    scaled = head_part * head_part.shape[-1] ** (-0.25)
    projected = jnp.einsum('thd,df->thf', scaled, features, precision=highest)
    return jnp.exp(projected - 0.5 * lax.optimization_barrier(jnp.sum(scaled * scaled, axis=-1, keepdims=True)))

def layer_norm(residual, scale_row, shift_row):
    centered = residual - lax.optimization_barrier(jnp.mean(residual, axis=-1, keepdims=True))
    variance = lax.optimization_barrier(jnp.mean(centered * centered, axis=-1, keepdims=True))
    return centered * lax.rsqrt(variance + eps) * scale_row + shift_row

def device_layer(params, features, tokens_dev, row_ids, live_tok):
    query_low, key_low, value_low, out_low, position_bias, up_low, up_bias, down_low, down_bias, gain_one, shift_one, gain_two, shift_two = params
    length = tokens_dev.shape[0]
    head_count = position_bias.shape[0]
    head_size = features.shape[0]
    head_shape = (length, head_count, head_size)
    queries = low_back(jnp.dot(tokens_dev, query_low, precision=highest))
    key_rows = low_back(jnp.dot(tokens_dev, key_low, precision=highest))
    values = low(low_back(jnp.dot(tokens_dev, value_low, precision=highest)))
    query_phi = low(feature_map(queries.reshape(head_shape), features))
    key_phi = low(feature_map(key_rows.reshape(head_shape), features))
    scores = low_back(jnp.einsum('ihf,jhf->hij', query_phi, key_phi, precision=highest))
    same_row = (row_ids[:, None] == row_ids[None, :]).astype(jnp.float32) * live_tok[None, :]
    coupling = jax.vmap(partial(toeplitz_from, length=length))(jnp.exp(position_bias)) * same_row[None]
    weights = coupling * scores
    totals = lax.optimization_barrier(jnp.sum(weights, axis=2, keepdims=True))
    prob_low = low(weights / totals)
    mixed = jnp.einsum('hij,jhd->ihd', prob_low, values.reshape(head_shape), precision=highest)
    mixed_low = low(low_back(mixed.reshape(length, -1)))
    attention = low_back(jnp.dot(mixed_low, out_low, precision=highest))
    normed_one = layer_norm(tokens_dev + attention, gain_one, shift_one)
    hidden = low_back(jnp.dot(low(normed_one), up_low, precision=highest) + up_bias)
    activation = low(jax.nn.gelu(hidden, approximate=False))
    branch = low_back(jnp.dot(activation, down_low.T, precision=highest) + down_bias)
    return layer_norm(normed_one + branch, gain_two, shift_two) * live_tok[:, None]

def forward(tokens_all, params, features, row_ids, live_tok):
    query_weight, key_weight, value_weight, out_weight, position_bias, up_weight, up_bias, down_weight, down_bias, gain_one, shift_one, gain_two, shift_two = params
    device_params = (low(query_weight), low(key_weight), low(value_weight), low(out_weight), position_bias, low(up_weight), up_bias, low(down_weight), down_bias, gain_one, shift_one, gain_two, shift_two)
    run_device = jax.checkpoint(device_layer)

    def device_step(carry, item):
        tokens_dev, rows_dev, live_dev = item
        return (carry, run_device(device_params, features, tokens_dev, rows_dev, live_dev))
    _, outputs = lax.scan(device_step, None, (tokens_all, row_ids, live_tok))
    return outputs

def reference(tokens, block_row, block_live, query_weight, key_weight, value_weight, out_weight, position_bias, features, up_weight, up_bias, down_weight, down_bias, gain_one, shift_one, gain_two, shift_two, cotangent):
    device_count = TOKENS // CAP
    row_ids, live_tok = token_masks(block_row, block_live, BLK)
    row_ids = row_ids.reshape(device_count, CAP)
    live_tok = live_tok.reshape(device_count, CAP)
    tokens_all = tokens.astype(jnp.float32).reshape(device_count, CAP, D)
    params = (query_weight, key_weight, value_weight, out_weight, position_bias, up_weight, up_bias, down_weight, down_bias, gain_one, shift_one, gain_two, shift_two)
    run_all = partial(forward, features=features, row_ids=row_ids, live_tok=live_tok)
    outputs, pullback = jax.vjp(run_all, tokens_all, params)
    grad_all, grads = pullback(cotangent.astype(jnp.float32).reshape(device_count, CAP, D))
    grad_query, grad_key, grad_value, grad_out, grad_bias, grad_up, grad_up_bias, grad_down, grad_down_bias, grad_gain_one, grad_shift_one, grad_gain_two, grad_shift_two = grads
    return (outputs.reshape(TOKENS, D).astype(jnp.bfloat16), grad_all.reshape(TOKENS, D), grad_query, grad_key, grad_value, grad_out, grad_bias, grad_up, grad_up_bias, grad_down, grad_down_bias, grad_gain_one, grad_shift_one, grad_gain_two, grad_shift_two)
```

```python
from functools import partial

import jax
import jax.numpy as jnp
from jax import lax
from jax.experimental import pallas as pl
from jax.experimental.pallas import tpu as pltpu
from jax.sharding import PartitionSpec as P

BLK = 128
f32 = jnp.float32
bf16 = jnp.bfloat16
nt_dims = (((1,), (1,)), ((), ()))


def dot(a, b):
    return jnp.dot(a, b, preferred_element_type=f32)


def dot_nt(a, b):
    return lax.dot_general(a, b, nt_dims, preferred_element_type=f32)


def split_low(x):
    high = x.astype(bf16)
    return high, (x - high.astype(f32)).astype(bf16)


def toeplitz_kernel(bias_ref, out_ref):
    heads = bias_ref.shape[0]
    rels = bias_ref.shape[1]
    for h in range(heads):
        row = jnp.broadcast_to(jnp.exp(bias_ref[h : h + 1, :]), (BLK, rels))
        out_ref[h] = pltpu.roll(row, rels - BLK + 1, 1, stride=1, stride_axis=0)


def toeplitz_tables(flipped_bias):
    heads, rels = flipped_bias.shape
    step = 2
    return pl.pallas_call(
        toeplitz_kernel,
        grid=(heads // step,),
        in_specs=[pl.BlockSpec((None, step, rels), lambda h: (h, 0, 0))],
        out_specs=pl.BlockSpec((step, BLK, rels), lambda h: (h, 0, 0)),
        out_shape=jax.ShapeDtypeStruct((heads, BLK, rels), f32),
        name="toeplitz",
    )(flipped_bias.reshape(heads // step, step, rels))


def pair_features(u, feat_ref):
    high, low = split_low(u)
    projected = dot(jnp.concatenate([high, high, low], axis=1), feat_ref[...])
    size = u.shape[1] // 2
    square = u * u
    norm_a = jnp.sum(square[:, :size], axis=1, keepdims=True)
    norm_b = jnp.sum(square[:, size:], axis=1, keepdims=True)
    lane = lax.broadcasted_iota(jnp.int32, u.shape, 1)
    norm = jnp.where(lane < size, norm_a, norm_b)
    return jnp.exp(projected - 0.5 * norm)


def attend_kernel(
    scale, tok_ref, w_ref, table_ref, mask_ref, feat_ref, mixed_ref, u_ref, phi_ref, val_ref
):
    length = tok_ref.shape[0]
    pair = mixed_ref.shape[1]
    size = pair // 2
    blocks = length // BLK
    qkv = dot(tok_ref[...], w_ref[...])
    uq = qkv[:, :pair] * scale
    uk = qkv[:, pair : 2 * pair] * scale
    value = qkv[:, 2 * pair :].astype(bf16)
    pq = pair_features(uq, feat_ref)
    pk = pair_features(uk, feat_ref)
    u_ref[:, :pair] = uq
    u_ref[:, pair:] = uk
    phi_ref[:, :pair] = pq
    phi_ref[:, pair:] = pk
    val_ref[...] = value
    pq = pq.astype(bf16)
    pk = pk.astype(bf16)
    for h in range(2):
        cols = slice(h * size, (h + 1) * size)
        key = pk[:, cols]
        val = value[:, cols]
        for b in range(blocks):
            rows = slice(b * BLK, (b + 1) * BLK)
            start = (blocks - 1 - b) * BLK
            scores = dot_nt(pq[rows, cols], key)
            weights = table_ref[h, :, start : start + length] * mask_ref[b : b + 1, :] * scores
            total = jnp.sum(weights, axis=1, keepdims=True)
            probs = (weights * (1.0 / total)).astype(bf16)
            mixed_ref[rows, cols] = dot(probs, val).astype(bf16)


def attend(tokens, weights, tables, mask, feat_split, heads):
    length, width = tokens.shape
    pair = 2 * width // heads
    pairs = heads // 2
    rels = tables.shape[2]
    scale = float((pair // 2) ** (-0.25))
    whole = lambda shape: pl.BlockSpec(shape, lambda h: (0,) * len(shape))
    column = lambda cols: pl.BlockSpec((length, cols), lambda h: (0, h))
    return pl.pallas_call(
        partial(attend_kernel, scale),
        grid=(pairs,),
        in_specs=[
            whole((length, width)),
            pl.BlockSpec((width, 3 * pair), lambda h: (0, h)),
            pl.BlockSpec((2, BLK, rels), lambda h: (h, 0, 0)),
            whole(mask.shape),
            whole(feat_split.shape),
        ],
        out_specs=[column(pair), column(2 * pair), column(2 * pair), column(pair)],
        out_shape=[
            jax.ShapeDtypeStruct((length, width), bf16),
            jax.ShapeDtypeStruct((length, 2 * width), f32),
            jax.ShapeDtypeStruct((length, 2 * width), f32),
            jax.ShapeDtypeStruct((length, width), bf16),
        ],
        name="attend",
    )(tokens, weights, tables, mask, feat_split)


def pair_backward(scale, grad_phi, phi, u, feat_ref):
    gp = grad_phi * phi
    high, low = split_low(gp)
    back = dot(jnp.concatenate([high, high, low], axis=1), feat_ref[...])
    size = u.shape[1] // 2
    sum_a = jnp.sum(gp[:, :size], axis=1, keepdims=True)
    sum_b = jnp.sum(gp[:, size:], axis=1, keepdims=True)
    lane = lax.broadcasted_iota(jnp.int32, u.shape, 1)
    return (scale * (back - u * jnp.where(lane < size, sum_a, sum_b))).astype(bf16)


def attend_back_kernel(
    scale,
    tok_t_ref,
    w_ref,
    table_ref,
    mask_ref,
    feat_ref,
    u_ref,
    phi_ref,
    val_ref,
    ga_ref,
    wo_ref,
    grad_one_ref,
    dw_ref,
    dbias_ref,
    gtok_ref,
    diag_ref,
):
    length, pair = val_ref.shape
    size = pair // 2
    blocks = length // BLK
    rels = table_ref.shape[2]

    @pl.when(pl.program_id(0) == 0)
    def _():
        gtok_ref[...] = grad_one_ref[...]

    gm = dot_nt(ga_ref[...], wo_ref[...]).astype(bf16)
    gm_t = gm.astype(f32).T.astype(bf16)
    phi = phi_ref[...]
    pq32, pk32 = phi[:, :pair], phi[:, pair:]
    pq = pq32.astype(bf16)
    pk = pk32.astype(bf16)
    pq_t = pq32.T.astype(bf16)
    value = val_ref[...]
    gq_heads = []
    gk_heads = []
    gv_heads = []
    for h in range(2):
        cols = slice(h * size, (h + 1) * size)
        key = pk[:, cols]
        val = value[:, cols]
        diag_ref[...] = jnp.zeros_like(diag_ref)
        gq_rows = []
        gk_t = None
        gv_t = None
        for b in range(blocks):
            rows = slice(b * BLK, (b + 1) * BLK)
            start = (blocks - 1 - b) * BLK
            window = slice(start, start + length)
            scores = dot_nt(pq[rows, cols], key)
            coupling = table_ref[h, :, window] * mask_ref[b : b + 1, :]
            weights = coupling * scores
            inverse = 1.0 / jnp.sum(weights, axis=1, keepdims=True)
            shares = weights * inverse
            grad_probs = dot_nt(gm[rows, cols], val)
            inner = jnp.sum(grad_probs * shares, axis=1, keepdims=True)
            grad_weights = (grad_probs - inner) * inverse
            diag_ref[:, window] += grad_weights * weights
            grad_scores = (grad_weights * coupling).astype(bf16)
            probs = shares.astype(bf16)
            gq_rows.append(dot(grad_scores, key))
            gk_part = dot(pq_t[cols, rows], grad_scores)
            gv_part = dot(gm_t[cols, rows], probs)
            gk_t = gk_part if gk_t is None else gk_t + gk_part
            gv_t = gv_part if gv_t is None else gv_t + gv_part
        gq_heads.append(jnp.concatenate(gq_rows, axis=0))
        gk_heads.append(gk_t)
        gv_heads.append(gv_t)
        folded = diag_ref[...]
        half = BLK // 2
        while half >= 1:
            folded = pltpu.roll(folded[:half], half, 1) + folded[half:]
            half //= 2
        dbias_ref[h : h + 1, :] = folded
    gq = jnp.concatenate(gq_heads, axis=1)
    gk = jnp.concatenate(gk_heads, axis=0).T
    gv = jnp.concatenate(gv_heads, axis=0).T.astype(bf16)
    u = u_ref[...]
    dq = pair_backward(scale, gq, pq32, u[:, :pair], feat_ref)
    dk = pair_backward(scale, gk, pk32, u[:, pair:], feat_ref)
    dqkv = jnp.concatenate([dq, dk, gv], axis=1)
    dw_ref[...] = dot(tok_t_ref[...], dqkv).astype(dw_ref.dtype)
    gtok_ref[...] += dot_nt(dqkv, w_ref[...])


def attend_back(
    tokens_t, weights, tables, mask, feat_back, u, phi, value, grad_attention, grad_one, heads
):
    width, length = tokens_t.shape
    pair = 2 * width // heads
    pairs = heads // 2
    rels = tables.shape[2]
    scale = float((pair // 2) ** (-0.25))
    whole = lambda shape: pl.BlockSpec(shape, lambda h: (0,) * len(shape))
    column = lambda rows, cols: pl.BlockSpec((rows, cols), lambda h: (0, h))
    dw, dbias, gtok = pl.pallas_call(
        partial(attend_back_kernel, scale),
        grid=(pairs,),
        in_specs=[
            whole((width, length)),
            column(width, 3 * pair),
            pl.BlockSpec((2, BLK, rels), lambda h: (h, 0, 0)),
            whole(mask.shape),
            whole(feat_back.shape),
            column(length, 2 * pair),
            column(length, 2 * pair),
            column(length, pair),
            whole((length, width)),
            pl.BlockSpec((pair, width), lambda h: (h, weights.shape[1] // width - 1)),
            whole((length, width)),
        ],
        out_specs=[
            column(width, 3 * pair),
            pl.BlockSpec((None, 2, rels), lambda h: (h, 0, 0)),
            whole((length, width)),
        ],
        out_shape=[
            jax.ShapeDtypeStruct((width, 3 * width), bf16),
            jax.ShapeDtypeStruct((pairs, 2, rels), f32),
            jax.ShapeDtypeStruct((length, width), f32),
        ],
        scratch_shapes=[pltpu.VMEM((BLK, rels), f32)],
        name="attend_back",
    )(
        tokens_t, weights, tables, mask, feat_back, u, phi, value, grad_attention, weights, grad_one
    )
    return dw, dbias.reshape(heads, rels), gtok


def block_diagonal(matrix):
    zero = jnp.zeros_like(matrix)
    return jnp.concatenate(
        [jnp.concatenate([matrix, zero], axis=1), jnp.concatenate([zero, matrix], axis=1)], axis=0
    )


def split_rows(matrix):
    high, low = split_low(matrix)
    return jnp.concatenate([high, low, high], axis=0)


root_half = 0.7071067811865476
inv_root_two_pi = 0.3989422804014327
eps = 1e-05


def norm_stats(residual):
    centered = residual - jnp.mean(residual, axis=1, keepdims=True)
    inverse = lax.rsqrt(jnp.mean(centered * centered, axis=1, keepdims=True) + eps)
    return centered * inverse, inverse


def norm_back(grad, xhat, inverse, gain):
    scaled = grad * gain
    mean_grad = jnp.mean(scaled, axis=1, keepdims=True)
    mean_dot = jnp.mean(scaled * xhat, axis=1, keepdims=True)
    return (scaled - mean_grad - xhat * mean_dot) * inverse


def column_sum(x):
    return jnp.sum(x, axis=0, keepdims=True)


def ffn_kernel(
    rows_up,
    tok_ref,
    mixed_ref,
    wo_ref,
    w_ref,
    up_bias_ref,
    vec_ref,
    live_ref,
    cot_ref,
    out_ref,
    grad_one_ref,
    grad_att_ref,
    dw_ref,
    dup_bias_ref,
    dvec_ref,
    normed_ref,
    low_ref,
    low_t_ref,
    xhat_ref,
    inv_ref,
    act_ref,
    slope_ref,
    acc_ref,
    grad_two_ref,
    gb_ref,
    gb_t_ref,
):
    phase = pl.program_id(0)
    part = pl.program_id(1)
    parts = pl.num_programs(1)
    length, width = tok_ref.shape
    hidden = w_ref.shape[2]
    chunk = 256 if hidden % 256 == 0 else hidden
    chunks = [slice(k, k + chunk) for k in range(0, hidden, chunk)]
    vec = vec_ref[...]
    down_bias, gain_one, shift_one, gain_two, shift_two = (vec[i : i + 1] for i in range(5))

    @pl.when((phase == 0) & (part == 0))
    def _():
        residual = tok_ref[...].astype(f32) + dot(mixed_ref[...], wo_ref[...])
        xhat, inverse = norm_stats(residual)
        normed = xhat * gain_one + shift_one
        xhat_ref[...] = xhat
        inv_ref[...] = inverse
        normed_ref[...] = normed
        low_ref[...] = normed.astype(bf16)
        low_t_ref[...] = normed.T.astype(bf16)
        acc_ref[...] = jnp.zeros_like(acc_ref)

    @pl.when(phase == 0)
    def _():
        for cols in chunks:
            up = w_ref[:, :rows_up, cols].reshape(width, chunk)
            down = w_ref[:, rows_up:, cols].reshape(width, chunk)
            v = dot(low_ref[...], up) + up_bias_ref[:, cols]
            half = 0.5 + 0.5 * lax.erf(v * root_half)
            act = (v * half).astype(bf16)
            act_ref[part, :, cols] = act
            slope_ref[part, :, cols] = half + v * (jnp.exp(-0.5 * v * v) * inv_root_two_pi)
            acc_ref[...] += dot_nt(act, down)

    @pl.when((phase == 0) & (part == parts - 1))
    def _():
        live = live_ref[...]
        xhat, inverse = norm_stats(normed_ref[...] + (acc_ref[...] + down_bias))
        out_ref[...] = ((xhat * gain_two + shift_two) * live).astype(bf16)
        grad = cot_ref[...].astype(f32) * live
        grad_two = norm_back(grad, xhat, inverse, gain_two)
        low = grad_two.astype(bf16)
        grad_two_ref[...] = grad_two
        gb_ref[...] = low
        gb_t_ref[...] = grad_two.T.astype(bf16)
        dvec_ref[0:1, :] = column_sum(low.astype(f32))
        dvec_ref[3:4, :] = column_sum(grad * xhat)
        dvec_ref[4:5, :] = column_sum(grad)
        acc_ref[...] = grad_two

    @pl.when(phase == 1)
    def _():
        for cols in chunks:
            up = w_ref[:, :rows_up, cols].reshape(width, chunk)
            down = w_ref[:, rows_up:, cols].reshape(width, chunk)
            grad_act = dot(gb_ref[...], down)
            grad_hidden = (grad_act * slope_ref[part, :, cols]).astype(bf16)
            dup_bias_ref[:, cols] = column_sum(grad_hidden.astype(f32))
            d_up = dot(low_t_ref[...], grad_hidden).astype(bf16)
            d_down = dot(gb_t_ref[...], act_ref[part, :, cols]).astype(bf16)
            dw_ref[:, :rows_up, cols] = d_up.reshape(-1, rows_up, chunk)
            dw_ref[:, rows_up:, cols] = d_down.reshape(-1, rows_up, chunk)
            acc_ref[...] += dot_nt(grad_hidden, up)

    @pl.when((phase == 1) & (part == parts - 1))
    def _():
        grad = acc_ref[...]
        xhat = xhat_ref[...]
        grad_one = norm_back(grad, xhat, inv_ref[...], gain_one)
        grad_one_ref[...] = grad_one
        grad_att_ref[...] = grad_one.astype(bf16)
        dvec_ref[1:2, :] = column_sum(grad * xhat)
        dvec_ref[2:3, :] = column_sum(grad)


def feed_forward(tokens, mixed, attention_weights, weights, up_bias, vectors, live, cotangent):
    length, width = tokens.shape
    parts, shards, double_rows, hidden = weights.shape
    whole = lambda shape: pl.BlockSpec(shape, lambda p, w: (0,) * len(shape))
    once = lambda shape: pl.BlockSpec(
        shape, lambda p, w: (0,) * len(shape), pipeline_mode=pl.Buffered(1)
    )
    wo_column = attention_weights.shape[1] // width - 1
    wide = (length, width)
    return pl.pallas_call(
        partial(ffn_kernel, double_rows // 2),
        grid=(2, parts),
        in_specs=[
            once(wide),
            once(wide),
            pl.BlockSpec(
                (width, width), lambda p, w: (0, wo_column), pipeline_mode=pl.Buffered(1)
            ),
            pl.BlockSpec((None, shards, double_rows, hidden), lambda p, w: (w, 0, 0, 0)),
            pl.BlockSpec((None, 1, hidden), lambda p, w: (w, 0, 0)),
            whole(vectors.shape),
            once((length, 1)),
            once(wide),
        ],
        out_specs=[
            whole(wide),
            whole(wide),
            whole(wide),
            pl.BlockSpec((None, shards, double_rows, hidden), lambda p, w: (w * p, 0, 0, 0)),
            pl.BlockSpec((None, 1, hidden), lambda p, w: (w * p, 0, 0)),
            whole((8, width)),
        ],
        out_shape=[
            jax.ShapeDtypeStruct(wide, bf16),
            jax.ShapeDtypeStruct(wide, f32),
            jax.ShapeDtypeStruct(wide, bf16),
            jax.ShapeDtypeStruct(weights.shape, bf16),
            jax.ShapeDtypeStruct((parts, 1, hidden), f32),
            jax.ShapeDtypeStruct((8, width), f32),
        ],
        scratch_shapes=[
            pltpu.VMEM(wide, f32),
            pltpu.VMEM(wide, bf16),
            pltpu.VMEM((width, length), bf16),
            pltpu.VMEM(wide, f32),
            pltpu.VMEM((length, 1), f32),
            pltpu.VMEM((parts, length, hidden), bf16),
            pltpu.VMEM((parts, length, hidden), f32),
            pltpu.VMEM(wide, f32),
            pltpu.VMEM(wide, f32),
            pltpu.VMEM(wide, bf16),
            pltpu.VMEM((width, length), bf16),
        ],
        compiler_params=pltpu.CompilerParams(vmem_limit_bytes=56 * 1024 * 1024),
        name="feed_forward",
    )(tokens, mixed, attention_weights, weights, up_bias, vectors, live, cotangent)


def exchange_sum(value, axes, devices):
    step = 1
    while step < devices:
        pairs = [(i, i ^ step) for i in range(devices)]
        value = value + lax.ppermute(value, axes, pairs)
        step *= 2
    return value


def per_device(
    batch,
    wide,
    tokens,
    block_row,
    block_live,
    query_weight,
    key_weight,
    value_weight,
    out_weight,
    position_bias,
    features,
    up_weight,
    up_bias,
    down_weight,
    down_bias,
    gain_one,
    shift_one,
    gain_two,
    shift_two,
    cotangent,
):
    axes = ("batch", "wide")
    devices = batch * wide
    length, width = tokens.shape
    heads = position_bias.shape[0]
    pairs = heads // 2
    own = query_weight.shape[0]
    lanes = width // pairs
    shard = jnp.stack(
        [w.astype(bf16).reshape(own, pairs, lanes) for w in (query_weight, key_weight, value_weight)],
        axis=2,
    ).reshape(own, 3 * width)
    shard = jnp.concatenate([shard, out_weight.astype(bf16)], axis=1)
    attention_weights = lax.all_gather(shard, axes, axis=0, tiled=True)
    up_rows, hidden = up_weight.shape
    ffn_shard = jnp.concatenate([up_weight.astype(bf16), down_weight.astype(bf16)], axis=0)
    ffn_weights = lax.all_gather(ffn_shard, ("wide", "batch"), axis=0, tiled=False)
    ffn_weights = ffn_weights.reshape(wide, batch, 2 * up_rows, hidden)

    offsets = jnp.arange(BLK, dtype=jnp.int32)
    live = (offsets[None, :] < block_live[:, None]).astype(f32).reshape(1, length)
    rows = jnp.broadcast_to(block_row[:, None], (block_row.shape[0], BLK)).reshape(1, length)
    mask = jnp.where(block_row[:, None] == rows, live, 0.0)
    tables = toeplitz_tables(position_bias[:, ::-1])
    feat = block_diagonal(features)
    mixed, u, phi, value = attend(tokens, attention_weights, tables, mask, split_rows(feat), heads)

    vectors = jnp.stack([down_bias, gain_one, shift_one, gain_two, shift_two] + [down_bias] * 3)
    out_tokens, grad_one, grad_attention, dw_ffn, dup_bias, dvec = feed_forward(
        tokens,
        mixed,
        attention_weights,
        ffn_weights,
        up_bias.reshape(wide, 1, hidden),
        vectors,
        live.reshape(length, 1),
        cotangent,
    )
    ffn_own = lax.psum_scatter(
        dw_ffn.reshape(devices, 2 * up_rows, hidden),
        ("wide", "batch"),
        scatter_dimension=0,
        tiled=False,
    ).astype(f32)
    dw_qkv, dbias, grad_tokens = attend_back(
        tokens.T,
        attention_weights,
        tables,
        mask,
        split_rows(feat.T),
        u,
        phi,
        value,
        grad_attention,
        grad_one,
        heads,
    )
    dw_out = lax.dot_general(
        mixed, grad_attention, (((0,), (0,)), ((), ())), preferred_element_type=f32
    )
    dw_att = jnp.concatenate([dw_qkv, dw_out.astype(bf16)], axis=1)
    att_own = lax.psum_scatter(dw_att, axes, scatter_dimension=0, tiled=True).astype(f32)
    qkv_own = att_own[:, : 3 * width].reshape(own, pairs, 3, lanes)
    dq, dk, dv = (qkv_own[:, :, i].reshape(own, width) for i in range(3))
    small = exchange_sum(
        jnp.concatenate([dup_bias.reshape(-1, 256), dvec.reshape(-1, 256)], axis=0), axes, devices
    )
    dbias = exchange_sum(dbias, axes, devices)
    count = up_bias.shape[0] // 256
    dvec = small[count:].reshape(8, width)
    return (
        out_tokens,
        grad_tokens,
        dq,
        dk,
        dv,
        att_own[:, 3 * width :],
        dbias[:, ::-1],
        ffn_own[:up_rows],
        small[:count].reshape(-1),
        ffn_own[up_rows:],
        dvec[0],
        dvec[1],
        dvec[2],
        dvec[3],
        dvec[4],
    )


def solution(mesh):
    both = P(("batch", "wide"), None)
    placed = (
        both,
        P(("batch", "wide")),
        P(("batch", "wide")),
        both,
        both,
        both,
        both,
        P(),
        P(),
        P("batch", "wide"),
        P(),
        P("batch", "wide"),
        P(),
        P(),
        P(),
        P(),
        P(),
        both,
    )
    outs = (
        both,
        both,
        both,
        both,
        both,
        both,
        P(),
        P("batch", "wide"),
        P(),
        P("batch", "wide"),
        P(),
        P(),
        P(),
        P(),
        P(),
    )
    return jax.shard_map(
        partial(per_device, mesh.shape["batch"], mesh.shape["wide"]),
        mesh=mesh,
        in_specs=placed,
        out_specs=outs,
        check_vma=False,
    )
```

```python
import itertools
from functools import partial

import jax
import jax.numpy as jnp
from jax import lax
from jax.experimental import pallas as pl
from jax.experimental.pallas import tpu as pltpu
from jax.sharding import PartitionSpec as P

BLK = 128
f32 = jnp.float32
bf16 = jnp.bfloat16
nt_dims = (((1,), (1,)), ((), ()))


def dot(a, b):
    return jnp.dot(a, b, preferred_element_type=f32)


def dot_nt(a, b):
    return lax.dot_general(a, b, nt_dims, preferred_element_type=f32)


def split_low(x):
    high = x.astype(bf16)
    return high, (x - high.astype(f32)).astype(bf16)


def toeplitz_kernel(bias_ref, out_ref):
    heads = bias_ref.shape[0]
    rels = bias_ref.shape[1]
    for h in range(heads):
        row = jnp.broadcast_to(jnp.exp(bias_ref[h : h + 1, :]), (BLK, rels))
        out_ref[h] = pltpu.roll(row, rels - BLK + 1, 1, stride=1, stride_axis=0)


def toeplitz_tables(flipped_bias):
    heads, rels = flipped_bias.shape
    step = 2
    return pl.pallas_call(
        toeplitz_kernel,
        grid=(heads // step,),
        in_specs=[pl.BlockSpec((None, step, rels), lambda h: (h, 0, 0))],
        out_specs=pl.BlockSpec((step, BLK, rels), lambda h: (h, 0, 0)),
        out_shape=jax.ShapeDtypeStruct((heads, BLK, rels), f32),
        cost_estimate=pl.CostEstimate(
            flops=5_000_000_000, bytes_accessed=8_000_000, transcendentals=0
        ),
        name="toeplitz",
    )(flipped_bias.reshape(heads // step, step, rels))


def lane_half(shape):
    return lax.broadcasted_iota(jnp.int32, shape, 1) < shape[1] // 2


def pair_features(u, feat_ref):
    high, low = split_low(u)
    square = u * u
    s_high, rest = split_low(square)
    rest = square - s_high.astype(f32)
    s_mid, s_low = split_low(rest)
    lhs = jnp.concatenate([high, high, low, s_high, s_mid, s_low], axis=1)
    return jnp.exp(dot(lhs, feat_ref[...]))


def attend_kernel(
    scale,
    tok_ref,
    w_ref,
    table_ref,
    mask_ref,
    feat_ref,
    mixed_ref,
    mixed32_ref,
    u_ref,
    phi_ref,
    val_ref,
    inv_ref,
    weights_ref,
):
    length = tok_ref.shape[0]
    pair = mixed_ref.shape[1]
    size = pair // 2
    blocks = length // BLK
    qkv = dot(tok_ref[...], w_ref[...])
    uq = qkv[:, :pair] * scale
    uk = qkv[:, pair : 2 * pair] * scale
    value = qkv[:, 2 * pair :].astype(bf16)
    pq = pair_features(uq, feat_ref)
    pk = pair_features(uk, feat_ref)
    u_ref[:, :pair] = uq
    u_ref[:, pair:] = uk
    phi_ref[:, :pair] = pq
    phi_ref[:, pair:] = pk
    val_ref[...] = value
    pq = pq.astype(bf16)
    pk = pk.astype(bf16)
    first = lane_half(value.shape)
    zero = jnp.zeros_like(value)
    one = jnp.ones_like(value)
    out = None
    for h in range(2):
        cols = slice(h * size, (h + 1) * size)
        here = first if h == 0 else jnp.logical_not(first)
        for b in range(blocks):
            rows = slice(b * BLK, (b + 1) * BLK)
            start = (blocks - 1 - b) * BLK
            scores = dot_nt(pq[rows, cols], pk[:, cols])
            coupling = table_ref[h, :, start : start + length] * mask_ref[b : b + 1, :]
            weights_ref[rows, :] = (coupling * scores).astype(bf16)
        rhs = jnp.concatenate([jnp.where(here, value, zero), jnp.where(here, one, zero)], axis=1)
        part = dot(weights_ref[...], rhs)
        out = part if out is None else out + part
    inverse = 1.0 / out[:, pair:]
    mixed = out[:, :pair] * inverse
    inv_ref[...] = inverse
    mixed32_ref[...] = mixed
    mixed_ref[...] = mixed.astype(bf16)


def attend(tokens, weights, tables, mask, feat_split, heads):
    length, width = tokens.shape
    pair = 2 * width // heads
    pairs = heads // 2
    rels = tables.shape[2]
    scale = float((pair // 2) ** (-0.25))
    whole = lambda shape: pl.BlockSpec(shape, lambda h: (0,) * len(shape))
    column = lambda cols: pl.BlockSpec((length, cols), lambda h: (0, h))
    return pl.pallas_call(
        partial(attend_kernel, scale),
        grid=(pairs,),
        in_specs=[
            whole((length, width)),
            pl.BlockSpec((width, 3 * pair), lambda h: (0, h)),
            pl.BlockSpec((2, BLK, rels), lambda h: (h, 0, 0)),
            whole(mask.shape),
            whole(feat_split.shape),
        ],
        out_specs=[
            column(pair),
            column(pair),
            column(2 * pair),
            column(2 * pair),
            column(pair),
            column(pair),
        ],
        out_shape=[
            jax.ShapeDtypeStruct((length, width), bf16),
            jax.ShapeDtypeStruct((length, width), f32),
            jax.ShapeDtypeStruct((length, 2 * width), f32),
            jax.ShapeDtypeStruct((length, 2 * width), f32),
            jax.ShapeDtypeStruct((length, width), bf16),
            jax.ShapeDtypeStruct((length, width), f32),
        ],
        scratch_shapes=[pltpu.VMEM((length, length), bf16)],
        cost_estimate=pl.CostEstimate(flops=0, bytes_accessed=0, transcendentals=0),
        name="attend",
    )(tokens, weights, tables, mask, feat_split)


def pair_backward(scale, grad_phi, phi, u, feat_ref):
    pair = u.shape[1]
    high, low = split_low(grad_phi * phi)
    back = dot(jnp.concatenate([high, high, low], axis=1), feat_ref[...])
    return (scale * (back[:, :pair] - u * back[:, pair:])).astype(bf16)


def attend_back_kernel(
    scale,
    place_ref,
    tok_t_ref,
    table_ref,
    mask_ref,
    feat_ref,
    swap_ref,
    turn_ref,
    u_ref,
    phi_ref,
    val_ref,
    inv_ref,
    mixed_ref,
    gm_ref,
    dw_mine_ref,
    dw_other_ref,
    dqkv_ref,
    dbias_ref,
    probs_ref,
    gs_ref,
    diag_ref,
):
    length, pair = val_ref.shape
    size = pair // 2
    blocks = length // BLK
    gm = gm_ref[...].astype(f32)
    scaled = gm * inv_ref[...]
    g_high, g_low = split_low(scaled)
    gt = scaled.T
    gt_high, gt_low = split_low(gt)
    d_high, d_low = split_low(scaled * mixed_ref[...])
    inner = dot(jnp.concatenate([d_high, d_low], axis=1), swap_ref[...])
    i_high, i_low = split_low(inner)
    phi = phi_ref[...]
    pq32, pk32 = phi[:, :pair], phi[:, pair:]
    pq = pq32.astype(bf16)
    pk = pk32.astype(bf16)
    pq_t = pq32.T.astype(bf16)
    value = val_ref[...]
    first = lane_half(value.shape)
    unit = jnp.full_like(value, 1.0 / size)
    zero = jnp.zeros_like(value)
    gq = None
    gk_heads = []
    gv_heads = []
    for h in range(2):
        cols = slice(h * size, (h + 1) * size)
        here = first if h == 0 else jnp.logical_not(first)
        lhs = jnp.concatenate(
            [jnp.where(here, g_high, i_high), jnp.where(here, g_low, i_low)], axis=1
        )
        rhs = jnp.where(here, value, unit)
        rhs = jnp.concatenate([rhs, rhs], axis=1)
        diag_ref[...] = jnp.zeros_like(diag_ref)
        for b in range(blocks):
            rows = slice(b * BLK, (b + 1) * BLK)
            start = (blocks - 1 - b) * BLK
            window = slice(start, start + length)
            mask = mask_ref[b : b + 1, :]
            scores = dot_nt(pq[rows, cols], pk[:, cols])
            coupling = table_ref[h, :, window] * mask
            probs_ref[rows, :] = (coupling * scores).astype(bf16)
            grad_scores = dot_nt(lhs[rows], rhs) * coupling
            gs_ref[rows, :] = grad_scores.astype(bf16)
            diag_ref[:, window] += grad_scores * scores
        part = dot(gs_ref[...], jnp.where(here, pk, zero))
        gq = part if gq is None else gq + part
        gk_heads.append(dot(pq_t[cols, :], gs_ref[...]))
        both = dot(jnp.concatenate([gt_high[cols], gt_low[cols]], axis=0), probs_ref[...])
        gv_heads.append(both[:size] + both[size:])
        folded = diag_ref[...]
        half = BLK // 2
        while half >= 1:
            folded = pltpu.roll(folded[:half], half, 1) + folded[half:]
            half //= 2
        split = [folded[:, n : n + BLK] for n in range(0, folded.shape[1], BLK)]
        f_high, rest = split_low(jnp.concatenate(split, axis=0))
        f_mid, f_low = split_low(jnp.concatenate(split, axis=0) - f_high.astype(f32))
        turned = dot(jnp.concatenate([f_high, f_mid, f_low], axis=1), turn_ref[...])
        for n in range(len(split)):
            dbias_ref[h : h + 1, n * BLK : (n + 1) * BLK] = turned[len(split) - 1 - n][None]
    gk = jnp.concatenate(gk_heads, axis=0).T
    gv = jnp.concatenate(gv_heads, axis=0).T.astype(bf16)
    u = u_ref[...]
    dq = pair_backward(scale, gq, pq32, u[:, :pair], feat_ref)
    dk = pair_backward(scale, gk, pk32, u[:, pair:], feat_ref)
    dqkv_ref[:, :pair] = dq
    dqkv_ref[:, pair : 2 * pair] = dk
    dqkv_ref[:, 2 * pair :] = gv
    half = tok_t_ref.shape[0] // 2
    place = place_ref[0]
    mine = pl.ds(pl.multiple_of(place * half, half), half)
    other = pl.ds(pl.multiple_of((1 - place) * half, half), half)
    dw_mine_ref[...] = dot(tok_t_ref[mine, :], dqkv_ref[...]).astype(bf16)
    dw_other_ref[...] = dot(tok_t_ref[other, :], dqkv_ref[...]).astype(bf16)


def attend_back(
    place,
    tokens_t,
    tables,
    mask,
    feat_back,
    swap,
    turn,
    u,
    phi,
    value,
    inverse,
    mixed,
    grad_mixed,
    heads,
    first,
    count,
):
    width, length = tokens_t.shape
    pair = 2 * width // heads
    rels = tables.shape[2]
    scale = float((pair // 2) ** (-0.25))
    whole = lambda shape: pl.BlockSpec(shape, lambda h, p: (0,) * len(shape))
    column = lambda cols: pl.BlockSpec((length, cols), lambda h, p: (0, h + first))
    own_column = lambda rows: pl.BlockSpec((rows, 3 * pair), lambda h, p: (0, h))
    return pl.pallas_call(
        partial(attend_back_kernel, scale),
        grid_spec=pltpu.PrefetchScalarGridSpec(
            num_scalar_prefetch=1,
            grid=(count,),
            in_specs=[
                whole((width, length)),
                pl.BlockSpec((2, BLK, rels), lambda h, p: (h + first, 0, 0)),
                whole(mask.shape),
                whole(feat_back.shape),
                whole(swap.shape),
                whole(turn.shape),
                column(2 * pair),
                column(2 * pair),
                column(pair),
                column(pair),
                column(pair),
                column(pair),
            ],
            out_specs=[
                own_column(width // 2),
                own_column(width // 2),
                own_column(length),
                pl.BlockSpec((None, 2, rels), lambda h, p: (h, 0, 0)),
            ],
            scratch_shapes=[
                pltpu.VMEM((length, length), bf16),
                pltpu.VMEM((length, length), bf16),
                pltpu.VMEM((BLK, rels), f32),
            ],
        ),
        out_shape=[
            jax.ShapeDtypeStruct((width // 2, count * 3 * pair), bf16),
            jax.ShapeDtypeStruct((width // 2, count * 3 * pair), bf16),
            jax.ShapeDtypeStruct((length, count * 3 * pair), bf16),
            jax.ShapeDtypeStruct((count, 2, rels), f32),
        ],
        cost_estimate=pl.CostEstimate(flops=0, bytes_accessed=0, transcendentals=0),
        name="attend_back",
    )(place, tokens_t, tables, mask, feat_back, swap, turn, u, phi, value, inverse, mixed, grad_mixed)


def block_diagonal(matrix):
    zero = jnp.zeros_like(matrix)
    return jnp.concatenate(
        [jnp.concatenate([matrix, zero], axis=1), jnp.concatenate([zero, matrix], axis=1)], axis=0
    )


def feature_tables(features):
    size = features.shape[0]
    ones = block_diagonal(jnp.ones((size, size), f32)).astype(bf16)
    high, low = split_low(block_diagonal(features))
    half = ones * -0.5
    forward = jnp.concatenate([high, low, high, half, half, half], axis=0)
    high, low = split_low(block_diagonal(features.T))
    none = jnp.zeros_like(ones)
    backward = jnp.concatenate(
        [jnp.concatenate([high, low, high], axis=0), jnp.concatenate([ones, none, ones], axis=0)],
        axis=1,
    )
    swap = jnp.concatenate([-ones[:, size:], -ones[:, :size]], axis=1)
    turn = jnp.eye(BLK, dtype=bf16)[::-1]
    return forward, backward, jnp.concatenate([swap, swap], axis=0), jnp.tile(turn, (3, 1))


def prepare_kernel(q_ref, k_ref, v_ref, o_ref, up_ref, down_ref, att_ref, ffn_ref):
    width = o_ref.shape[1]
    lanes = att_ref.shape[1] // 4 // (width // 128)
    for j, ref in enumerate((q_ref, k_ref, v_ref)):
        for p in range(width // lanes):
            to = (3 * p + j) * lanes
            att_ref[:, to : to + lanes] = ref[:, p * lanes : (p + 1) * lanes].astype(bf16)
    att_ref[:, 3 * width :] = o_ref[...].astype(bf16)
    rows = up_ref.shape[0]
    ffn_ref[:rows] = up_ref[...].astype(bf16)
    ffn_ref[rows:] = down_ref[...].astype(bf16)


def prepare(query, key, value, out, up, down):
    own, width = query.shape
    return pl.pallas_call(
        prepare_kernel,
        out_shape=[
            jax.ShapeDtypeStruct((own, 4 * width), bf16),
            jax.ShapeDtypeStruct((2 * up.shape[0], up.shape[1]), bf16),
        ],
        name="prepare",
    )(query, key, value, out, up, down)


root_half = 0.7071067811865476
inv_root_two_pi = 0.3989422804014327
eps = 1e-05


def norm_stats(residual):
    centered = residual - jnp.mean(residual, axis=1, keepdims=True)
    inverse = lax.rsqrt(jnp.mean(centered * centered, axis=1, keepdims=True) + eps)
    return centered * inverse, inverse


def norm_back(grad, xhat, inverse, gain):
    scaled = grad * gain
    mean_grad = jnp.mean(scaled, axis=1, keepdims=True)
    mean_dot = jnp.mean(scaled * xhat, axis=1, keepdims=True)
    return (scaled - mean_grad - xhat * mean_dot) * inverse


def column_sum(x):
    return jnp.sum(x, axis=0, keepdims=True)


def ffn_kernel(
    place_ref,
    tok_ref,
    mixed_ref,
    mixed_t_ref,
    wo_ref,
    up_ref,
    down_ref,
    up_bias_ref,
    vec_ref,
    live_ref,
    cot_ref,
    out_ref,
    grad_one_ref,
    gm_ref,
    up_other_ref,
    up_mine_ref,
    down_other_ref,
    down_mine_ref,
    wo_other_ref,
    wo_mine_ref,
    dup_bias_ref,
    dvec_ref,
    normed_ref,
    low_ref,
    low_t_ref,
    xhat_ref,
    inv_ref,
    act_ref,
    slope_ref,
    acc_ref,
    gb_ref,
    gb_t_ref,
):
    phase = pl.program_id(0)
    part = pl.program_id(1)
    parts = pl.num_programs(1)
    length, width = tok_ref.shape
    rows, hidden = up_ref.shape[1:]
    chunk = 256 if hidden % 256 == 0 else hidden
    chunks = [slice(k, k + chunk) for k in range(0, hidden, chunk)]
    vec = vec_ref[...]
    down_bias, gain_one, shift_one, gain_two, shift_two = (vec[i : i + 1] for i in range(5))

    @pl.when((phase == 0) & (part == 0))
    def _():
        residual = tok_ref[...].astype(f32) + dot(mixed_ref[...], wo_ref[...])
        xhat, inverse = norm_stats(residual)
        normed = xhat * gain_one + shift_one
        xhat_ref[...] = xhat
        inv_ref[...] = inverse
        normed_ref[...] = normed
        low_ref[...] = normed.astype(bf16)
        low_t_ref[...] = normed.T.astype(bf16)
        acc_ref[...] = jnp.zeros_like(acc_ref)

    @pl.when(phase == 0)
    def _():
        for cols in chunks:
            up = up_ref[:, :, cols].reshape(width, chunk)
            down = down_ref[:, :, cols].reshape(width, chunk)
            v = dot(low_ref[...], up) + up_bias_ref[:, cols]
            half = 0.5 + 0.5 * lax.erf(v * root_half)
            act = (v * half).astype(bf16)
            act_ref[part, :, cols] = act
            slope_ref[part, :, cols] = half + v * (jnp.exp(-0.5 * v * v) * inv_root_two_pi)
            acc_ref[...] += dot_nt(act, down)

    @pl.when((phase == 0) & (part == parts - 1))
    def _():
        live = live_ref[...]
        xhat, inverse = norm_stats(normed_ref[...] + (acc_ref[...] + down_bias))
        out_ref[...] = ((xhat * gain_two + shift_two) * live).astype(bf16)
        grad = cot_ref[...].astype(f32) * live
        grad_two = norm_back(grad, xhat, inverse, gain_two)
        low = grad_two.astype(bf16)
        gb_ref[...] = low
        gb_t_ref[...] = grad_two.T.astype(bf16)
        dvec_ref[0:1, :] = column_sum(low.astype(f32))
        dvec_ref[3:4, :] = column_sum(grad * xhat)
        dvec_ref[4:5, :] = column_sum(grad)
        dvec_ref[5:8, :] = jnp.zeros((3, width), f32)
        acc_ref[...] = grad_two

    def backward(d_up_ref, d_down_ref):
        for cols in chunks:
            up = up_ref[:, :, cols].reshape(width, chunk)
            down = down_ref[:, :, cols].reshape(width, chunk)
            grad_act = dot(gb_ref[...], down)
            grad_hidden = (grad_act * slope_ref[part, :, cols]).astype(bf16)
            dup_bias_ref[:, cols] = column_sum(grad_hidden.astype(f32))
            d_up = dot(low_t_ref[...], grad_hidden).astype(bf16)
            d_down = dot(gb_t_ref[...], act_ref[part, :, cols]).astype(bf16)
            d_up_ref[:, :, cols] = d_up.reshape(-1, rows, chunk)
            d_down_ref[:, :, cols] = d_down.reshape(-1, rows, chunk)
            acc_ref[...] += dot_nt(grad_hidden, up)

    @pl.when((phase == 1) & (part < parts // 2))
    def _():
        backward(up_other_ref, down_other_ref)

    @pl.when((phase == 1) & (part >= parts // 2))
    def _():
        backward(up_mine_ref, down_mine_ref)

    @pl.when((phase == 1) & (part == parts - 1))
    def _():
        grad = acc_ref[...]
        xhat = xhat_ref[...]
        grad_one = norm_back(grad, xhat, inv_ref[...], gain_one)
        grad_one_ref[...] = grad_one
        grad_att = grad_one.astype(bf16)
        gm_ref[...] = dot_nt(grad_att, wo_ref[...]).astype(bf16)
        half = width // 2
        place = place_ref[0]
        mine = pl.ds(pl.multiple_of(place * half, half), half)
        other = pl.ds(pl.multiple_of((1 - place) * half, half), half)
        wo_mine_ref[...] = dot(mixed_t_ref[mine, :], grad_att).astype(bf16)
        wo_other_ref[...] = dot(mixed_t_ref[other, :], grad_att).astype(bf16)
        dvec_ref[1:2, :] = column_sum(grad * xhat)
        dvec_ref[2:3, :] = column_sum(grad)


def feed_forward(
    place, tokens, mixed, mixed_t, attention_weights, weights, up_bias, vectors, live, cotangent
):
    length, width = tokens.shape
    parts, shards, _, rows, hidden = weights.shape
    xs = parts // 2
    whole = lambda shape: pl.BlockSpec(shape, lambda p, w, c: (0,) * len(shape))
    once = lambda shape: pl.BlockSpec(
        shape, lambda p, w, c: (0,) * len(shape), pipeline_mode=pl.Buffered(1)
    )
    wo_column = attention_weights.shape[1] // width - 1
    wide = (length, width)
    part_of = lambda w, c: 2 * lax.rem(w, xs) + jnp.where(w < xs, 1 - c[0], c[0])
    weight_spec = lambda which: pl.BlockSpec(
        (None, shards, None, rows, hidden), lambda p, w, c: (part_of(w, c), 0, which, 0, 0)
    )
    other_spec = pl.BlockSpec(
        (None, shards, rows, hidden), lambda p, w, c: (p * jnp.minimum(w, xs - 1), 0, 0, 0)
    )
    mine_spec = pl.BlockSpec(
        (None, shards, rows, hidden), lambda p, w, c: (p * jnp.maximum(w - xs, 0), 0, 0, 0)
    )
    grads = jax.ShapeDtypeStruct((xs, shards, rows, hidden), bf16)
    return pl.pallas_call(
        ffn_kernel,
        grid_spec=pltpu.PrefetchScalarGridSpec(
            num_scalar_prefetch=1,
            grid=(2, parts),
            in_specs=[
                once(wide),
                once(wide),
                once((width, length)),
                pl.BlockSpec(
                    (width, width), lambda p, w, c: (0, wo_column), pipeline_mode=pl.Buffered(1)
                ),
                weight_spec(0),
                weight_spec(1),
                pl.BlockSpec((None, 1, hidden), lambda p, w, c: (part_of(w, c), 0, 0)),
                whole(vectors.shape),
                once((length, 1)),
                once(wide),
            ],
            out_specs=[
                whole(wide),
                whole(wide),
                whole(wide),
                other_spec,
                mine_spec,
                other_spec,
                mine_spec,
                whole((width // 2, width)),
                whole((width // 2, width)),
                pl.BlockSpec(
                    (None, 1, hidden), lambda p, w, c: (part_of(w * p, c), 0, 0)
                ),
                whole((8, width)),
            ],
            scratch_shapes=[
                pltpu.VMEM(wide, f32),
                pltpu.VMEM(wide, bf16),
                pltpu.VMEM((width, length), bf16),
                pltpu.VMEM(wide, f32),
                pltpu.VMEM((length, 1), f32),
                pltpu.VMEM((parts, length, hidden), bf16),
                pltpu.VMEM((parts, length, hidden), f32),
                pltpu.VMEM(wide, f32),
                pltpu.VMEM(wide, bf16),
                pltpu.VMEM((width, length), bf16),
            ],
        ),
        out_shape=[
            jax.ShapeDtypeStruct(wide, bf16),
            jax.ShapeDtypeStruct(wide, f32),
            jax.ShapeDtypeStruct(wide, bf16),
            grads,
            grads,
            grads,
            grads,
            jax.ShapeDtypeStruct((width // 2, width), bf16),
            jax.ShapeDtypeStruct((width // 2, width), bf16),
            jax.ShapeDtypeStruct((parts, 1, hidden), f32),
            jax.ShapeDtypeStruct((8, width), f32),
        ],
        compiler_params=pltpu.CompilerParams(vmem_limit_bytes=58 * 1024 * 1024),
        cost_estimate=pl.CostEstimate(flops=0, bytes_accessed=0, transcendentals=0),
        name="feed_forward",
    )(
        place,
        tokens,
        mixed,
        mixed_t,
        attention_weights,
        weights,
        weights,
        up_bias,
        vectors,
        live,
        cotangent,
    )


class Grid:
    def __init__(self, batch, wide):
        self.devices = batch * wide
        self.sizes = dict(z=4, y=batch // 4, x=wide // 2, c=2)
        self.strides = dict(z=batch // 4 * wide, y=wide, x=2, c=1)
        flat = lax.axis_index("batch") * wide + lax.axis_index("wide")
        self.place = {d: lax.rem(flat // self.strides[d], n) for d, n in self.sizes.items()}
        self.vector = jnp.stack([self.place[d] for d in "zyxc"])

    def shift(self, value, **offsets):
        pairs = []
        for i in range(self.devices):
            target = i
            for d, o in offsets.items():
                s, n = self.strides[d], self.sizes[d]
                target += ((i // s + o) % n - i // s % n) * s
            pairs.append((i, target))
        return lax.ppermute(value, ("batch", "wide"), pairs)

    def at(self, d, offset):
        return lax.rem(self.place[d] + (offset + self.sizes[d]), self.sizes[d])

    def block_at(self, d, offset):
        k, n = "zyxc".index(d), self.sizes[d]
        return lambda vector: lax.rem(vector[k] + offset, n)

    def offsets(self, dims):
        ranges = [range(self.sizes[d]) for d in dims]
        return [dict(zip(dims, o)) for o in itertools.product(*ranges)]

    def gather(self, value, names, dims):
        parts = [(o, self.shift(value, **o) if any(o.values()) else value) for o in self.offsets(dims)]
        if len(parts) == 2:
            (d,) = dims
            own, other = value, parts[1][1]
            first = self.place[d] == 0
            return jnp.concatenate(
                [jnp.where(first, own, other), jnp.where(first, other, own)], axis=names.index(d)
            )
        shape = [self.sizes[d] if d in dims else n for d, n in zip(names, value.shape)]
        out = jnp.zeros(shape + list(value.shape[len(names) :]), value.dtype)
        for o, part in parts:
            start = [self.at(d, -o[d]) if d in dims else 0 for d in names]
            out = lax.dynamic_update_slice(out, part, start + [0] * (value.ndim - len(names)))
        return out

    def send(self, sends, dims):
        return [self.shift(value, **o) for o, value in zip(self.offsets(dims)[1:], sends)]


class Combine:
    def __init__(self, grid, steps):
        self.grid, self.steps = grid, steps
        self.inputs, self.in_specs, self.shapes, self.out_specs, self.terms = [], [], [], [], []

    def spec(self, block, where):
        picks = []
        for w in where:
            if w is None:
                picks.append(lambda i, v: 0)
            elif w == "step":
                picks.append(lambda i, v: i)
            else:
                at = self.grid.block_at(*w)
                picks.append(lambda i, v, at=at: at(v))
        return pl.BlockSpec(block, lambda i, v: tuple(p(i, v) for p in picks))

    def read(self, arrays, where):
        numbers = []
        for a in arrays:
            block = tuple(n if w is None else None for n, w in zip(a.shape, where))
            numbers.append(len(self.inputs))
            self.inputs.append(a)
            self.in_specs.append(self.spec(block, where))
        return numbers

    def add(self, addends, picks):
        numbers = []
        for names, array in addends:
            where = tuple(picks.get(d) for d in names)
            where = tuple((d, w) if isinstance(w, int) else w for d, w in zip(names, where))
            numbers += self.read([array], where + (None,) * (array.ndim - len(names)))
        return numbers

    def write(self, shape, dtype, terms, stepped=False):
        where = ("step",) + (None,) * (len(shape) - 1) if stepped else (None,) * len(shape)
        block = tuple(n if w is None else None for n, w in zip(shape, where))
        self.shapes.append(jax.ShapeDtypeStruct(shape, dtype))
        self.out_specs.append(self.spec(block, where))
        self.terms.append(terms)

    def run(self, name):
        count = len(self.inputs)

        def kernel(vector_ref, *refs):
            for out_ref, terms in zip(refs[count:], self.terms):
                for target, *rest in terms:
                    total = None
                    for source, numbers in [rest] if len(rest) == 2 else rest[0]:
                        for n in numbers:
                            value = refs[n][source].astype(f32)
                            total = value if total is None else total + value
                    total = total.astype(out_ref.dtype)
                    if len(out_ref.shape) == 1:
                        total = total.reshape(out_ref.shape)
                    out_ref[target] = total

        return pl.pallas_call(
            kernel,
            grid_spec=pltpu.PrefetchScalarGridSpec(
                num_scalar_prefetch=1,
                grid=(self.steps,),
                in_specs=self.in_specs,
                out_specs=self.out_specs,
            ),
            out_shape=self.shapes,
            compiler_params=pltpu.CompilerParams(vmem_limit_bytes=60 * 1024 * 1024),
            cost_estimate=pl.CostEstimate(flops=0, bytes_accessed=0, transcendentals=0),
            name=name,
        )(self.grid.vector, *self.inputs)


everything = (Ellipsis,)


def hold(value, *others):
    return lax.optimization_barrier((value, others))


def per_device(
    batch,
    wide,
    tokens,
    block_row,
    block_live,
    query_weight,
    key_weight,
    value_weight,
    out_weight,
    position_bias,
    features,
    up_weight,
    up_bias,
    down_weight,
    down_bias,
    gain_one,
    shift_one,
    gain_two,
    shift_two,
    cotangent,
):
    grid = Grid(batch, wide)
    zs, ys, xs, cs = (grid.sizes[d] for d in "zyxc")
    length, width = tokens.shape
    heads, rels = position_bias.shape
    pairs = heads // 2
    own = query_weight.shape[0]
    lanes = width // pairs
    shard, ffn_shard = prepare(
        query_weight, key_weight, value_weight, out_weight, up_weight, down_weight
    )
    tables = toeplitz_tables(position_bias[:, ::-1])
    feat_forward, feat_back, swap, turn = feature_tables(features)
    offsets = jnp.arange(BLK, dtype=jnp.int32)
    live = (offsets[None, :] < block_live[:, None]).astype(f32).reshape(1, length)
    rows = jnp.broadcast_to(block_row[:, None], (block_row.shape[0], BLK)).reshape(1, length)
    mask = jnp.where(block_row[:, None] == rows, live, 0.0)
    by_core = lambda m: m.reshape(-1, cs, own, length).swapaxes(0, 1).reshape(width, length)
    tokens_t = by_core(tokens.T)
    vectors = jnp.stack([down_bias, gain_one, shift_one, gain_two, shift_two] + [down_bias] * 3)
    live_column = live.reshape(length, 1)

    up_rows, hidden = up_weight.shape
    gathered = grid.gather(shard.reshape(1, 1, 1, 1, own, 4 * width), "zyxc", "z")
    gathered = grid.gather(gathered, "zyxc", "yx")
    early = (tables, feat_forward, feat_back, swap, turn, mask, tokens_t, vectors, live_column)
    gathered, early = hold(gathered, *early)
    tables, feat_forward, feat_back, swap, turn, mask, tokens_t, vectors, live_column = early
    attention_weights = grid.gather(gathered, "zyxc", "c").reshape(width, 4 * width)
    ffn_weights = lax.all_gather(ffn_shard, ("wide", "batch"), axis=0, tiled=False)
    ffn_weights = ffn_weights.reshape(wide, batch, 2, up_rows, hidden)
    mixed, mixed32, u, phi, value, inverse = attend(
        tokens, attention_weights, tables, mask, feat_forward, heads
    )
    place = grid.place["c"].reshape(1)
    (
        out_tokens,
        grad_one,
        grad_mixed,
        up_other_grad,
        up_mine_grad,
        down_other,
        down_mine,
        out_other,
        out_mine,
        dup_bias,
        dvec,
    ) = feed_forward(
        place,
        tokens,
        mixed,
        by_core(mixed.T),
        attention_weights,
        ffn_weights,
        up_bias.reshape(wide, 1, hidden),
        vectors,
        live_column,
        cotangent,
    )
    ffn_view = lambda m: ("xzy", m.reshape(xs, zs, ys, up_rows, hidden))
    att_view = lambda m: ("zyx", m.reshape(zs, ys, xs, own, -1))
    down = [ffn_view(down_mine), ffn_view(grid.shift(down_other, c=1))]
    up = [ffn_view(up_mine_grad), ffn_view(grid.shift(up_other_grad, c=1))]
    out = [att_view(out_mine), att_view(grid.shift(out_other, c=1))]

    step = Combine(grid, 1)
    for y in range(1, ys):
        terms = [(everything, everything, step.add(down, dict(y=y)))]
        step.write((xs, zs, up_rows, hidden), bf16, terms)
    down_sends = step.run("down_sum_core")
    step = Combine(grid, 1)
    for x in range(1, xs):
        terms = [(everything, everything, step.add(up, dict(x=x)))]
        step.write((zs, ys, up_rows, hidden), bf16, terms)
    up_sends = step.run("up_sum_core")
    grad_mixed, (down_sends, up_sends) = hold(grad_mixed, down_sends, up_sends)
    down_new = grid.send(down_sends, "y")
    up_new = grid.send(up_sends, "x")

    dw_mine, dw_other, dqkv, dbias = attend_back(
        place,
        tokens_t,
        tables,
        mask,
        feat_back,
        swap,
        turn,
        u,
        phi,
        value,
        inverse,
        mixed32,
        grad_mixed,
        heads,
        0,
        pairs,
    )
    dw_mine, (dw_other, dqkv, dbias, down_new, up_new) = hold(
        dw_mine, dw_other, dqkv, dbias, down_new, up_new
    )
    down += [("xz", v) for v in down_new]
    up += [("zy", v) for v in up_new]
    att = [att_view(dw_mine), att_view(grid.shift(dw_other, c=1))]

    step = Combine(grid, 1)
    block = (zs, up_rows, hidden)
    for x in range(1, xs):
        terms = [(everything, everything, step.add(down, dict(y=0, x=x)))]
        step.write(block, bf16, terms)
    for y in range(1, ys):
        terms = [(everything, everything, step.add(up, dict(x=0, y=y)))]
        step.write(block, bf16, terms)
    sends = step.run("ffn_sum_plane")
    dbias, sends = hold(dbias, *sends)
    down_new = grid.send(sends[: xs - 1], "x")
    up_new = grid.send(sends[xs - 1 :], "y")

    columns = 4 * width
    per_row = columns // rels
    total_rows = 3 + heads // per_row
    extra = -(-total_rows // 8) * 8
    places = []
    for w in range(wide):
        places.append(("up", w, 0, slice(w * hidden, (w + 1) * hidden)))
    for j in range(8):
        places.append(("vec", j, 1 + j // 4, slice(j % 4 * width, (j % 4 + 1) * width)))
    for h in range(heads):
        places.append(
            ("bias", h, 3 + h // per_row, slice(h % per_row * rels, (h % per_row + 1) * rels))
        )
    step = Combine(grid, 1)
    ins = dict(
        up=step.read([dup_bias], (None, None, None)),
        vec=step.read([dvec], (None, None)),
        bias=step.read([dbias], (None, None, None)),
    )
    sources = dict(
        up=lambda n: (n,),
        vec=lambda n: (slice(n, n + 1),),
        bias=lambda n: (n // 2, slice(n % 2, n % 2 + 1)),
    )
    terms = [
        ((slice(r, r + 1), cols), sources[kind](n), ins[kind])
        for kind, n, r, cols in places
    ]
    step.write((extra, columns), f32, terms)
    (small,) = step.run("small_rows")
    small = small + grid.shift(small, c=1)
    small = [small] + grid.send([small.astype(bf16)] * (ys * xs - 1), "yx")
    dw_mine, sends = hold(dw_mine, *sends)
    att[0] = att_view(dw_mine)
    step = Combine(grid, 1)
    for o in grid.offsets("yx")[1:]:
        terms = [
            ((..., slice(0, 3 * width)), everything, step.add(att, o)),
            ((..., slice(3 * width, None)), everything, step.add(out, o)),
        ]
        step.write((zs, own, columns), bf16, terms)
    att_sends = step.run("att_sum_core")
    down_new, (up_new, att_sends) = hold(down_new, up_new, att_sends)
    down += [("z", v) for v in down_new]
    up += [("z", v) for v in up_new]
    att_new = grid.send(att_sends, "yx")

    here = dict(z=0, y=0, x=0)
    step = Combine(grid, 1)
    for z in range(1, zs):
        terms = [
            ((j,), everything, step.add(addends, dict(z=z, y=0, x=0)))
            for j, addends in enumerate((up, down))
        ]
        step.write((2, up_rows, hidden), bf16, terms)
    sends = step.run("ffn_sum_second")
    ffn_new = grid.send(sends, "z")
    att_new, sends = hold(att_new, *sends)
    att_new = [("z", v) for v in att_new]

    step = Combine(grid, 1)
    small_in = step.read(small, (None, None))
    for z in range(1, zs):
        picks = dict(z=z, y=0, x=0)
        top = slice(0, own)
        new = step.add(att_new, picks)
        head, tail = slice(0, 3 * width), slice(3 * width, None)
        terms = [
            ((top, head), everything, step.add(att, picks)),
            ((top, tail), everything, step.add(out, picks)),
        ]
        terms = [
            (target, [(everything, numbers), ((slice(None), target[1]), new)])
            for target, _, numbers in terms
        ]
        terms.append(((slice(own, None),), everything, small_in))
        step.write((own + extra, columns), bf16, terms)
    att_sends = step.run("att_sum_plane")
    last = grid.send(att_sends, "z")

    grad_tokens = grad_one + dot_nt(dqkv, attention_weights[:, : 3 * width])

    step = Combine(grid, 1)
    new = step.read(ffn_new, (None, None, None))
    for j, addends in enumerate((up, down)):
        terms = [(everything, [(everything, step.add(addends, here)), ((j,), new)])]
        step.write((up_rows, hidden), f32, terms)
    up_own, down_own = step.run("ffn_sum_last")

    step = Combine(grid, 1)
    new = step.add(att_new, here)
    mine = step.add(att, here)
    last = step.read(last, (None, None))
    for j in range(3):
        terms = []
        for p in range(pairs):
            cols = slice((3 * p + j) * lanes, (3 * p + j + 1) * lanes)
            source = (slice(None), cols)
            terms.append(
                (
                    (slice(None), slice(p * lanes, (p + 1) * lanes)),
                    [(source, new + mine), ((slice(0, own), cols), last)],
                )
            )
        step.write((own, width), f32, terms)
    tail = slice(3 * width, None)
    terms = [
        (everything, step.add(out, here)),
        ((slice(None), tail), new),
        ((slice(0, own), tail), last),
    ]
    step.write((own, width), f32, [(everything, terms)])
    small_in = step.read(small, (None, None))

    def small_term(r, cols):
        row = lambda base: (slice(base + r, base + r + 1), cols)
        return [(row(0), small_in), (row(own), last)]

    step.write((columns,), f32, [(everything, small_term(0, slice(None)))])
    terms = []
    for kind, n, r, cols in places:
        if kind == "vec" and n < 5:
            step.write((width,), f32, [(everything, small_term(r, cols))])
        if kind == "bias":
            terms.append(((slice(n, n + 1),), small_term(r, cols)))
    step.write((heads, rels), f32, terms)
    dq, dk, dv, out_own, dup_bias, *dvec, dbias = step.run("last_sum")
    return (
        out_tokens,
        grad_tokens,
        dq,
        dk,
        dv,
        out_own,
        dbias,
        up_own,
        dup_bias,
        down_own,
        *dvec,
    )


def solution(mesh):
    both = P(("batch", "wide"), None)
    placed = (
        both,
        P(("batch", "wide")),
        P(("batch", "wide")),
        both,
        both,
        both,
        both,
        P(),
        P(),
        P("batch", "wide"),
        P(),
        P("batch", "wide"),
        P(),
        P(),
        P(),
        P(),
        P(),
        both,
    )
    outs = (
        both,
        both,
        both,
        both,
        both,
        both,
        P(),
        P("batch", "wide"),
        P(),
        P("batch", "wide"),
        P(),
        P(),
        P(),
        P(),
        P(),
    )
    return jax.shard_map(
        partial(per_device, mesh.shape["batch"], mesh.shape["wide"]),
        mesh=mesh,
        in_specs=placed,
        out_specs=outs,
        check_vma=False,
    )
```

```python
import itertools
from functools import partial

import jax
import jax.numpy as jnp
from jax import lax
from jax.experimental import pallas as pl
from jax.experimental.pallas import tpu as pltpu
from jax.sharding import PartitionSpec as P

BLK = 128
f32 = jnp.float32
bf16 = jnp.bfloat16
nt_dims = (((1,), (1,)), ((), ()))


def dot(a, b):
    return jnp.dot(a, b, preferred_element_type=f32)


def dot_nt(a, b):
    return lax.dot_general(a, b, nt_dims, preferred_element_type=f32)


def split_low(x):
    high = x.astype(bf16)
    return high, (x - high.astype(f32)).astype(bf16)


def toeplitz_kernel(bias_ref, out_ref):
    heads = bias_ref.shape[0]
    rels = bias_ref.shape[1]
    for h in range(heads):
        row = jnp.broadcast_to(jnp.exp(bias_ref[h : h + 1, :]), (BLK, rels))
        out_ref[h] = pltpu.roll(row, rels - BLK + 1, 1, stride=1, stride_axis=0)


def toeplitz_tables(flipped_bias):
    heads, rels = flipped_bias.shape
    step = 2
    return pl.pallas_call(
        toeplitz_kernel,
        grid=(heads // step,),
        in_specs=[pl.BlockSpec((None, step, rels), lambda h: (h, 0, 0))],
        out_specs=pl.BlockSpec((step, BLK, rels), lambda h: (h, 0, 0)),
        out_shape=jax.ShapeDtypeStruct((heads, BLK, rels), f32),
        cost_estimate=pl.CostEstimate(
            flops=5_000_000_000, bytes_accessed=8_000_000, transcendentals=0
        ),
        name="toeplitz",
    )(flipped_bias.reshape(heads // step, step, rels))


def lane_half(shape):
    return lax.broadcasted_iota(jnp.int32, shape, 1) < shape[1] // 2


def pair_features(u, feat_ref):
    high, low = split_low(u)
    square = u * u
    s_high, rest = split_low(square)
    rest = square - s_high.astype(f32)
    s_mid, s_low = split_low(rest)
    lhs = jnp.concatenate([high, high, low, s_high, s_mid, s_low], axis=1)
    return jnp.exp(dot(lhs, feat_ref[...]))


def attend_kernel(
    scale,
    tok_ref,
    w_ref,
    table_ref,
    mask_ref,
    feat_ref,
    mixed_ref,
    mixed32_ref,
    u_ref,
    phi_ref,
    val_ref,
    inv_ref,
    weights_ref,
):
    length = tok_ref.shape[0]
    pair = mixed_ref.shape[1]
    size = pair // 2
    blocks = length // BLK
    qkv = dot(tok_ref[...], w_ref[...])
    uq = qkv[:, :pair] * scale
    uk = qkv[:, pair : 2 * pair] * scale
    value = qkv[:, 2 * pair :].astype(bf16)
    pq = pair_features(uq, feat_ref)
    pk = pair_features(uk, feat_ref)
    u_ref[:, :pair] = uq
    u_ref[:, pair:] = uk
    phi_ref[:, :pair] = pq
    phi_ref[:, pair:] = pk
    val_ref[...] = value
    pq = pq.astype(bf16)
    pk = pk.astype(bf16)
    first = lane_half(value.shape)
    zero = jnp.zeros_like(value)
    one = jnp.ones_like(value)
    out = None
    for h in range(2):
        cols = slice(h * size, (h + 1) * size)
        here = first if h == 0 else jnp.logical_not(first)
        for b in range(blocks):
            rows = slice(b * BLK, (b + 1) * BLK)
            start = (blocks - 1 - b) * BLK
            scores = dot_nt(pq[rows, cols], pk[:, cols])
            coupling = table_ref[h, :, start : start + length] * mask_ref[b : b + 1, :]
            weights_ref[rows, :] = (coupling * scores).astype(bf16)
        rhs = jnp.concatenate([jnp.where(here, value, zero), jnp.where(here, one, zero)], axis=1)
        part = dot(weights_ref[...], rhs)
        out = part if out is None else out + part
    inverse = 1.0 / out[:, pair:]
    mixed = out[:, :pair] * inverse
    inv_ref[...] = inverse
    mixed32_ref[...] = mixed
    mixed_ref[...] = mixed.astype(bf16)


def attend(tokens, weights, tables, mask, feat_split, heads):
    length, width = tokens.shape
    pair = 2 * width // heads
    pairs = heads // 2
    rels = tables.shape[2]
    scale = float((pair // 2) ** (-0.25))
    whole = lambda shape: pl.BlockSpec(shape, lambda h: (0,) * len(shape))
    column = lambda cols: pl.BlockSpec((length, cols), lambda h: (0, h))
    return pl.pallas_call(
        partial(attend_kernel, scale),
        grid=(pairs,),
        in_specs=[
            whole((length, width)),
            pl.BlockSpec((width, 3 * pair), lambda h: (0, h)),
            pl.BlockSpec((2, BLK, rels), lambda h: (h, 0, 0)),
            whole(mask.shape),
            whole(feat_split.shape),
        ],
        out_specs=[
            column(pair),
            column(pair),
            column(2 * pair),
            column(2 * pair),
            column(pair),
            column(pair),
        ],
        out_shape=[
            jax.ShapeDtypeStruct((length, width), bf16),
            jax.ShapeDtypeStruct((length, width), f32),
            jax.ShapeDtypeStruct((length, 2 * width), f32),
            jax.ShapeDtypeStruct((length, 2 * width), f32),
            jax.ShapeDtypeStruct((length, width), bf16),
            jax.ShapeDtypeStruct((length, width), f32),
        ],
        scratch_shapes=[pltpu.VMEM((length, length), bf16)],
        cost_estimate=pl.CostEstimate(flops=0, bytes_accessed=0, transcendentals=0),
        name="attend",
    )(tokens, weights, tables, mask, feat_split)


def pair_backward(scale, grad_phi, phi, u, feat_ref):
    pair = u.shape[1]
    high, low = split_low(grad_phi * phi)
    back = dot(jnp.concatenate([high, high, low], axis=1), feat_ref[...])
    return (scale * (back[:, :pair] - u * back[:, pair:])).astype(bf16)


def attend_back_kernel(
    scale,
    place_ref,
    tok_t_ref,
    table_ref,
    mask_ref,
    feat_ref,
    swap_ref,
    turn_ref,
    u_ref,
    phi_ref,
    val_ref,
    inv_ref,
    mixed_ref,
    gm_ref,
    top_ref,
    dw_mine_ref,
    dw_other_ref,
    dqkv_ref,
    small_ref,
    probs_ref,
    gs_ref,
    diag_ref,
):
    length, pair = val_ref.shape
    size = pair // 2
    blocks = length // BLK

    @pl.when(pl.program_id(0) == 0)
    def _():
        small_ref[...] = top_ref[...]

    gm = gm_ref[...].astype(f32)
    scaled = gm * inv_ref[...]
    g_high, g_low = split_low(scaled)
    gt = scaled.T
    gt_high, gt_low = split_low(gt)
    d_high, d_low = split_low(scaled * mixed_ref[...])
    inner = dot(jnp.concatenate([d_high, d_low], axis=1), swap_ref[...])
    i_high, i_low = split_low(inner)
    phi = phi_ref[...]
    pq32, pk32 = phi[:, :pair], phi[:, pair:]
    pq = pq32.astype(bf16)
    pk = pk32.astype(bf16)
    pq_t = pq32.T.astype(bf16)
    value = val_ref[...]
    first = lane_half(value.shape)
    unit = jnp.full_like(value, 1.0 / size)
    zero = jnp.zeros_like(value)
    gq = None
    gk_heads = []
    gv_heads = []
    for h in range(2):
        cols = slice(h * size, (h + 1) * size)
        here = first if h == 0 else jnp.logical_not(first)
        lhs = jnp.concatenate(
            [jnp.where(here, g_high, i_high), jnp.where(here, g_low, i_low)], axis=1
        )
        rhs = jnp.where(here, value, unit)
        rhs = jnp.concatenate([rhs, rhs], axis=1)
        diag_ref[...] = jnp.zeros_like(diag_ref)
        for b in range(blocks):
            rows = slice(b * BLK, (b + 1) * BLK)
            start = (blocks - 1 - b) * BLK
            window = slice(start, start + length)
            mask = mask_ref[b : b + 1, :]
            scores = dot_nt(pq[rows, cols], pk[:, cols])
            coupling = table_ref[h, :, window] * mask
            probs_ref[rows, :] = (coupling * scores).astype(bf16)
            grad_scores = dot_nt(lhs[rows], rhs) * coupling
            gs_ref[rows, :] = grad_scores.astype(bf16)
            diag_ref[:, window] += grad_scores * scores
        part = dot(gs_ref[...], jnp.where(here, pk, zero))
        gq = part if gq is None else gq + part
        gk_heads.append(dot(pq_t[cols, :], gs_ref[...]))
        both = dot(jnp.concatenate([gt_high[cols], gt_low[cols]], axis=0), probs_ref[...])
        gv_heads.append(both[:size] + both[size:])
        folded = diag_ref[...]
        half = BLK // 2
        while half >= 1:
            folded = pltpu.roll(folded[:half], half, 1) + folded[half:]
            half //= 2
        split = [folded[:, n : n + BLK] for n in range(0, folded.shape[1], BLK)]
        f_high, rest = split_low(jnp.concatenate(split, axis=0))
        f_mid, f_low = split_low(jnp.concatenate(split, axis=0) - f_high.astype(f32))
        turned = dot(jnp.concatenate([f_high, f_mid, f_low], axis=1), turn_ref[...])
        turned = [turned[n : n + 1] for n in reversed(range(len(split)))]
        head = 2 * pl.program_id(0) + h
        rels = table_ref.shape[2]
        per_row = small_ref.shape[1] // rels
        column = pl.multiple_of(lax.rem(head, per_row) * rels, rels)
        row = small_ref.shape[0] - pl.num_programs(0) * 2 // per_row + head // per_row
        small_ref[pl.ds(row, 1), pl.ds(column, rels)] = jnp.concatenate(turned, axis=1)
    gk = jnp.concatenate(gk_heads, axis=0).T
    gv = jnp.concatenate(gv_heads, axis=0).T.astype(bf16)
    u = u_ref[...]
    dq = pair_backward(scale, gq, pq32, u[:, :pair], feat_ref)
    dk = pair_backward(scale, gk, pk32, u[:, pair:], feat_ref)
    dqkv_ref[:, :pair] = dq
    dqkv_ref[:, pair : 2 * pair] = dk
    dqkv_ref[:, 2 * pair :] = gv
    half = tok_t_ref.shape[0] // 2
    place = place_ref[0]
    mine = pl.ds(pl.multiple_of(place * half, half), half)
    other = pl.ds(pl.multiple_of((1 - place) * half, half), half)
    dw_mine_ref[...] = dot(tok_t_ref[mine, :], dqkv_ref[...]).astype(bf16)
    dw_other_ref[...] = dot(tok_t_ref[other, :], dqkv_ref[...]).astype(bf16)


def attend_back(
    place,
    tokens_t,
    tables,
    mask,
    feat_back,
    swap,
    turn,
    u,
    phi,
    value,
    inverse,
    mixed,
    grad_mixed,
    small_top,
    heads,
):
    width, length = tokens_t.shape
    pair = 2 * width // heads
    rels = tables.shape[2]
    scale = float((pair // 2) ** (-0.25))
    whole = lambda shape: pl.BlockSpec(shape, lambda h, p: (0,) * len(shape))
    column = lambda cols: pl.BlockSpec((length, cols), lambda h, p: (0, h))
    own_column = lambda rows: pl.BlockSpec((rows, 3 * pair), lambda h, p: (0, h))
    return pl.pallas_call(
        partial(attend_back_kernel, scale),
        grid_spec=pltpu.PrefetchScalarGridSpec(
            num_scalar_prefetch=1,
            grid=(heads // 2,),
            in_specs=[
                whole((width, length)),
                pl.BlockSpec((2, BLK, rels), lambda h, p: (h, 0, 0)),
                whole(mask.shape),
                whole(feat_back.shape),
                whole(swap.shape),
                whole(turn.shape),
                column(2 * pair),
                column(2 * pair),
                column(pair),
                column(pair),
                column(pair),
                column(pair),
                whole(small_top.shape),
            ],
            out_specs=[
                own_column(width // 2),
                own_column(width // 2),
                own_column(length),
                whole(small_top.shape),
            ],
            scratch_shapes=[
                pltpu.VMEM((length, length), bf16),
                pltpu.VMEM((length, length), bf16),
                pltpu.VMEM((BLK, rels), f32),
            ],
        ),
        out_shape=[
            jax.ShapeDtypeStruct((width // 2, 3 * width), bf16),
            jax.ShapeDtypeStruct((width // 2, 3 * width), bf16),
            jax.ShapeDtypeStruct((length, 3 * width), bf16),
            jax.ShapeDtypeStruct(small_top.shape, f32),
        ],
        cost_estimate=pl.CostEstimate(flops=0, bytes_accessed=0, transcendentals=0),
        name="attend_back",
    )(place, tokens_t, tables, mask, feat_back, swap, turn, u, phi, value, inverse, mixed, grad_mixed, small_top)


def block_diagonal(matrix):
    zero = jnp.zeros_like(matrix)
    return jnp.concatenate(
        [jnp.concatenate([matrix, zero], axis=1), jnp.concatenate([zero, matrix], axis=1)], axis=0
    )


def feature_tables(features):
    size = features.shape[0]
    ones = block_diagonal(jnp.ones((size, size), f32)).astype(bf16)
    high, low = split_low(block_diagonal(features))
    half = ones * -0.5
    forward = jnp.concatenate([high, low, high, half, half, half], axis=0)
    high, low = split_low(block_diagonal(features.T))
    none = jnp.zeros_like(ones)
    backward = jnp.concatenate(
        [jnp.concatenate([high, low, high], axis=0), jnp.concatenate([ones, none, ones], axis=0)],
        axis=1,
    )
    swap = jnp.concatenate([-ones[:, size:], -ones[:, :size]], axis=1)
    turn = jnp.eye(BLK, dtype=bf16)[::-1]
    return forward, backward, jnp.concatenate([swap, swap], axis=0), jnp.tile(turn, (3, 1))


def prepare_kernel(q_ref, k_ref, v_ref, o_ref, up_ref, down_ref, att_ref, ffn_ref):
    width = o_ref.shape[1]
    lanes = att_ref.shape[1] // 4 // (width // 128)
    for j, ref in enumerate((q_ref, k_ref, v_ref)):
        for p in range(width // lanes):
            to = (3 * p + j) * lanes
            att_ref[:, to : to + lanes] = ref[:, p * lanes : (p + 1) * lanes].astype(bf16)
    att_ref[:, 3 * width :] = o_ref[...].astype(bf16)
    rows = up_ref.shape[0]
    ffn_ref[:rows] = up_ref[...].astype(bf16)
    ffn_ref[rows:] = down_ref[...].astype(bf16)


def prepare(query, key, value, out, up, down):
    own, width = query.shape
    return pl.pallas_call(
        prepare_kernel,
        out_shape=[
            jax.ShapeDtypeStruct((own, 4 * width), bf16),
            jax.ShapeDtypeStruct((2 * up.shape[0], up.shape[1]), bf16),
        ],
        name="prepare",
    )(query, key, value, out, up, down)


root_half = 0.7071067811865476
inv_root_two_pi = 0.3989422804014327
eps = 1e-05


def norm_stats(residual):
    centered = residual - jnp.mean(residual, axis=1, keepdims=True)
    inverse = lax.rsqrt(jnp.mean(centered * centered, axis=1, keepdims=True) + eps)
    return centered * inverse, inverse


def norm_back(grad, xhat, inverse, gain):
    scaled = grad * gain
    mean_grad = jnp.mean(scaled, axis=1, keepdims=True)
    mean_dot = jnp.mean(scaled * xhat, axis=1, keepdims=True)
    return (scaled - mean_grad - xhat * mean_dot) * inverse


def column_sum(x):
    return jnp.sum(x, axis=0, keepdims=True)


def ffn_kernel(
    place_ref,
    tok_ref,
    mixed_ref,
    mixed_t_ref,
    wo_ref,
    up_ref,
    down_ref,
    up_bias_ref,
    vec_ref,
    live_ref,
    cot_ref,
    out_ref,
    grad_one_ref,
    gm_ref,
    up_other_ref,
    up_mine_ref,
    down_other_ref,
    down_mine_ref,
    wo_other_ref,
    wo_mine_ref,
    dup_bias_ref,
    dvec_ref,
    normed_ref,
    low_ref,
    low_t_ref,
    xhat_ref,
    inv_ref,
    act_ref,
    slope_ref,
    acc_ref,
    gb_ref,
    gb_t_ref,
):
    phase = pl.program_id(0)
    part = pl.program_id(1)
    parts = pl.num_programs(1)
    length, width = tok_ref.shape
    rows, hidden = up_ref.shape[1:]
    vec = vec_ref[...]
    down_bias, gain_one, shift_one, gain_two, shift_two = (vec[i : i + 1] for i in range(5))

    @pl.when((phase == 0) & (part == 0))
    def _():
        residual = tok_ref[...].astype(f32) + dot(mixed_ref[...], wo_ref[...])
        xhat, inverse = norm_stats(residual)
        normed = xhat * gain_one + shift_one
        xhat_ref[...] = xhat
        inv_ref[...] = inverse
        normed_ref[...] = normed
        low_ref[...] = normed.astype(bf16)
        low_t_ref[...] = normed.T.astype(bf16)
        acc_ref[...] = jnp.zeros_like(acc_ref)

    @pl.when(phase == 0)
    def _():
        up = up_ref[...].reshape(width, hidden)
        down = down_ref[...].reshape(width, hidden)
        v = dot(low_ref[...], up) + up_bias_ref[...]
        half = 0.5 + 0.5 * lax.erf(v * root_half)
        act = (v * half).astype(bf16)
        act_ref[part] = act
        slope_ref[part] = half + v * (jnp.exp(-0.5 * v * v) * inv_root_two_pi)
        acc_ref[...] += dot_nt(act, down)

    @pl.when((phase == 0) & (part == parts - 1))
    def _():
        live = live_ref[...]
        xhat, inverse = norm_stats(normed_ref[...] + (acc_ref[...] + down_bias))
        out_ref[...] = ((xhat * gain_two + shift_two) * live).astype(bf16)
        grad = cot_ref[...].astype(f32) * live
        grad_two = norm_back(grad, xhat, inverse, gain_two)
        low = grad_two.astype(bf16)
        gb_ref[...] = low
        gb_t_ref[...] = grad_two.T.astype(bf16)
        dvec_ref[0:1, :] = column_sum(low.astype(f32))
        dvec_ref[3:4, :] = column_sum(grad * xhat)
        dvec_ref[4:5, :] = column_sum(grad)
        dvec_ref[5:8, :] = jnp.zeros((3, width), f32)
        acc_ref[...] = grad_two

    def backward(d_up_ref, d_down_ref):
        up = up_ref[...].reshape(width, hidden)
        down = down_ref[...].reshape(width, hidden)
        grad_act = dot(gb_ref[...], down)
        grad_hidden = (grad_act * slope_ref[part]).astype(bf16)
        dup_bias_ref[...] = column_sum(grad_hidden.astype(f32))
        d_up = dot(low_t_ref[...], grad_hidden).astype(bf16)
        d_down = dot(gb_t_ref[...], act_ref[part]).astype(bf16)
        d_up_ref[...] = d_up.reshape(-1, rows, hidden)
        d_down_ref[...] = d_down.reshape(-1, rows, hidden)
        acc_ref[...] += dot_nt(grad_hidden, up)

    @pl.when((phase == 1) & (part < parts // 2))
    def _():
        backward(up_other_ref, down_other_ref)

    @pl.when((phase == 1) & (part >= parts // 2))
    def _():
        backward(up_mine_ref, down_mine_ref)

    @pl.when((phase == 1) & (part == parts - 1))
    def _():
        grad = acc_ref[...]
        xhat = xhat_ref[...]
        grad_one = norm_back(grad, xhat, inv_ref[...], gain_one)
        grad_one_ref[...] = grad_one
        grad_att = grad_one.astype(bf16)
        gm_ref[...] = dot_nt(grad_att, wo_ref[...]).astype(bf16)
        half = width // 2
        place = place_ref[0]
        mine = pl.ds(pl.multiple_of(place * half, half), half)
        other = pl.ds(pl.multiple_of((1 - place) * half, half), half)
        wo_mine_ref[...] = dot(mixed_t_ref[mine, :], grad_att).astype(bf16)
        wo_other_ref[...] = dot(mixed_t_ref[other, :], grad_att).astype(bf16)
        dvec_ref[1:2, :] = column_sum(grad * xhat)
        dvec_ref[2:3, :] = column_sum(grad)


def feed_forward(
    place, tokens, mixed, mixed_t, attention_weights, weights, up_bias, vectors, live, cotangent
):
    length, width = tokens.shape
    parts, shards, _, rows, hidden = weights.shape
    xs = parts // 2
    whole = lambda shape: pl.BlockSpec(shape, lambda p, w, c: (0,) * len(shape))
    once = lambda shape: pl.BlockSpec(
        shape, lambda p, w, c: (0,) * len(shape), pipeline_mode=pl.Buffered(1)
    )
    wo_column = attention_weights.shape[1] // width - 1
    wide = (length, width)
    part_of = lambda w, c: 2 * lax.rem(w, xs) + jnp.where(w < xs, 1 - c[0], c[0])
    weight_spec = lambda which: pl.BlockSpec(
        (None, shards, None, rows, hidden), lambda p, w, c: (part_of(w, c), 0, which, 0, 0)
    )
    other_spec = pl.BlockSpec(
        (None, shards, rows, hidden), lambda p, w, c: (p * jnp.minimum(w, xs - 1), 0, 0, 0)
    )
    mine_spec = pl.BlockSpec(
        (None, shards, rows, hidden), lambda p, w, c: (p * jnp.maximum(w - xs, 0), 0, 0, 0)
    )
    grads = jax.ShapeDtypeStruct((xs, shards, rows, hidden), bf16)
    return pl.pallas_call(
        ffn_kernel,
        grid_spec=pltpu.PrefetchScalarGridSpec(
            num_scalar_prefetch=1,
            grid=(2, parts),
            in_specs=[
                once(wide),
                once(wide),
                once((width, length)),
                pl.BlockSpec(
                    (width, width), lambda p, w, c: (0, wo_column), pipeline_mode=pl.Buffered(1)
                ),
                weight_spec(0),
                weight_spec(1),
                pl.BlockSpec((None, 1, hidden), lambda p, w, c: (part_of(w, c), 0, 0)),
                whole(vectors.shape),
                once((length, 1)),
                once(wide),
            ],
            out_specs=[
                whole(wide),
                whole(wide),
                whole(wide),
                other_spec,
                mine_spec,
                other_spec,
                mine_spec,
                whole((width // 2, width)),
                whole((width // 2, width)),
                pl.BlockSpec(
                    (None, 1, hidden), lambda p, w, c: (part_of(w * p, c), 0, 0)
                ),
                whole((8, width)),
            ],
            scratch_shapes=[
                pltpu.VMEM(wide, f32),
                pltpu.VMEM(wide, bf16),
                pltpu.VMEM((width, length), bf16),
                pltpu.VMEM(wide, f32),
                pltpu.VMEM((length, 1), f32),
                pltpu.VMEM((parts, length, hidden), bf16),
                pltpu.VMEM((parts, length, hidden), f32),
                pltpu.VMEM(wide, f32),
                pltpu.VMEM(wide, bf16),
                pltpu.VMEM((width, length), bf16),
            ],
        ),
        out_shape=[
            jax.ShapeDtypeStruct(wide, bf16),
            jax.ShapeDtypeStruct(wide, f32),
            jax.ShapeDtypeStruct(wide, bf16),
            grads,
            grads,
            grads,
            grads,
            jax.ShapeDtypeStruct((width // 2, width), bf16),
            jax.ShapeDtypeStruct((width // 2, width), bf16),
            jax.ShapeDtypeStruct((parts, 1, hidden), f32),
            jax.ShapeDtypeStruct((8, width), f32),
        ],
        compiler_params=pltpu.CompilerParams(vmem_limit_bytes=58 * 1024 * 1024),
        cost_estimate=pl.CostEstimate(flops=0, bytes_accessed=0, transcendentals=0),
        name="feed_forward",
    )(
        place,
        tokens,
        mixed,
        mixed_t,
        attention_weights,
        weights,
        weights,
        up_bias,
        vectors,
        live,
        cotangent,
    )


class Grid:
    def __init__(self, batch, wide):
        self.devices = batch * wide
        self.sizes = dict(z=4, y=batch // 4, x=wide // 2, c=2)
        self.strides = dict(z=batch // 4 * wide, y=wide, x=2, c=1)
        flat = lax.axis_index("batch") * wide + lax.axis_index("wide")
        self.place = {d: lax.rem(flat // self.strides[d], n) for d, n in self.sizes.items()}
        self.vector = jnp.stack([self.place[d] for d in "zyxc"])

    def shift(self, value, **offsets):
        pairs = []
        for i in range(self.devices):
            target = i
            for d, o in offsets.items():
                s, n = self.strides[d], self.sizes[d]
                target += ((i // s + o) % n - i // s % n) * s
            pairs.append((i, target))
        return lax.ppermute(value, ("batch", "wide"), pairs)

    def at(self, d, offset):
        return lax.rem(self.place[d] + (offset + self.sizes[d]), self.sizes[d])

    def block_at(self, d, offset):
        k, n = "zyxc".index(d), self.sizes[d]
        return lambda vector: lax.rem(vector[k] + offset, n)

    def offsets(self, dims):
        ranges = [range(self.sizes[d]) for d in dims]
        return [dict(zip(dims, o)) for o in itertools.product(*ranges)]

    def gather(self, value, names, dims):
        parts = [(o, self.shift(value, **o) if any(o.values()) else value) for o in self.offsets(dims)]
        if len(parts) == 2:
            (d,) = dims
            own, other = value, parts[1][1]
            first = self.place[d] == 0
            return jnp.concatenate(
                [jnp.where(first, own, other), jnp.where(first, other, own)], axis=names.index(d)
            )
        shape = [self.sizes[d] if d in dims else n for d, n in zip(names, value.shape)]
        out = jnp.zeros(shape + list(value.shape[len(names) :]), value.dtype)
        for o, part in parts:
            start = [self.at(d, -o[d]) if d in dims else 0 for d in names]
            out = lax.dynamic_update_slice(out, part, start + [0] * (value.ndim - len(names)))
        return out

    def send(self, sends, dims):
        return [self.shift(value, **o) for o, value in zip(self.offsets(dims)[1:], sends)]


class Combine:
    def __init__(self, grid, steps):
        self.grid, self.steps = grid, steps
        self.inputs, self.in_specs, self.shapes, self.out_specs, self.terms = [], [], [], [], []

    def spec(self, block, where):
        picks = []
        for w in where:
            if w is None:
                picks.append(lambda i, v: 0)
            elif w == "step":
                picks.append(lambda i, v: i)
            else:
                at = self.grid.block_at(*w)
                picks.append(lambda i, v, at=at: at(v))
        return pl.BlockSpec(block, lambda i, v: tuple(p(i, v) for p in picks))

    def read(self, arrays, where):
        numbers = []
        for a in arrays:
            block = tuple(n if w is None else None for n, w in zip(a.shape, where))
            numbers.append(len(self.inputs))
            self.inputs.append(a)
            self.in_specs.append(self.spec(block, where))
        return numbers

    def add(self, addends, picks):
        numbers = []
        for names, array in addends:
            where = tuple(picks.get(d) for d in names)
            where = tuple((d, w) if isinstance(w, int) else w for d, w in zip(names, where))
            numbers += self.read([array], where + (None,) * (array.ndim - len(names)))
        return numbers

    def write(self, shape, dtype, terms, stepped=None):
        where = tuple("step" if n == stepped else None for n in range(len(shape)))
        block = tuple(n if w is None else None for n, w in zip(shape, where))
        self.shapes.append(jax.ShapeDtypeStruct(shape, dtype))
        self.out_specs.append(self.spec(block, where))
        self.terms.append(terms)

    def run(self, name):
        count = len(self.inputs)

        def kernel(vector_ref, *refs):
            for out_ref, terms in zip(refs[count:], self.terms):
                for target, *rest in terms:
                    total = None
                    for source, numbers in [rest] if len(rest) == 2 else rest[0]:
                        for n in numbers:
                            value = refs[n][source].astype(f32)
                            total = value if total is None else total + value
                    total = total.astype(out_ref.dtype)
                    if len(out_ref.shape) == 1:
                        total = total.reshape(out_ref.shape)
                    out_ref[target] = total

        return pl.pallas_call(
            kernel,
            grid_spec=pltpu.PrefetchScalarGridSpec(
                num_scalar_prefetch=1,
                grid=(self.steps,),
                in_specs=self.in_specs,
                out_specs=self.out_specs,
            ),
            out_shape=self.shapes,
            compiler_params=pltpu.CompilerParams(vmem_limit_bytes=60 * 1024 * 1024),
            cost_estimate=pl.CostEstimate(flops=0, bytes_accessed=0, transcendentals=0),
            name=name,
        )(self.grid.vector, *self.inputs)


everything = (Ellipsis,)


def hold(value, *others):
    return lax.optimization_barrier((value, others))


def per_device(
    batch,
    wide,
    tokens,
    block_row,
    block_live,
    query_weight,
    key_weight,
    value_weight,
    out_weight,
    position_bias,
    features,
    up_weight,
    up_bias,
    down_weight,
    down_bias,
    gain_one,
    shift_one,
    gain_two,
    shift_two,
    cotangent,
):
    grid = Grid(batch, wide)
    zs, ys, xs, cs = (grid.sizes[d] for d in "zyxc")
    length, width = tokens.shape
    heads, rels = position_bias.shape
    pairs = heads // 2
    own = query_weight.shape[0]
    lanes = width // pairs
    shard, ffn_shard = prepare(
        query_weight, key_weight, value_weight, out_weight, up_weight, down_weight
    )
    tables = toeplitz_tables(position_bias[:, ::-1])
    feat_forward, feat_back, swap, turn = feature_tables(features)
    offsets = jnp.arange(BLK, dtype=jnp.int32)
    live = (offsets[None, :] < block_live[:, None]).astype(f32).reshape(1, length)
    rows = jnp.broadcast_to(block_row[:, None], (block_row.shape[0], BLK)).reshape(1, length)
    mask = jnp.where(block_row[:, None] == rows, live, 0.0)
    by_core = lambda m: m.reshape(-1, cs, own, length).swapaxes(0, 1).reshape(width, length)
    tokens_t = by_core(tokens.T)
    vectors = jnp.stack([down_bias, gain_one, shift_one, gain_two, shift_two] + [down_bias] * 3)
    live_column = live.reshape(length, 1)

    up_rows, hidden = up_weight.shape
    gathered = grid.gather(shard.reshape(1, 1, 1, 1, own, 4 * width), "zyxc", "z")
    gathered = grid.gather(gathered, "zyxc", "yx")
    early = (tables, feat_forward, feat_back, swap, turn, mask, tokens_t, vectors, live_column)
    gathered, early = hold(gathered, *early)
    tables, feat_forward, feat_back, swap, turn, mask, tokens_t, vectors, live_column = early
    attention_weights = grid.gather(gathered, "zyxc", "c").reshape(width, 4 * width)
    ffn_weights = lax.all_gather(ffn_shard, ("wide", "batch"), axis=0, tiled=False)
    ffn_weights = ffn_weights.reshape(wide, batch, 2, up_rows, hidden)
    mixed, mixed32, u, phi, value, inverse = attend(
        tokens, attention_weights, tables, mask, feat_forward, heads
    )
    place = grid.place["c"].reshape(1)
    (
        out_tokens,
        grad_one,
        grad_mixed,
        up_other_grad,
        up_mine_grad,
        down_other,
        down_mine,
        out_other,
        out_mine,
        dup_bias,
        dvec,
    ) = feed_forward(
        place,
        tokens,
        mixed,
        by_core(mixed.T),
        attention_weights,
        ffn_weights,
        up_bias.reshape(wide, 1, hidden),
        vectors,
        live_column,
        cotangent,
    )
    ffn_view = lambda m: ("xzy", m.reshape(xs, zs, ys, up_rows, hidden))
    att_view = lambda m: ("zyx", m.reshape(zs, ys, xs, own, -1))
    down_recv = grid.shift(down_other, c=1)
    up = [ffn_view(up_mine_grad), ffn_view(grid.shift(up_other_grad, c=1))]
    out = [att_view(out_mine), att_view(grid.shift(out_other, c=1))]

    columns = 4 * width
    bias_rows = heads * rels // columns
    extra = -(-(3 + bias_rows) // 8) * 8
    first_row = extra - bias_rows
    small_top = jnp.concatenate(
        [dup_bias.reshape(1, columns), dvec.reshape(2, columns), jnp.zeros((extra - 3, columns), f32)]
    )
    down_mine, (small_top,) = hold(down_mine, small_top)
    down = [ffn_view(down_mine), ffn_view(down_recv)]

    step = Combine(grid, zs)
    for y in range(1, ys):
        terms = [(everything, everything, step.add(down, dict(z="step", y=y)))]
        step.write((xs, zs, up_rows, hidden), bf16, terms, stepped=1)
    for x in range(1, xs):
        terms = [(everything, everything, step.add(up, dict(z="step", x=x)))]
        step.write((zs, ys, up_rows, hidden), bf16, terms, stepped=0)
    sends = step.run("ffn_sum_core")
    down_sends, up_sends = sends[: ys - 1], sends[ys - 1 :]
    grad_mixed, (down_sends, up_sends) = hold(grad_mixed, down_sends, up_sends)
    down_new = grid.send(down_sends, "y")
    up_new = grid.send(up_sends, "x")

    dw_mine, dw_other, dqkv, small = attend_back(
        place,
        tokens_t,
        tables,
        mask,
        feat_back,
        swap,
        turn,
        u,
        phi,
        value,
        inverse,
        mixed32,
        grad_mixed,
        small_top,
        heads,
    )
    dw_mine, (dw_other, dqkv, small, down_new, up_new) = hold(
        dw_mine, dw_other, dqkv, small, down_new, up_new
    )
    down += [("xz", v) for v in down_new]
    up += [("zy", v) for v in up_new]
    att = [att_view(dw_mine), att_view(grid.shift(dw_other, c=1))]

    step = Combine(grid, 1)
    block = (zs, up_rows, hidden)
    for x in range(1, xs):
        terms = [(everything, everything, step.add(down, dict(y=0, x=x)))]
        step.write(block, bf16, terms)
    for y in range(1, ys):
        terms = [(everything, everything, step.add(up, dict(x=0, y=y)))]
        step.write(block, bf16, terms)
    sends = step.run("ffn_sum_plane")
    down_new = grid.send(sends[: xs - 1], "x")
    up_new = grid.send(sends[xs - 1 :], "y")
    small = small + grid.shift(small, c=1)
    small = [small] + grid.send([small.astype(bf16)] * (ys * xs - 1), "yx")
    dw_mine, sends = hold(dw_mine, *sends)
    att[0] = att_view(dw_mine)
    step = Combine(grid, 1)
    for o in grid.offsets("yx")[1:]:
        terms = [
            ((..., slice(0, 3 * width)), everything, step.add(att, o)),
            ((..., slice(3 * width, None)), everything, step.add(out, o)),
        ]
        step.write((zs, own, columns), bf16, terms)
    att_sends = step.run("att_sum_core")
    down_new, (up_new, att_sends, small) = hold(down_new, up_new, att_sends, small)
    down += [("z", v) for v in down_new]
    up += [("z", v) for v in up_new]
    att_new = grid.send(att_sends, "yx")

    here = dict(z=0, y=0, x=0)
    step = Combine(grid, 1)
    for z in range(1, zs):
        terms = [
            ((j,), everything, step.add(addends, dict(z=z, y=0, x=0)))
            for j, addends in enumerate((up, down))
        ]
        step.write((2, up_rows, hidden), bf16, terms)
    sends = step.run("ffn_sum_second")
    ffn_new = grid.send(sends, "z")
    grad_tokens = grad_one + dot_nt(dqkv, attention_weights[:, : 3 * width])
    att_new, (grad_tokens, *sends) = hold(att_new, grad_tokens, *sends)
    att_new = [("z", v) for v in att_new]

    step = Combine(grid, 1)
    small_in = step.read(small, (None, None))
    for z in range(1, zs):
        picks = dict(z=z, y=0, x=0)
        top = slice(0, own)
        new = step.add(att_new, picks)
        head, tail = slice(0, 3 * width), slice(3 * width, None)
        terms = [
            ((top, head), everything, step.add(att, picks)),
            ((top, tail), everything, step.add(out, picks)),
        ]
        terms = [
            (target, [(everything, numbers), ((slice(None), target[1]), new)])
            for target, _, numbers in terms
        ]
        terms.append(((slice(own, None),), everything, small_in))
        step.write((own + extra, columns), bf16, terms)
    att_sends = step.run("att_sum_plane")
    last = grid.send(att_sends, "z")

    step = Combine(grid, 1)
    new = step.read(ffn_new, (None, None, None))
    for j, addends in enumerate((up, down)):
        terms = [(everything, [(everything, step.add(addends, here)), ((j,), new)])]
        step.write((up_rows, hidden), f32, terms)
    up_own, down_own = step.run("ffn_sum_last")

    step = Combine(grid, 1)
    new = step.add(att_new, here)
    head = (slice(None), slice(0, 3 * width))
    tail = (slice(None), slice(3 * width, None))
    top = slice(0, own)
    terms = [
        ((top, head[1]), [(everything, step.add(att, here)), (head, new)]),
        ((top, tail[1]), [(everything, step.add(out, here)), (tail, new)]),
        ((slice(own, None),), everything, step.read(small, (None, None))),
    ]
    step.write((own + extra, columns), f32, terms)
    (before,) = step.run("att_sum_own")

    step = Combine(grid, 1)
    last = step.read([before, *last], (None, None))
    for j in range(3):
        terms = []
        for p in range(pairs):
            cols = slice((3 * p + j) * lanes, (3 * p + j + 1) * lanes)
            terms.append(((slice(None), slice(p * lanes, (p + 1) * lanes)), (top, cols), last))
        step.write((own, width), f32, terms)
    step.write((own, width), f32, [(everything, (top, tail[1]), last)])

    def small_term(r, cols):
        return [((slice(own + r, own + r + 1), cols), last)]

    step.write((columns,), f32, [(everything, small_term(0, slice(None)))])
    for j in range(5):
        at = j % 4 * width
        step.write((width,), f32, [(everything, small_term(1 + j // 4, slice(at, at + width)))])
    per_row = columns // rels
    terms = []
    for h in range(heads):
        at = h % per_row * rels
        term = small_term(first_row + h // per_row, slice(at, at + rels))
        terms.append(((slice(h, h + 1),), term))
    step.write((heads, rels), f32, terms)
    dq, dk, dv, out_own, dup_bias, *dvec, dbias = step.run("last_sum")
    return (
        out_tokens,
        grad_tokens,
        dq,
        dk,
        dv,
        out_own,
        dbias,
        up_own,
        dup_bias,
        down_own,
        *dvec,
    )


def solution(mesh):
    both = P(("batch", "wide"), None)
    placed = (
        both,
        P(("batch", "wide")),
        P(("batch", "wide")),
        both,
        both,
        both,
        both,
        P(),
        P(),
        P("batch", "wide"),
        P(),
        P("batch", "wide"),
        P(),
        P(),
        P(),
        P(),
        P(),
        both,
    )
    outs = (
        both,
        both,
        both,
        both,
        both,
        both,
        P(),
        P("batch", "wide"),
        P(),
        P("batch", "wide"),
        P(),
        P(),
        P(),
        P(),
        P(),
    )
    return jax.shard_map(
        partial(per_device, mesh.shape["batch"], mesh.shape["wide"]),
        mesh=mesh,
        in_specs=placed,
        out_specs=outs,
        check_vma=False,
    )
```

```python
import itertools
from functools import partial

import jax
import jax.numpy as jnp
from jax import lax
from jax.experimental import pallas as pl
from jax.experimental.pallas import tpu as pltpu
from jax.sharding import PartitionSpec as P

BLK = 128
f32 = jnp.float32
bf16 = jnp.bfloat16
nt_dims = (((1,), (1,)), ((), ()))


def dot(a, b):
    return jnp.dot(a, b, preferred_element_type=f32)


def dot_nt(a, b):
    return lax.dot_general(a, b, nt_dims, preferred_element_type=f32)


def split_low(x):
    high = x.astype(bf16)
    return high, (x - high.astype(f32)).astype(bf16)


def toeplitz_kernel(bias_ref, out_ref):
    heads = bias_ref.shape[0]
    rels = bias_ref.shape[1]
    for h in range(heads):
        row = jnp.broadcast_to(jnp.exp(bias_ref[h : h + 1, :]), (BLK, rels))
        out_ref[h] = pltpu.roll(row, rels - BLK + 1, 1, stride=1, stride_axis=0)


def toeplitz_tables(flipped_bias):
    heads, rels = flipped_bias.shape
    step = 2
    return pl.pallas_call(
        toeplitz_kernel,
        grid=(heads // step,),
        in_specs=[pl.BlockSpec((None, step, rels), lambda h: (h, 0, 0))],
        out_specs=pl.BlockSpec((step, BLK, rels), lambda h: (h, 0, 0)),
        out_shape=jax.ShapeDtypeStruct((heads, BLK, rels), f32),
        cost_estimate=pl.CostEstimate(
            flops=5_000_000_000, bytes_accessed=8_000_000, transcendentals=0
        ),
        name="toeplitz",
    )(flipped_bias.reshape(heads // step, step, rels))


def lane_half(shape):
    return lax.broadcasted_iota(jnp.int32, shape, 1) < shape[1] // 2


def pair_features(u, feat_ref):
    high, low = split_low(u)
    square = u * u
    s_high, rest = split_low(square)
    rest = square - s_high.astype(f32)
    s_mid, s_low = split_low(rest)
    lhs = jnp.concatenate([high, high, low, s_high, s_mid, s_low], axis=1)
    return jnp.exp(dot(lhs, feat_ref[...]))


def attend_kernel(
    scale,
    tok_ref,
    w_ref,
    table_ref,
    mask_ref,
    feat_ref,
    mixed_ref,
    mixed32_ref,
    u_ref,
    phi_ref,
    val_ref,
    inv_ref,
    weights_ref,
):
    length = tok_ref.shape[0]
    pair = mixed_ref.shape[1]
    size = pair // 2
    blocks = length // BLK
    qkv = dot(tok_ref[...], w_ref[...])
    uq = qkv[:, :pair] * scale
    uk = qkv[:, pair : 2 * pair] * scale
    value = qkv[:, 2 * pair :].astype(bf16)
    pq = pair_features(uq, feat_ref)
    pk = pair_features(uk, feat_ref)
    u_ref[:, :pair] = uq
    u_ref[:, pair:] = uk
    phi_ref[:, :pair] = pq
    phi_ref[:, pair:] = pk
    val_ref[...] = value
    pq = pq.astype(bf16)
    pk = pk.astype(bf16)
    first = lane_half(value.shape)
    zero = jnp.zeros_like(value)
    one = jnp.ones_like(value)
    out = None
    for h in range(2):
        cols = slice(h * size, (h + 1) * size)
        here = first if h == 0 else jnp.logical_not(first)
        for b in range(blocks):
            rows = slice(b * BLK, (b + 1) * BLK)
            start = (blocks - 1 - b) * BLK
            scores = dot_nt(pq[rows, cols], pk[:, cols])
            coupling = table_ref[h, :, start : start + length] * mask_ref[b : b + 1, :]
            weights_ref[rows, :] = (coupling * scores).astype(bf16)
        rhs = jnp.concatenate([jnp.where(here, value, zero), jnp.where(here, one, zero)], axis=1)
        part = dot(weights_ref[...], rhs)
        out = part if out is None else out + part
    inverse = 1.0 / out[:, pair:]
    mixed = out[:, :pair] * inverse
    inv_ref[...] = inverse
    mixed32_ref[...] = mixed
    mixed_ref[...] = mixed.astype(bf16)


def attend(tokens, weights, tables, mask, feat_split, heads):
    length, width = tokens.shape
    pair = 2 * width // heads
    pairs = heads // 2
    rels = tables.shape[2]
    scale = float((pair // 2) ** (-0.25))
    whole = lambda shape: pl.BlockSpec(shape, lambda h: (0,) * len(shape))
    column = lambda cols: pl.BlockSpec((length, cols), lambda h: (0, h))
    return pl.pallas_call(
        partial(attend_kernel, scale),
        grid=(pairs,),
        in_specs=[
            whole((length, width)),
            pl.BlockSpec((width, 3 * pair), lambda h: (0, h)),
            pl.BlockSpec((2, BLK, rels), lambda h: (h, 0, 0)),
            whole(mask.shape),
            whole(feat_split.shape),
        ],
        out_specs=[
            column(pair),
            column(pair),
            column(2 * pair),
            column(2 * pair),
            column(pair),
            column(pair),
        ],
        out_shape=[
            jax.ShapeDtypeStruct((length, width), bf16),
            jax.ShapeDtypeStruct((length, width), f32),
            jax.ShapeDtypeStruct((length, 2 * width), f32),
            jax.ShapeDtypeStruct((length, 2 * width), f32),
            jax.ShapeDtypeStruct((length, width), bf16),
            jax.ShapeDtypeStruct((length, width), f32),
        ],
        scratch_shapes=[pltpu.VMEM((length, length), bf16)],
        cost_estimate=pl.CostEstimate(flops=0, bytes_accessed=0, transcendentals=0),
        name="attend",
    )(tokens, weights, tables, mask, feat_split)


def pair_backward(scale, grad_phi, phi, u, feat_ref):
    pair = u.shape[1]
    high, low = split_low(grad_phi * phi)
    back = dot(jnp.concatenate([high, high, low], axis=1), feat_ref[...])
    return (scale * (back[:, :pair] - u * back[:, pair:])).astype(bf16)


def attend_back_kernel(
    scale,
    place_ref,
    tok_t_ref,
    table_ref,
    mask_ref,
    feat_ref,
    swap_ref,
    turn_ref,
    u_ref,
    phi_ref,
    val_ref,
    inv_ref,
    mixed_ref,
    gm_ref,
    top_ref,
    dw_mine_ref,
    dw_other_ref,
    dqkv_ref,
    small_ref,
    probs_ref,
    gs_ref,
    diag_ref,
):
    length, pair = val_ref.shape
    size = pair // 2
    blocks = length // BLK

    @pl.when(pl.program_id(0) == 0)
    def _():
        small_ref[...] = top_ref[...]

    gm = gm_ref[...].astype(f32)
    scaled = gm * inv_ref[...]
    g_high, g_low = split_low(scaled)
    gt = scaled.T
    gt_high, gt_low = split_low(gt)
    d_high, d_low = split_low(scaled * mixed_ref[...])
    inner = dot(jnp.concatenate([d_high, d_low], axis=1), swap_ref[...])
    i_high, i_low = split_low(inner)
    phi = phi_ref[...]
    pq32, pk32 = phi[:, :pair], phi[:, pair:]
    pq = pq32.astype(bf16)
    pk = pk32.astype(bf16)
    pq_t = pq32.T.astype(bf16)
    value = val_ref[...]
    first = lane_half(value.shape)
    unit = jnp.full_like(value, 1.0 / size)
    zero = jnp.zeros_like(value)
    gq = None
    gk_heads = []
    gv_heads = []
    for h in range(2):
        cols = slice(h * size, (h + 1) * size)
        here = first if h == 0 else jnp.logical_not(first)
        lhs = jnp.concatenate(
            [jnp.where(here, g_high, i_high), jnp.where(here, g_low, i_low)], axis=1
        )
        rhs = jnp.where(here, value, unit)
        rhs = jnp.concatenate([rhs, rhs], axis=1)
        diag_ref[...] = jnp.zeros_like(diag_ref)
        for b in range(blocks):
            rows = slice(b * BLK, (b + 1) * BLK)
            start = (blocks - 1 - b) * BLK
            window = slice(start, start + length)
            mask = mask_ref[b : b + 1, :]
            scores = dot_nt(pq[rows, cols], pk[:, cols])
            coupling = table_ref[h, :, window] * mask
            probs_ref[rows, :] = (coupling * scores).astype(bf16)
            grad_scores = dot_nt(lhs[rows], rhs) * coupling
            gs_ref[rows, :] = grad_scores.astype(bf16)
            diag_ref[:, window] += grad_scores * scores
        part = dot(gs_ref[...], jnp.where(here, pk, zero))
        gq = part if gq is None else gq + part
        gk_heads.append(dot(pq_t[cols, :], gs_ref[...]))
        both = dot(jnp.concatenate([gt_high[cols], gt_low[cols]], axis=0), probs_ref[...])
        gv_heads.append(both[:size] + both[size:])
        folded = diag_ref[...]
        half = BLK // 2
        while half >= 1:
            folded = pltpu.roll(folded[:half], half, 1) + folded[half:]
            half //= 2
        split = [folded[:, n : n + BLK] for n in range(0, folded.shape[1], BLK)]
        f_high, rest = split_low(jnp.concatenate(split, axis=0))
        f_mid, f_low = split_low(jnp.concatenate(split, axis=0) - f_high.astype(f32))
        turned = dot(jnp.concatenate([f_high, f_mid, f_low], axis=1), turn_ref[...])
        turned = [turned[n : n + 1] for n in reversed(range(len(split)))]
        head = 2 * pl.program_id(0) + h
        rels = table_ref.shape[2]
        per_row = small_ref.shape[1] // rels
        column = pl.multiple_of(lax.rem(head, per_row) * rels, rels)
        row = small_ref.shape[0] - pl.num_programs(0) * 2 // per_row + head // per_row
        small_ref[pl.ds(row, 1), pl.ds(column, rels)] = jnp.concatenate(turned, axis=1)
    gk = jnp.concatenate(gk_heads, axis=0).T
    gv = jnp.concatenate(gv_heads, axis=0).T.astype(bf16)
    u = u_ref[...]
    dq = pair_backward(scale, gq, pq32, u[:, :pair], feat_ref)
    dk = pair_backward(scale, gk, pk32, u[:, pair:], feat_ref)
    dqkv_ref[:, :pair] = dq
    dqkv_ref[:, pair : 2 * pair] = dk
    dqkv_ref[:, 2 * pair :] = gv
    half = tok_t_ref.shape[0] // 2
    place = place_ref[0]
    mine = pl.ds(pl.multiple_of(place * half, half), half)
    other = pl.ds(pl.multiple_of((1 - place) * half, half), half)
    dw_mine_ref[...] = dot(tok_t_ref[mine, :], dqkv_ref[...]).astype(bf16)
    dw_other_ref[...] = dot(tok_t_ref[other, :], dqkv_ref[...]).astype(bf16)


def attend_back(
    place,
    tokens_t,
    tables,
    mask,
    feat_back,
    swap,
    turn,
    u,
    phi,
    value,
    inverse,
    mixed,
    grad_mixed,
    small_top,
    heads,
):
    width, length = tokens_t.shape
    pair = 2 * width // heads
    rels = tables.shape[2]
    scale = float((pair // 2) ** (-0.25))
    whole = lambda shape: pl.BlockSpec(shape, lambda h, p: (0,) * len(shape))
    column = lambda cols: pl.BlockSpec((length, cols), lambda h, p: (0, h))
    own_column = lambda rows: pl.BlockSpec((rows, 3 * pair), lambda h, p: (0, h))
    return pl.pallas_call(
        partial(attend_back_kernel, scale),
        grid_spec=pltpu.PrefetchScalarGridSpec(
            num_scalar_prefetch=1,
            grid=(heads // 2,),
            in_specs=[
                whole((width, length)),
                pl.BlockSpec((2, BLK, rels), lambda h, p: (h, 0, 0)),
                whole(mask.shape),
                whole(feat_back.shape),
                whole(swap.shape),
                whole(turn.shape),
                column(2 * pair),
                column(2 * pair),
                column(pair),
                column(pair),
                column(pair),
                column(pair),
                whole(small_top.shape),
            ],
            out_specs=[
                own_column(width // 2),
                own_column(width // 2),
                own_column(length),
                whole(small_top.shape),
            ],
            scratch_shapes=[
                pltpu.VMEM((length, length), bf16),
                pltpu.VMEM((length, length), bf16),
                pltpu.VMEM((BLK, rels), f32),
            ],
        ),
        out_shape=[
            jax.ShapeDtypeStruct((width // 2, 3 * width), bf16),
            jax.ShapeDtypeStruct((width // 2, 3 * width), bf16),
            jax.ShapeDtypeStruct((length, 3 * width), bf16),
            jax.ShapeDtypeStruct(small_top.shape, f32),
        ],
        cost_estimate=pl.CostEstimate(flops=0, bytes_accessed=0, transcendentals=0),
        name="attend_back",
    )(place, tokens_t, tables, mask, feat_back, swap, turn, u, phi, value, inverse, mixed, grad_mixed, small_top)


def block_diagonal(matrix):
    zero = jnp.zeros_like(matrix)
    return jnp.concatenate(
        [jnp.concatenate([matrix, zero], axis=1), jnp.concatenate([zero, matrix], axis=1)], axis=0
    )


def feature_tables(features):
    size = features.shape[0]
    ones = block_diagonal(jnp.ones((size, size), f32)).astype(bf16)
    high, low = split_low(block_diagonal(features))
    half = ones * -0.5
    forward = jnp.concatenate([high, low, high, half, half, half], axis=0)
    high, low = split_low(block_diagonal(features.T))
    none = jnp.zeros_like(ones)
    backward = jnp.concatenate(
        [jnp.concatenate([high, low, high], axis=0), jnp.concatenate([ones, none, ones], axis=0)],
        axis=1,
    )
    swap = jnp.concatenate([-ones[:, size:], -ones[:, :size]], axis=1)
    turn = jnp.eye(BLK, dtype=bf16)[::-1]
    return forward, backward, jnp.concatenate([swap, swap], axis=0), jnp.tile(turn, (3, 1))


def prepare_ffn_kernel(up_ref, down_ref, ffn_ref):
    rows = up_ref.shape[0]
    ffn_ref[:rows] = up_ref[...].astype(bf16)
    ffn_ref[rows:] = down_ref[...].astype(bf16)


def prepare_ffn(up, down):
    return pl.pallas_call(
        prepare_ffn_kernel,
        out_shape=jax.ShapeDtypeStruct((2 * up.shape[0], up.shape[1]), bf16),
        name="prepare_ffn",
    )(up, down)


def prepare_kernel(q_ref, k_ref, v_ref, o_ref, att_ref):
    width = o_ref.shape[1]
    lanes = att_ref.shape[1] // 4 // (width // 128)
    for j, ref in enumerate((q_ref, k_ref, v_ref)):
        for p in range(width // lanes):
            to = (3 * p + j) * lanes
            att_ref[:, to : to + lanes] = ref[:, p * lanes : (p + 1) * lanes].astype(bf16)
    att_ref[:, 3 * width :] = o_ref[...].astype(bf16)


def prepare(query, key, value, out):
    own, width = query.shape
    return pl.pallas_call(
        prepare_kernel,
        out_shape=jax.ShapeDtypeStruct((own, 4 * width), bf16),
        name="prepare",
    )(query, key, value, out)


root_half = 0.7071067811865476
inv_root_two_pi = 0.3989422804014327
eps = 1e-05


def norm_stats(residual):
    centered = residual - jnp.mean(residual, axis=1, keepdims=True)
    inverse = lax.rsqrt(jnp.mean(centered * centered, axis=1, keepdims=True) + eps)
    return centered * inverse, inverse


def norm_back(grad, xhat, inverse, gain):
    scaled = grad * gain
    mean_grad = jnp.mean(scaled, axis=1, keepdims=True)
    mean_dot = jnp.mean(scaled * xhat, axis=1, keepdims=True)
    return (scaled - mean_grad - xhat * mean_dot) * inverse


def column_sum(x):
    return jnp.sum(x, axis=0, keepdims=True)


def ffn_kernel(
    place_ref,
    low_ref,
    low_t_ref,
    xhat_ref,
    up_ref,
    down_ref,
    up_bias_ref,
    vec_ref,
    live_ref,
    cot_ref,
    out_ref,
    acc_ref,
    up_other_ref,
    up_mine_ref,
    down_other_ref,
    down_mine_ref,
    dup_bias_ref,
    dvec_ref,
    act_ref,
    slope_ref,
    gb_ref,
    gb_t_ref,
):
    phase = pl.program_id(0)
    part = pl.program_id(1)
    parts = pl.num_programs(1)
    length, width = low_ref.shape
    rows, hidden = up_ref.shape[1:]
    vec = vec_ref[...]
    down_bias, gain_one, shift_one, gain_two, shift_two = (vec[i : i + 1] for i in range(5))

    @pl.when((phase == 0) & (part == 0))
    def _():
        acc_ref[...] = jnp.zeros_like(acc_ref)

    @pl.when(phase == 0)
    def _():
        up = up_ref[...].reshape(width, hidden)
        down = down_ref[...].reshape(width, hidden)
        v = dot(low_ref[...], up) + up_bias_ref[...]
        half = 0.5 + 0.5 * lax.erf(v * root_half)
        act = (v * half).astype(bf16)
        act_ref[part] = act
        slope_ref[part] = half + v * (jnp.exp(-0.5 * v * v) * inv_root_two_pi)
        acc_ref[...] += dot_nt(act, down)

    @pl.when((phase == 0) & (part == parts - 1))
    def _():
        live = live_ref[...]
        normed = xhat_ref[...] * gain_one + shift_one
        xhat, inverse = norm_stats(normed + (acc_ref[...] + down_bias))
        out_ref[...] = ((xhat * gain_two + shift_two) * live).astype(bf16)
        grad = cot_ref[...].astype(f32) * live
        grad_two = norm_back(grad, xhat, inverse, gain_two)
        low = grad_two.astype(bf16)
        gb_ref[...] = low
        gb_t_ref[...] = grad_two.T.astype(bf16)
        dvec_ref[0:1, :] = column_sum(low.astype(f32))
        dvec_ref[3:4, :] = column_sum(grad * xhat)
        dvec_ref[4:5, :] = column_sum(grad)
        dvec_ref[1:3, :] = jnp.zeros((2, width), f32)
        dvec_ref[5:8, :] = jnp.zeros((3, width), f32)
        acc_ref[...] = grad_two

    def backward(d_up_ref, d_down_ref):
        up = up_ref[...].reshape(width, hidden)
        down = down_ref[...].reshape(width, hidden)
        grad_act = dot(gb_ref[...], down)
        grad_hidden = (grad_act * slope_ref[part]).astype(bf16)
        dup_bias_ref[...] = column_sum(grad_hidden.astype(f32))
        d_up = dot(low_t_ref[...], grad_hidden).astype(bf16)
        d_down = dot(gb_t_ref[...], act_ref[part]).astype(bf16)
        d_up_ref[...] = d_up.reshape(-1, rows, hidden)
        d_down_ref[...] = d_down.reshape(-1, rows, hidden)
        acc_ref[...] += dot_nt(grad_hidden, up)

    @pl.when((phase == 1) & (part < parts // 2))
    def _():
        backward(up_other_ref, down_other_ref)

    @pl.when((phase == 1) & (part >= parts // 2))
    def _():
        backward(up_mine_ref, down_mine_ref)


def ffn_last_kernel(
    place_ref,
    acc_ref,
    xhat_ref,
    inv_ref,
    mixed_t_ref,
    wo_ref,
    vec_ref,
    dvec_in_ref,
    grad_one_ref,
    gm_ref,
    wo_other_ref,
    wo_mine_ref,
    dvec_ref,
):
    width = acc_ref.shape[1]
    grad = acc_ref[...]
    xhat = xhat_ref[...]
    grad_one = norm_back(grad, xhat, inv_ref[...], vec_ref[1:2, :])
    grad_one_ref[...] = grad_one
    grad_att = grad_one.astype(bf16)
    gm_ref[...] = dot_nt(grad_att, wo_ref[...]).astype(bf16)
    half = width // 2
    place = place_ref[0]
    mine = pl.ds(pl.multiple_of(place * half, half), half)
    other = pl.ds(pl.multiple_of((1 - place) * half, half), half)
    wo_mine_ref[...] = dot(mixed_t_ref[mine, :], grad_att).astype(bf16)
    wo_other_ref[...] = dot(mixed_t_ref[other, :], grad_att).astype(bf16)
    dvec_ref[...] = dvec_in_ref[...]
    dvec_ref[1:2, :] = column_sum(grad * xhat)
    dvec_ref[2:3, :] = column_sum(grad)


def first_norm_kernel(tok_ref, mixed_ref, wo_ref, vec_ref, low_ref, low_t_ref, xhat_ref, inv_ref):
    residual = tok_ref[...].astype(f32) + dot(mixed_ref[...], wo_ref[...])
    xhat, inverse = norm_stats(residual)
    normed = xhat * vec_ref[1:2, :] + vec_ref[2:3, :]
    xhat_ref[...] = xhat
    inv_ref[...] = inverse
    low_ref[...] = normed.astype(bf16)
    low_t_ref[...] = normed.T.astype(bf16)


def first_norm(tokens, mixed, attention_weights, vectors):
    length, width = tokens.shape
    wo_column = attention_weights.shape[1] // width - 1
    whole = lambda shape: pl.BlockSpec(shape, lambda i: (0,) * len(shape))
    return pl.pallas_call(
        first_norm_kernel,
        grid=(1,),
        in_specs=[
            whole((length, width)),
            whole((length, width)),
            pl.BlockSpec((width, width), lambda i: (0, wo_column)),
            whole(vectors.shape),
        ],
        out_specs=[
            whole((length, width)),
            whole((width, length)),
            whole((length, width)),
            whole((length, 1)),
        ],
        out_shape=[
            jax.ShapeDtypeStruct((length, width), bf16),
            jax.ShapeDtypeStruct((width, length), bf16),
            jax.ShapeDtypeStruct((length, width), f32),
            jax.ShapeDtypeStruct((length, 1), f32),
        ],
        cost_estimate=pl.CostEstimate(flops=0, bytes_accessed=0, transcendentals=0),
        name="first_norm",
    )(tokens, mixed, attention_weights, vectors)


def feed_forward(
    place,
    low,
    low_t,
    xhat,
    inverse,
    mixed_t,
    attention_weights,
    weights,
    up_bias,
    vectors,
    live,
    cotangent,
):
    length, width = low.shape
    parts, shards, _, rows, hidden = weights.shape
    xs = parts // 2
    whole = lambda shape: pl.BlockSpec(shape, lambda p, w, c: (0,) * len(shape))
    once = lambda shape: pl.BlockSpec(
        shape, lambda p, w, c: (0,) * len(shape), pipeline_mode=pl.Buffered(1)
    )
    wo_column = attention_weights.shape[1] // width - 1
    wide = (length, width)
    part_of = lambda w, c: 2 * lax.rem(w, xs) + jnp.where(w < xs, 1 - c[0], c[0])
    weight_spec = lambda which: pl.BlockSpec(
        (None, shards, None, rows, hidden), lambda p, w, c: (part_of(w, c), 0, which, 0, 0)
    )
    other_spec = pl.BlockSpec(
        (None, shards, rows, hidden), lambda p, w, c: (p * jnp.minimum(w, xs - 1), 0, 0, 0)
    )
    mine_spec = pl.BlockSpec(
        (None, shards, rows, hidden), lambda p, w, c: (p * jnp.maximum(w - xs, 0), 0, 0, 0)
    )
    grads = jax.ShapeDtypeStruct((xs, shards, rows, hidden), bf16)
    out, acc, up_other, up_mine, down_other, down_mine, dup_bias, dvec = pl.pallas_call(
        ffn_kernel,
        grid_spec=pltpu.PrefetchScalarGridSpec(
            num_scalar_prefetch=1,
            grid=(2, parts),
            in_specs=[
                once(wide),
                once((width, length)),
                once(wide),
                weight_spec(0),
                weight_spec(1),
                pl.BlockSpec((None, 1, hidden), lambda p, w, c: (part_of(w, c), 0, 0)),
                whole(vectors.shape),
                once((length, 1)),
                once(wide),
            ],
            out_specs=[
                whole(wide),
                whole(wide),
                other_spec,
                mine_spec,
                other_spec,
                mine_spec,
                pl.BlockSpec(
                    (None, 1, hidden), lambda p, w, c: (part_of(w * p, c), 0, 0)
                ),
                whole((8, width)),
            ],
            scratch_shapes=[
                pltpu.VMEM((parts, length, hidden), bf16),
                pltpu.VMEM((parts, length, hidden), f32),
                pltpu.VMEM(wide, bf16),
                pltpu.VMEM((width, length), bf16),
            ],
        ),
        out_shape=[
            jax.ShapeDtypeStruct(wide, bf16),
            jax.ShapeDtypeStruct(wide, f32),
            grads,
            grads,
            grads,
            grads,
            jax.ShapeDtypeStruct((parts, 1, hidden), f32),
            jax.ShapeDtypeStruct((8, width), f32),
        ],
        compiler_params=pltpu.CompilerParams(vmem_limit_bytes=58 * 1024 * 1024),
        cost_estimate=pl.CostEstimate(flops=0, bytes_accessed=0, transcendentals=0),
        name="feed_forward",
    )(
        place,
        low,
        low_t,
        xhat,
        weights,
        weights,
        up_bias,
        vectors,
        live,
        cotangent,
    )
    grad_one, gm, wo_other, wo_mine, dvec = pl.pallas_call(
        ffn_last_kernel,
        grid_spec=pltpu.PrefetchScalarGridSpec(
            num_scalar_prefetch=1,
            grid=(1,),
            in_specs=[
                pl.BlockSpec(wide, lambda i, c: (0, 0)),
                pl.BlockSpec(wide, lambda i, c: (0, 0)),
                pl.BlockSpec((length, 1), lambda i, c: (0, 0)),
                pl.BlockSpec((width, length), lambda i, c: (0, 0)),
                pl.BlockSpec((width, width), lambda i, c: (0, wo_column)),
                pl.BlockSpec(vectors.shape, lambda i, c: (0, 0)),
                pl.BlockSpec((8, width), lambda i, c: (0, 0)),
            ],
            out_specs=[
                pl.BlockSpec(wide, lambda i, c: (0, 0)),
                pl.BlockSpec(wide, lambda i, c: (0, 0)),
                pl.BlockSpec((width // 2, width), lambda i, c: (0, 0)),
                pl.BlockSpec((width // 2, width), lambda i, c: (0, 0)),
                pl.BlockSpec((8, width), lambda i, c: (0, 0)),
            ],
        ),
        out_shape=[
            jax.ShapeDtypeStruct(wide, f32),
            jax.ShapeDtypeStruct(wide, bf16),
            jax.ShapeDtypeStruct((width // 2, width), bf16),
            jax.ShapeDtypeStruct((width // 2, width), bf16),
            jax.ShapeDtypeStruct((8, width), f32),
        ],
        cost_estimate=pl.CostEstimate(flops=0, bytes_accessed=0, transcendentals=0),
        name="ffn_last",
    )(place, acc, xhat, inverse, mixed_t, attention_weights, vectors, dvec)
    return (
        out,
        grad_one,
        gm,
        up_other,
        up_mine,
        down_other,
        down_mine,
        wo_other,
        wo_mine,
        dup_bias,
        dvec,
    )


class Grid:
    def __init__(self, batch, wide):
        self.devices = batch * wide
        self.sizes = dict(z=4, y=batch // 4, x=wide // 2, c=2)
        self.strides = dict(z=batch // 4 * wide, y=wide, x=2, c=1)
        flat = lax.axis_index("batch") * wide + lax.axis_index("wide")
        self.place = {d: lax.rem(flat // self.strides[d], n) for d, n in self.sizes.items()}
        self.vector = jnp.stack([self.place[d] for d in "zyxc"])

    def shift(self, value, **offsets):
        pairs = []
        for i in range(self.devices):
            target = i
            for d, o in offsets.items():
                s, n = self.strides[d], self.sizes[d]
                target += ((i // s + o) % n - i // s % n) * s
            pairs.append((i, target))
        return lax.ppermute(value, ("batch", "wide"), pairs)

    def at(self, d, offset):
        return lax.rem(self.place[d] + (offset + self.sizes[d]), self.sizes[d])

    def block_at(self, d, offset):
        k, n = "zyxc".index(d), self.sizes[d]
        return lambda vector: lax.rem(vector[k] + offset, n)

    def offsets(self, dims):
        ranges = [range(self.sizes[d]) for d in dims]
        return [dict(zip(dims, o)) for o in itertools.product(*ranges)]

    def swap(self, value, dims):
        groups = {}
        for i in range(self.devices):
            key = tuple(i // self.strides[d] % n for d, n in self.sizes.items() if d not in dims)
            groups.setdefault(key, []).append(i)
        return lax.all_to_all(
            value, ("batch", "wide"), 0, 0, axis_index_groups=list(groups.values())
        )

    def gather(self, value, names, dims):
        parts = [(o, self.shift(value, **o) if any(o.values()) else value) for o in self.offsets(dims)]
        if len(parts) == 2:
            (d,) = dims
            own, other = value, parts[1][1]
            first = self.place[d] == 0
            return jnp.concatenate(
                [jnp.where(first, own, other), jnp.where(first, other, own)], axis=names.index(d)
            )
        shape = [self.sizes[d] if d in dims else n for d, n in zip(names, value.shape)]
        out = jnp.zeros(shape + list(value.shape[len(names) :]), value.dtype)
        for o, part in parts:
            start = [self.at(d, -o[d]) if d in dims else 0 for d in names]
            out = lax.dynamic_update_slice(out, part, start + [0] * (value.ndim - len(names)))
        return out

    def send(self, sends, dims):
        return [self.shift(value, **o) for o, value in zip(self.offsets(dims)[1:], sends)]


class Combine:
    def __init__(self, grid, steps):
        self.grid, self.steps = grid, steps
        self.inputs, self.in_specs, self.shapes, self.out_specs, self.terms = [], [], [], [], []

    def spec(self, block, where):
        picks = []
        for w in where:
            if w is None:
                picks.append(lambda i, v: 0)
            elif w == "step":
                picks.append(lambda i, v: i)
            else:
                at = self.grid.block_at(*w)
                picks.append(lambda i, v, at=at: at(v))
        return pl.BlockSpec(block, lambda i, v: tuple(p(i, v) for p in picks))

    def read(self, arrays, where):
        numbers = []
        for a in arrays:
            block = tuple(n if w is None else None for n, w in zip(a.shape, where))
            numbers.append(len(self.inputs))
            self.inputs.append(a)
            self.in_specs.append(self.spec(block, where))
        return numbers

    def add(self, addends, picks):
        numbers = []
        for names, array in addends:
            where = tuple(picks.get(d) for d in names)
            where = tuple((d, w) if isinstance(w, int) else w for d, w in zip(names, where))
            numbers += self.read([array], where + (None,) * (array.ndim - len(names)))
        return numbers

    def write(self, shape, dtype, terms, stepped=None):
        where = tuple("step" if n == stepped else None for n in range(len(shape)))
        block = tuple(n if w is None else None for n, w in zip(shape, where))
        self.shapes.append(jax.ShapeDtypeStruct(shape, dtype))
        self.out_specs.append(self.spec(block, where))
        self.terms.append(terms)

    def run(self, name):
        count = len(self.inputs)

        def kernel(vector_ref, *refs):
            for out_ref, terms in zip(refs[count:], self.terms):
                for target, *rest in terms:
                    total = None
                    for source, numbers in [rest] if len(rest) == 2 else rest[0]:
                        for n in numbers:
                            value = refs[n][source].astype(f32)
                            total = value if total is None else total + value
                    total = total.astype(out_ref.dtype)
                    if len(out_ref.shape) == 1:
                        total = total.reshape(out_ref.shape)
                    out_ref[target] = total

        return pl.pallas_call(
            kernel,
            grid_spec=pltpu.PrefetchScalarGridSpec(
                num_scalar_prefetch=1,
                grid=(self.steps,),
                in_specs=self.in_specs,
                out_specs=self.out_specs,
            ),
            out_shape=self.shapes,
            compiler_params=pltpu.CompilerParams(vmem_limit_bytes=63 * 1024 * 1024 + 900 * 1024),
            cost_estimate=pl.CostEstimate(flops=0, bytes_accessed=0, transcendentals=0),
            name=name,
        )(self.grid.vector, *self.inputs)


everything = (Ellipsis,)


def hold(value, *others):
    return lax.optimization_barrier((value, others))


def per_device(
    batch,
    wide,
    tokens,
    block_row,
    block_live,
    query_weight,
    key_weight,
    value_weight,
    out_weight,
    position_bias,
    features,
    up_weight,
    up_bias,
    down_weight,
    down_bias,
    gain_one,
    shift_one,
    gain_two,
    shift_two,
    cotangent,
):
    grid = Grid(batch, wide)
    zs, ys, xs, cs = (grid.sizes[d] for d in "zyxc")
    length, width = tokens.shape
    heads, rels = position_bias.shape
    pairs = heads // 2
    own = query_weight.shape[0]
    lanes = width // pairs
    ffn_shard = prepare_ffn(up_weight, down_weight)
    query_weight, (ffn_shard,) = hold(query_weight, ffn_shard)
    shard = prepare(query_weight, key_weight, value_weight, out_weight)
    up_rows, hidden = up_weight.shape
    half = 2 * width
    gathered = grid.gather(shard.reshape(1, 1, 1, 1, own, 4 * width), "zyxc", "z")
    first = grid.gather(gathered[..., :half], "zyxc", "x")
    second = grid.gather(gathered[..., half:], "zyxc", "y")
    inputs = (position_bias, features, block_row, block_live, tokens, down_bias)
    first, (second, *inputs) = hold(first, second, *inputs)
    position_bias, features, block_row, block_live, tokens, down_bias = inputs
    tables = toeplitz_tables(position_bias[:, ::-1])
    feat_forward, feat_back, swap, turn = feature_tables(features)
    offsets = jnp.arange(BLK, dtype=jnp.int32)
    live = (offsets[None, :] < block_live[:, None]).astype(f32).reshape(1, length)
    rows = jnp.broadcast_to(block_row[:, None], (block_row.shape[0], BLK)).reshape(1, length)
    mask = jnp.where(block_row[:, None] == rows, live, 0.0)
    by_core = lambda m: m.reshape(-1, cs, own, length).swapaxes(0, 1).reshape(width, length)
    tokens_t = by_core(tokens.T)
    vectors = jnp.stack([down_bias, gain_one, shift_one, gain_two, shift_two] + [down_bias] * 3)
    live_column = live.reshape(length, 1)

    first = grid.gather(first, "zyxc", "y")
    second = grid.gather(second, "zyxc", "x")
    early = (tables, feat_forward, feat_back, swap, turn, mask, tokens_t, vectors, live_column)
    first, (second, *early) = hold(first, second, *early)
    tables, feat_forward, feat_back, swap, turn, mask, tokens_t, vectors, live_column = early
    first = grid.gather(first, "zyxc", "c").reshape(width, half)
    second = grid.gather(second, "zyxc", "c").reshape(width, half)
    attention_weights = jnp.concatenate([first, second], axis=1)
    ffn_weights = lax.all_gather(ffn_shard, ("wide", "batch"), axis=0, tiled=False)
    ffn_weights = ffn_weights.reshape(wide, batch, 2, up_rows, hidden)
    mixed, mixed32, u, phi, value, inverse = attend(
        tokens, attention_weights, tables, mask, feat_forward, heads
    )
    place = grid.place["c"].reshape(1)
    (
        out_tokens,
        grad_one,
        grad_mixed,
        up_other_grad,
        up_mine_grad,
        down_other,
        down_mine,
        out_other,
        out_mine,
        dup_bias,
        dvec,
    ) = feed_forward(
        place,
        *first_norm(tokens, mixed, attention_weights, vectors),
        by_core(mixed.T),
        attention_weights,
        ffn_weights,
        up_bias.reshape(wide, 1, hidden),
        vectors,
        live_column,
        cotangent,
    )
    ffn_view = lambda m: ("xzy", m.reshape(xs, zs, ys, up_rows, hidden))
    att_view = lambda m: ("zyx", m.reshape(zs, ys, xs, own, -1))
    down_recv = grid.shift(down_other, c=1)
    up = [ffn_view(up_mine_grad), ffn_view(grid.shift(up_other_grad, c=1))]
    out = [att_view(out_mine), att_view(grid.shift(out_other, c=1))]

    columns = 4 * width
    bias_rows = heads * rels // columns
    extra = -(-(3 + bias_rows) // 8) * 8
    first_row = extra - bias_rows
    small_top = jnp.concatenate(
        [dup_bias.reshape(1, columns), dvec.reshape(2, columns), jnp.zeros((extra - 3, columns), f32)]
    )
    down_mine, (small_top,) = hold(down_mine, small_top)
    down = [ffn_view(down_mine), ffn_view(down_recv)]

    step = Combine(grid, zs)
    for y in range(1, ys):
        terms = [(everything, everything, step.add(down, dict(z="step", y=y)))]
        step.write((xs, zs, up_rows, hidden), bf16, terms, stepped=1)
    for x in range(1, xs):
        terms = [(everything, everything, step.add(up, dict(z="step", x=x)))]
        step.write((zs, ys, up_rows, hidden), bf16, terms, stepped=0)
    sends = step.run("ffn_sum_core")
    down_sends, up_sends = sends[: ys - 1], sends[ys - 1 :]
    grad_mixed, (down_sends, up_sends) = hold(grad_mixed, down_sends, up_sends)
    down_new = grid.send(down_sends, "y")
    up_new = grid.send(up_sends, "x")

    dw_mine, dw_other, dqkv, small = attend_back(
        place,
        tokens_t,
        tables,
        mask,
        feat_back,
        swap,
        turn,
        u,
        phi,
        value,
        inverse,
        mixed32,
        grad_mixed,
        small_top,
        heads,
    )
    dw_mine, (dw_other, dqkv, small, down_new, up_new) = hold(
        dw_mine, dw_other, dqkv, small, down_new, up_new
    )
    down += [("xz", v) for v in down_new]
    up += [("zy", v) for v in up_new]
    att = [att_view(dw_mine), att_view(grid.shift(dw_other, c=1))]

    step = Combine(grid, 1)
    block = (zs, up_rows, hidden)
    for x in range(1, xs):
        terms = [(everything, everything, step.add(down, dict(y=0, x=x)))]
        step.write(block, bf16, terms)
    for y in range(1, ys):
        terms = [(everything, everything, step.add(up, dict(x=0, y=y)))]
        step.write(block, bf16, terms)
    sends = step.run("ffn_sum_plane")
    down_new = grid.send(sends[: xs - 1], "x")
    up_new = grid.send(sends[xs - 1 :], "y")
    small = small + grid.shift(small, c=1)
    small_new = grid.send([small.astype(bf16)] * (zs - 1), "z")
    dw_mine, sends = hold(dw_mine, *sends)
    att[0] = att_view(dw_mine)
    step = Combine(grid, 1)
    for o in grid.offsets("yx")[1:]:
        terms = [
            ((..., slice(0, 3 * width)), everything, step.add(att, o)),
            ((..., slice(3 * width, None)), everything, step.add(out, o)),
        ]
        step.write((zs, own, columns), bf16, terms)
    att_sends = step.run("att_sum_core")
    small, (*small_new, att_sends) = hold(small, *small_new, att_sends)
    small = (small + sum(v.astype(f32) for v in small_new)).astype(bf16)
    small = jnp.broadcast_to(small[None], (ys * xs,) + small.shape)
    down_new, (up_new, att_sends) = hold(down_new, up_new, att_sends)
    down += [("z", v) for v in down_new]
    up += [("z", v) for v in up_new]
    att_new = grid.send(att_sends, "yx")

    here = dict(z=0, y=0, x=0)
    step = Combine(grid, 1)
    for z in range(1, zs):
        terms = [
            ((j,), everything, step.add(addends, dict(z=z, y=0, x=0)))
            for j, addends in enumerate((up, down))
        ]
        step.write((2, up_rows, hidden), bf16, terms)
    sends = step.run("ffn_sum_second")
    dqkv, (small, *sends) = hold(dqkv, small, *sends)
    small = grid.swap(small, "yx")
    ffn_new = grid.send(sends, "z")
    grad_tokens = grad_one + dot_nt(dqkv, attention_weights[:, : 3 * width])
    att_new, (grad_tokens, *sends) = hold(att_new, grad_tokens, *sends)
    att_new = [("z", v) for v in att_new]

    step = Combine(grid, 1)
    for z in range(1, zs):
        picks = dict(z=z, y=0, x=0)
        top = slice(0, own)
        new = step.add(att_new, picks)
        head, tail = slice(0, 3 * width), slice(3 * width, None)
        terms = [
            ((top, head), everything, step.add(att, picks)),
            ((top, tail), everything, step.add(out, picks)),
        ]
        terms = [
            (target, [(everything, numbers), ((slice(None), target[1]), new)])
            for target, _, numbers in terms
        ]
        step.write((own, columns), bf16, terms)
    att_sends = step.run("att_sum_plane")
    last = grid.send(att_sends, "z")

    step = Combine(grid, 1)
    new = step.read(ffn_new, (None, None, None))
    for j, addends in enumerate((up, down)):
        terms = [(everything, [(everything, step.add(addends, here)), ((j,), new)])]
        step.write((up_rows, hidden), f32, terms)
    up_own, down_own = step.run("ffn_sum_last")

    step = Combine(grid, 1)
    new = step.add(att_new, here)
    head = (slice(None), slice(0, 3 * width))
    tail = (slice(None), slice(3 * width, None))
    top = slice(0, own)
    terms = [
        ((top, head[1]), [(everything, step.add(att, here)), (head, new)]),
        ((top, tail[1]), [(everything, step.add(out, here)), (tail, new)]),
    ]
    step.write((own, columns), f32, terms)
    small_in = step.read([small], (None, None, None))

    def small_term(r, cols):
        return [((k, slice(r, r + 1), cols), small_in) for k in range(ys * xs)]

    step.write((columns,), f32, [(everything, small_term(0, slice(None)))])
    for j in range(5):
        at = j % 4 * width
        step.write((width,), f32, [(everything, small_term(1 + j // 4, slice(at, at + width)))])
    per_row = columns // rels
    terms = []
    for h in range(heads):
        at = h % per_row * rels
        term = small_term(first_row + h // per_row, slice(at, at + rels))
        terms.append(((slice(h, h + 1),), term))
    step.write((heads, rels), f32, terms)
    before, dup_bias, *dvec, dbias = step.run("att_sum_own")

    step = Combine(grid, 1)
    last = step.read([before, *last], (None, None))
    for j in range(3):
        terms = []
        for p in range(pairs):
            cols = slice((3 * p + j) * lanes, (3 * p + j + 1) * lanes)
            terms.append(((slice(None), slice(p * lanes, (p + 1) * lanes)), (top, cols), last))
        step.write((own, width), f32, terms)
    step.write((own, width), f32, [(everything, (top, tail[1]), last)])

    dq, dk, dv, out_own = step.run("last_sum")
    return (
        out_tokens,
        grad_tokens,
        dq,
        dk,
        dv,
        out_own,
        dbias,
        up_own,
        dup_bias,
        down_own,
        *dvec,
    )


def solution(mesh):
    both = P(("batch", "wide"), None)
    placed = (
        both,
        P(("batch", "wide")),
        P(("batch", "wide")),
        both,
        both,
        both,
        both,
        P(),
        P(),
        P("batch", "wide"),
        P(),
        P("batch", "wide"),
        P(),
        P(),
        P(),
        P(),
        P(),
        both,
    )
    outs = (
        both,
        both,
        both,
        both,
        both,
        both,
        P(),
        P("batch", "wide"),
        P(),
        P("batch", "wide"),
        P(),
        P(),
        P(),
        P(),
        P(),
    )
    return jax.shard_map(
        partial(per_device, mesh.shape["batch"], mesh.shape["wide"]),
        mesh=mesh,
        in_specs=placed,
        out_specs=outs,
        check_vma=False,
    )
```

```python
import itertools
from functools import partial

import jax
import jax.numpy as jnp
from jax import lax
from jax.experimental import pallas as pl
from jax.experimental.pallas import tpu as pltpu
from jax.sharding import PartitionSpec as P

BLK = 128
f32 = jnp.float32
bf16 = jnp.bfloat16
nt_dims = (((1,), (1,)), ((), ()))


def dot(a, b):
    return jnp.dot(a, b, preferred_element_type=f32)


def dot_nt(a, b):
    return lax.dot_general(a, b, nt_dims, preferred_element_type=f32)


def split_low(x):
    high = x.astype(bf16)
    return high, (x - high.astype(f32)).astype(bf16)


def toeplitz_kernel(bias_ref, out_ref):
    heads = bias_ref.shape[0]
    rels = bias_ref.shape[1]
    for h in range(heads):
        row = jnp.broadcast_to(jnp.exp(bias_ref[h : h + 1, :]), (BLK, rels))
        out_ref[h] = pltpu.roll(row, rels - BLK + 1, 1, stride=1, stride_axis=0)


def toeplitz_tables(flipped_bias):
    heads, rels = flipped_bias.shape
    step = 2
    return pl.pallas_call(
        toeplitz_kernel,
        grid=(heads // step,),
        in_specs=[pl.BlockSpec((None, step, rels), lambda h: (h, 0, 0))],
        out_specs=pl.BlockSpec((step, BLK, rels), lambda h: (h, 0, 0)),
        out_shape=jax.ShapeDtypeStruct((heads, BLK, rels), f32),
        cost_estimate=pl.CostEstimate(
            flops=5_000_000_000, bytes_accessed=8_000_000, transcendentals=0
        ),
        name="toeplitz",
    )(flipped_bias.reshape(heads // step, step, rels))


def lane_half(shape):
    return lax.broadcasted_iota(jnp.int32, shape, 1) < shape[1] // 2


def pair_features(u, feat_ref):
    high, low = split_low(u)
    square = u * u
    s_high, rest = split_low(square)
    rest = square - s_high.astype(f32)
    s_mid, s_low = split_low(rest)
    lhs = jnp.concatenate([high, high, low, s_high, s_mid, s_low], axis=1)
    return jnp.exp(dot(lhs, feat_ref[...]))


def attend_kernel(
    scale,
    tok_ref,
    w_ref,
    table_ref,
    mask_ref,
    feat_ref,
    mixed_ref,
    mixed32_ref,
    u_ref,
    phi_ref,
    val_ref,
    inv_ref,
    weights_ref,
):
    length = tok_ref.shape[0]
    pair = mixed_ref.shape[1]
    size = pair // 2
    blocks = length // BLK
    qkv = dot(tok_ref[...], w_ref[...])
    uq = qkv[:, :pair] * scale
    uk = qkv[:, pair : 2 * pair] * scale
    value = qkv[:, 2 * pair :].astype(bf16)
    pq = pair_features(uq, feat_ref)
    pk = pair_features(uk, feat_ref)
    u_ref[:, :pair] = uq
    u_ref[:, pair:] = uk
    phi_ref[:, :pair] = pq
    phi_ref[:, pair:] = pk
    val_ref[...] = value
    pq = pq.astype(bf16)
    pk = pk.astype(bf16)
    first = lane_half(value.shape)
    zero = jnp.zeros_like(value)
    one = jnp.ones_like(value)
    out = None
    for h in range(2):
        cols = slice(h * size, (h + 1) * size)
        here = first if h == 0 else jnp.logical_not(first)
        for b in range(blocks):
            rows = slice(b * BLK, (b + 1) * BLK)
            start = (blocks - 1 - b) * BLK
            scores = dot_nt(pq[rows, cols], pk[:, cols])
            coupling = table_ref[h, :, start : start + length] * mask_ref[b : b + 1, :]
            weights_ref[rows, :] = (coupling * scores).astype(bf16)
        rhs = jnp.concatenate([jnp.where(here, value, zero), jnp.where(here, one, zero)], axis=1)
        part = dot(weights_ref[...], rhs)
        out = part if out is None else out + part
    inverse = 1.0 / out[:, pair:]
    mixed = out[:, :pair] * inverse
    inv_ref[...] = inverse
    mixed32_ref[...] = mixed
    mixed_ref[...] = mixed.astype(bf16)


def attend(tokens, weights, tables, mask, feat_split, heads):
    length, width = tokens.shape
    pair = 2 * width // heads
    pairs = heads // 2
    rels = tables.shape[2]
    scale = float((pair // 2) ** (-0.25))
    whole = lambda shape: pl.BlockSpec(shape, lambda h: (0,) * len(shape))
    column = lambda cols: pl.BlockSpec((length, cols), lambda h: (0, h))
    return pl.pallas_call(
        partial(attend_kernel, scale),
        grid=(pairs,),
        in_specs=[
            whole((length, width)),
            pl.BlockSpec((width, 3 * pair), lambda h: (0, h)),
            pl.BlockSpec((2, BLK, rels), lambda h: (h, 0, 0)),
            whole(mask.shape),
            whole(feat_split.shape),
        ],
        out_specs=[
            column(pair),
            column(pair),
            column(2 * pair),
            column(2 * pair),
            column(pair),
            column(pair),
        ],
        out_shape=[
            jax.ShapeDtypeStruct((length, width), bf16),
            jax.ShapeDtypeStruct((length, width), f32),
            jax.ShapeDtypeStruct((length, 2 * width), f32),
            jax.ShapeDtypeStruct((length, 2 * width), f32),
            jax.ShapeDtypeStruct((length, width), bf16),
            jax.ShapeDtypeStruct((length, width), f32),
        ],
        scratch_shapes=[pltpu.VMEM((length, length), bf16)],
        cost_estimate=pl.CostEstimate(flops=0, bytes_accessed=0, transcendentals=0),
        name="attend",
    )(tokens, weights, tables, mask, feat_split)


def pair_backward(scale, grad_phi, phi, u, feat_ref):
    pair = u.shape[1]
    high, low = split_low(grad_phi * phi)
    back = dot(jnp.concatenate([high, high, low], axis=1), feat_ref[...])
    return (scale * (back[:, :pair] - u * back[:, pair:])).astype(bf16)


def attend_back_kernel(
    scale,
    place_ref,
    tok_t_ref,
    table_ref,
    mask_ref,
    feat_ref,
    swap_ref,
    turn_ref,
    u_ref,
    phi_ref,
    val_ref,
    inv_ref,
    mixed_ref,
    gm_ref,
    top_ref,
    dw_mine_ref,
    dw_other_ref,
    dqkv_ref,
    small_ref,
    probs_ref,
    gs_ref,
    diag_ref,
):
    length, pair = val_ref.shape
    size = pair // 2
    blocks = length // BLK

    @pl.when(pl.program_id(0) == 0)
    def _():
        small_ref[...] = top_ref[...]

    gm = gm_ref[...].astype(f32)
    scaled = gm * inv_ref[...]
    g_high, g_low = split_low(scaled)
    gt = scaled.T
    gt_high, gt_low = split_low(gt)
    d_high, d_low = split_low(scaled * mixed_ref[...])
    inner = dot(jnp.concatenate([d_high, d_low], axis=1), swap_ref[...])
    i_high, i_low = split_low(inner)
    phi = phi_ref[...]
    pq32, pk32 = phi[:, :pair], phi[:, pair:]
    pq = pq32.astype(bf16)
    pk = pk32.astype(bf16)
    pq_t = pq32.T.astype(bf16)
    value = val_ref[...]
    first = lane_half(value.shape)
    unit = jnp.full_like(value, 1.0 / size)
    zero = jnp.zeros_like(value)
    gq = None
    gk_heads = []
    gv_heads = []
    for h in range(2):
        cols = slice(h * size, (h + 1) * size)
        here = first if h == 0 else jnp.logical_not(first)
        lhs = jnp.concatenate(
            [jnp.where(here, g_high, i_high), jnp.where(here, g_low, i_low)], axis=1
        )
        rhs = jnp.where(here, value, unit)
        rhs = jnp.concatenate([rhs, rhs], axis=1)
        diag_ref[...] = jnp.zeros_like(diag_ref)
        for b in range(blocks):
            rows = slice(b * BLK, (b + 1) * BLK)
            start = (blocks - 1 - b) * BLK
            window = slice(start, start + length)
            mask = mask_ref[b : b + 1, :]
            scores = dot_nt(pq[rows, cols], pk[:, cols])
            coupling = table_ref[h, :, window] * mask
            probs_ref[rows, :] = (coupling * scores).astype(bf16)
            grad_scores = dot_nt(lhs[rows], rhs) * coupling
            gs_ref[rows, :] = grad_scores.astype(bf16)
            diag_ref[:, window] += grad_scores * scores
        part = dot(gs_ref[...], jnp.where(here, pk, zero))
        gq = part if gq is None else gq + part
        gk_heads.append(dot(pq_t[cols, :], gs_ref[...]))
        both = dot(jnp.concatenate([gt_high[cols], gt_low[cols]], axis=0), probs_ref[...])
        gv_heads.append(both[:size] + both[size:])
        folded = diag_ref[...]
        half = BLK // 2
        while half >= 1:
            folded = pltpu.roll(folded[:half], half, 1) + folded[half:]
            half //= 2
        split = [folded[:, n : n + BLK] for n in range(0, folded.shape[1], BLK)]
        f_high, rest = split_low(jnp.concatenate(split, axis=0))
        f_mid, f_low = split_low(jnp.concatenate(split, axis=0) - f_high.astype(f32))
        turned = dot(jnp.concatenate([f_high, f_mid, f_low], axis=1), turn_ref[...])
        turned = [turned[n : n + 1] for n in reversed(range(len(split)))]
        head = 2 * pl.program_id(0) + h
        rels = table_ref.shape[2]
        per_row = small_ref.shape[1] // rels
        column = pl.multiple_of(lax.rem(head, per_row) * rels, rels)
        row = small_ref.shape[0] - pl.num_programs(0) * 2 // per_row + head // per_row
        small_ref[pl.ds(row, 1), pl.ds(column, rels)] = jnp.concatenate(turned, axis=1)
    gk = jnp.concatenate(gk_heads, axis=0).T
    gv = jnp.concatenate(gv_heads, axis=0).T.astype(bf16)
    u = u_ref[...]
    dq = pair_backward(scale, gq, pq32, u[:, :pair], feat_ref)
    dk = pair_backward(scale, gk, pk32, u[:, pair:], feat_ref)
    dqkv_ref[:, :pair] = dq
    dqkv_ref[:, pair : 2 * pair] = dk
    dqkv_ref[:, 2 * pair :] = gv
    half = tok_t_ref.shape[0] // 2
    place = place_ref[0]
    mine = pl.ds(pl.multiple_of(place * half, half), half)
    other = pl.ds(pl.multiple_of((1 - place) * half, half), half)
    dw_mine_ref[...] = dot(tok_t_ref[mine, :], dqkv_ref[...]).astype(bf16)
    dw_other_ref[...] = dot(tok_t_ref[other, :], dqkv_ref[...]).astype(bf16)


def attend_back(
    place,
    tokens_t,
    tables,
    mask,
    feat_back,
    swap,
    turn,
    u,
    phi,
    value,
    inverse,
    mixed,
    grad_mixed,
    small_top,
    heads,
):
    width, length = tokens_t.shape
    pair = 2 * width // heads
    rels = tables.shape[2]
    scale = float((pair // 2) ** (-0.25))
    whole = lambda shape: pl.BlockSpec(shape, lambda h, p: (0,) * len(shape))
    column = lambda cols: pl.BlockSpec((length, cols), lambda h, p: (0, h))
    own_column = lambda rows: pl.BlockSpec((rows, 3 * pair), lambda h, p: (0, h))
    return pl.pallas_call(
        partial(attend_back_kernel, scale),
        grid_spec=pltpu.PrefetchScalarGridSpec(
            num_scalar_prefetch=1,
            grid=(heads // 2,),
            in_specs=[
                whole((width, length)),
                pl.BlockSpec((2, BLK, rels), lambda h, p: (h, 0, 0)),
                whole(mask.shape),
                whole(feat_back.shape),
                whole(swap.shape),
                whole(turn.shape),
                column(2 * pair),
                column(2 * pair),
                column(pair),
                column(pair),
                column(pair),
                column(pair),
                whole(small_top.shape),
            ],
            out_specs=[
                own_column(width // 2),
                own_column(width // 2),
                own_column(length),
                whole(small_top.shape),
            ],
            scratch_shapes=[
                pltpu.VMEM((length, length), bf16),
                pltpu.VMEM((length, length), bf16),
                pltpu.VMEM((BLK, rels), f32),
            ],
        ),
        out_shape=[
            jax.ShapeDtypeStruct((width // 2, 3 * width), bf16),
            jax.ShapeDtypeStruct((width // 2, 3 * width), bf16),
            jax.ShapeDtypeStruct((length, 3 * width), bf16),
            jax.ShapeDtypeStruct(small_top.shape, f32),
        ],
        cost_estimate=pl.CostEstimate(flops=0, bytes_accessed=0, transcendentals=0),
        name="attend_back",
    )(place, tokens_t, tables, mask, feat_back, swap, turn, u, phi, value, inverse, mixed, grad_mixed, small_top)


def block_diagonal(matrix):
    zero = jnp.zeros_like(matrix)
    return jnp.concatenate(
        [jnp.concatenate([matrix, zero], axis=1), jnp.concatenate([zero, matrix], axis=1)], axis=0
    )


def feature_tables(features):
    size = features.shape[0]
    ones = block_diagonal(jnp.ones((size, size), f32)).astype(bf16)
    high, low = split_low(block_diagonal(features))
    half = ones * -0.5
    forward = jnp.concatenate([high, low, high, half, half, half], axis=0)
    high, low = split_low(block_diagonal(features.T))
    none = jnp.zeros_like(ones)
    backward = jnp.concatenate(
        [jnp.concatenate([high, low, high], axis=0), jnp.concatenate([ones, none, ones], axis=0)],
        axis=1,
    )
    swap = jnp.concatenate([-ones[:, size:], -ones[:, :size]], axis=1)
    turn = jnp.eye(BLK, dtype=bf16)[::-1]
    return forward, backward, jnp.concatenate([swap, swap], axis=0), jnp.tile(turn, (3, 1))


def prepare_ffn_kernel(up_ref, down_ref, ffn_ref):
    rows = up_ref.shape[0]
    ffn_ref[:rows] = up_ref[...].astype(bf16)
    ffn_ref[rows:] = down_ref[...].astype(bf16)


def prepare_ffn(up, down):
    return pl.pallas_call(
        prepare_ffn_kernel,
        out_shape=jax.ShapeDtypeStruct((2 * up.shape[0], up.shape[1]), bf16),
        name="prepare_ffn",
    )(up, down)


def prepare_kernel(q_ref, k_ref, v_ref, o_ref, att_ref):
    width = o_ref.shape[1]
    lanes = att_ref.shape[1] // 4 // (width // 128)
    for j, ref in enumerate((q_ref, k_ref, v_ref)):
        for p in range(width // lanes):
            to = (3 * p + j) * lanes
            att_ref[:, to : to + lanes] = ref[:, p * lanes : (p + 1) * lanes].astype(bf16)
    att_ref[:, 3 * width :] = o_ref[...].astype(bf16)


def prepare(query, key, value, out):
    own, width = query.shape
    return pl.pallas_call(
        prepare_kernel,
        out_shape=jax.ShapeDtypeStruct((own, 4 * width), bf16),
        name="prepare",
    )(query, key, value, out)


root_half = 0.7071067811865476
inv_root_two_pi = 0.3989422804014327
eps = 1e-05


def norm_stats(residual):
    centered = residual - jnp.mean(residual, axis=1, keepdims=True)
    inverse = lax.rsqrt(jnp.mean(centered * centered, axis=1, keepdims=True) + eps)
    return centered * inverse, inverse


def norm_back(grad, xhat, inverse, gain):
    scaled = grad * gain
    mean_grad = jnp.mean(scaled, axis=1, keepdims=True)
    mean_dot = jnp.mean(scaled * xhat, axis=1, keepdims=True)
    return (scaled - mean_grad - xhat * mean_dot) * inverse


def column_sum(x):
    return jnp.sum(x, axis=0, keepdims=True)


def ffn_kernel(
    place_ref,
    low_ref,
    low_t_ref,
    xhat_ref,
    up_ref,
    down_ref,
    up_bias_ref,
    vec_ref,
    live_ref,
    cot_ref,
    out_ref,
    acc_ref,
    up_other_ref,
    up_mine_ref,
    down_other_ref,
    down_mine_ref,
    dup_bias_ref,
    dvec_ref,
    act_ref,
    slope_ref,
    gb_ref,
    gb_t_ref,
):
    phase = pl.program_id(0)
    part = pl.program_id(1)
    parts = pl.num_programs(1)
    length, width = low_ref.shape
    rows, hidden = up_ref.shape[1:]
    vec = vec_ref[...]
    down_bias, gain_one, shift_one, gain_two, shift_two = (vec[i : i + 1] for i in range(5))

    @pl.when((phase == 0) & (part == 0))
    def _():
        acc_ref[...] = jnp.zeros_like(acc_ref)

    @pl.when(phase == 0)
    def _():
        up = up_ref[...].reshape(width, hidden)
        down = down_ref[...].reshape(width, hidden)
        v = dot(low_ref[...], up) + up_bias_ref[...]
        half = 0.5 + 0.5 * lax.erf(v * root_half)
        act = (v * half).astype(bf16)
        act_ref[part] = act
        slope_ref[part] = half + v * (jnp.exp(-0.5 * v * v) * inv_root_two_pi)
        acc_ref[...] += dot_nt(act, down)

    @pl.when((phase == 0) & (part == parts - 1))
    def _():
        live = live_ref[...]
        normed = xhat_ref[...] * gain_one + shift_one
        xhat, inverse = norm_stats(normed + (acc_ref[...] + down_bias))
        out_ref[...] = ((xhat * gain_two + shift_two) * live).astype(bf16)
        grad = cot_ref[...].astype(f32) * live
        grad_two = norm_back(grad, xhat, inverse, gain_two)
        low = grad_two.astype(bf16)
        gb_ref[...] = low
        gb_t_ref[...] = grad_two.T.astype(bf16)
        dvec_ref[0:1, :] = column_sum(low.astype(f32))
        dvec_ref[3:4, :] = column_sum(grad * xhat)
        dvec_ref[4:5, :] = column_sum(grad)
        dvec_ref[1:3, :] = jnp.zeros((2, width), f32)
        dvec_ref[5:8, :] = jnp.zeros((3, width), f32)
        acc_ref[...] = grad_two

    def backward(d_up_ref, d_down_ref):
        up = up_ref[...].reshape(width, hidden)
        down = down_ref[...].reshape(width, hidden)
        grad_act = dot(gb_ref[...], down)
        grad_hidden = (grad_act * slope_ref[part]).astype(bf16)
        dup_bias_ref[...] = column_sum(grad_hidden.astype(f32))
        d_up = dot(low_t_ref[...], grad_hidden).astype(bf16)
        d_down = dot(gb_t_ref[...], act_ref[part]).astype(bf16)
        d_up_ref[...] = d_up.reshape(-1, rows, hidden)
        d_down_ref[...] = d_down.reshape(-1, rows, hidden)
        acc_ref[...] += dot_nt(grad_hidden, up)

    @pl.when((phase == 1) & (part < parts // 2))
    def _():
        backward(up_other_ref, down_other_ref)

    @pl.when((phase == 1) & (part >= parts // 2))
    def _():
        backward(up_mine_ref, down_mine_ref)


def ffn_last_kernel(
    place_ref,
    acc_ref,
    xhat_ref,
    inv_ref,
    mixed_t_ref,
    wo_ref,
    vec_ref,
    dvec_in_ref,
    grad_one_ref,
    gm_ref,
    wo_other_ref,
    wo_mine_ref,
    dvec_ref,
):
    width = acc_ref.shape[1]
    grad = acc_ref[...]
    xhat = xhat_ref[...]
    grad_one = norm_back(grad, xhat, inv_ref[...], vec_ref[1:2, :])
    grad_one_ref[...] = grad_one
    grad_att = grad_one.astype(bf16)
    gm_ref[...] = dot_nt(grad_att, wo_ref[...]).astype(bf16)
    half = width // 2
    place = place_ref[0]
    mine = pl.ds(pl.multiple_of(place * half, half), half)
    other = pl.ds(pl.multiple_of((1 - place) * half, half), half)
    wo_mine_ref[...] = dot(mixed_t_ref[mine, :], grad_att).astype(bf16)
    wo_other_ref[...] = dot(mixed_t_ref[other, :], grad_att).astype(bf16)
    dvec_ref[...] = dvec_in_ref[...]
    dvec_ref[1:2, :] = column_sum(grad * xhat)
    dvec_ref[2:3, :] = column_sum(grad)


def first_norm_kernel(tok_ref, mixed_ref, wo_ref, vec_ref, low_ref, low_t_ref, xhat_ref, inv_ref):
    residual = tok_ref[...].astype(f32) + dot(mixed_ref[...], wo_ref[...])
    xhat, inverse = norm_stats(residual)
    normed = xhat * vec_ref[1:2, :] + vec_ref[2:3, :]
    xhat_ref[...] = xhat
    inv_ref[...] = inverse
    low_ref[...] = normed.astype(bf16)
    low_t_ref[...] = normed.T.astype(bf16)


def first_norm(tokens, mixed, attention_weights, vectors):
    length, width = tokens.shape
    wo_column = attention_weights.shape[1] // width - 1
    whole = lambda shape: pl.BlockSpec(shape, lambda i: (0,) * len(shape))
    return pl.pallas_call(
        first_norm_kernel,
        grid=(1,),
        in_specs=[
            whole((length, width)),
            whole((length, width)),
            pl.BlockSpec((width, width), lambda i: (0, wo_column)),
            whole(vectors.shape),
        ],
        out_specs=[
            whole((length, width)),
            whole((width, length)),
            whole((length, width)),
            whole((length, 1)),
        ],
        out_shape=[
            jax.ShapeDtypeStruct((length, width), bf16),
            jax.ShapeDtypeStruct((width, length), bf16),
            jax.ShapeDtypeStruct((length, width), f32),
            jax.ShapeDtypeStruct((length, 1), f32),
        ],
        cost_estimate=pl.CostEstimate(flops=0, bytes_accessed=0, transcendentals=0),
        name="first_norm",
    )(tokens, mixed, attention_weights, vectors)


def feed_forward(
    place,
    low,
    low_t,
    xhat,
    inverse,
    mixed_t,
    attention_weights,
    weights,
    up_bias,
    vectors,
    live,
    cotangent,
):
    length, width = low.shape
    parts, shards, _, rows, hidden = weights.shape
    xs = parts // 2
    whole = lambda shape: pl.BlockSpec(shape, lambda p, w, c: (0,) * len(shape))
    once = lambda shape: pl.BlockSpec(
        shape, lambda p, w, c: (0,) * len(shape), pipeline_mode=pl.Buffered(1)
    )
    wo_column = attention_weights.shape[1] // width - 1
    wide = (length, width)
    part_of = lambda w, c: 2 * lax.rem(w, xs) + jnp.where(w < xs, 1 - c[0], c[0])
    weight_spec = lambda which: pl.BlockSpec(
        (None, shards, None, rows, hidden), lambda p, w, c: (part_of(w, c), 0, which, 0, 0)
    )
    other_spec = pl.BlockSpec(
        (None, shards, rows, hidden), lambda p, w, c: (p * jnp.minimum(w, xs - 1), 0, 0, 0)
    )
    mine_spec = pl.BlockSpec(
        (None, shards, rows, hidden), lambda p, w, c: (p * jnp.maximum(w - xs, 0), 0, 0, 0)
    )
    grads = jax.ShapeDtypeStruct((xs, shards, rows, hidden), bf16)
    out, acc, up_other, up_mine, down_other, down_mine, dup_bias, dvec = pl.pallas_call(
        ffn_kernel,
        grid_spec=pltpu.PrefetchScalarGridSpec(
            num_scalar_prefetch=1,
            grid=(2, parts),
            in_specs=[
                once(wide),
                once((width, length)),
                once(wide),
                weight_spec(0),
                weight_spec(1),
                pl.BlockSpec((None, 1, hidden), lambda p, w, c: (part_of(w, c), 0, 0)),
                whole(vectors.shape),
                once((length, 1)),
                once(wide),
            ],
            out_specs=[
                whole(wide),
                whole(wide),
                other_spec,
                mine_spec,
                other_spec,
                mine_spec,
                pl.BlockSpec(
                    (None, 1, hidden), lambda p, w, c: (part_of(w * p, c), 0, 0)
                ),
                whole((8, width)),
            ],
            scratch_shapes=[
                pltpu.VMEM((parts, length, hidden), bf16),
                pltpu.VMEM((parts, length, hidden), f32),
                pltpu.VMEM(wide, bf16),
                pltpu.VMEM((width, length), bf16),
            ],
        ),
        out_shape=[
            jax.ShapeDtypeStruct(wide, bf16),
            jax.ShapeDtypeStruct(wide, f32),
            grads,
            grads,
            grads,
            grads,
            jax.ShapeDtypeStruct((parts, 1, hidden), f32),
            jax.ShapeDtypeStruct((8, width), f32),
        ],
        compiler_params=pltpu.CompilerParams(vmem_limit_bytes=58 * 1024 * 1024),
        cost_estimate=pl.CostEstimate(flops=0, bytes_accessed=0, transcendentals=0),
        name="feed_forward",
    )(
        place,
        low,
        low_t,
        xhat,
        weights,
        weights,
        up_bias,
        vectors,
        live,
        cotangent,
    )
    grad_one, gm, wo_other, wo_mine, dvec = pl.pallas_call(
        ffn_last_kernel,
        grid_spec=pltpu.PrefetchScalarGridSpec(
            num_scalar_prefetch=1,
            grid=(1,),
            in_specs=[
                pl.BlockSpec(wide, lambda i, c: (0, 0)),
                pl.BlockSpec(wide, lambda i, c: (0, 0)),
                pl.BlockSpec((length, 1), lambda i, c: (0, 0)),
                pl.BlockSpec((width, length), lambda i, c: (0, 0)),
                pl.BlockSpec((width, width), lambda i, c: (0, wo_column)),
                pl.BlockSpec(vectors.shape, lambda i, c: (0, 0)),
                pl.BlockSpec((8, width), lambda i, c: (0, 0)),
            ],
            out_specs=[
                pl.BlockSpec(wide, lambda i, c: (0, 0)),
                pl.BlockSpec(wide, lambda i, c: (0, 0)),
                pl.BlockSpec((width // 2, width), lambda i, c: (0, 0)),
                pl.BlockSpec((width // 2, width), lambda i, c: (0, 0)),
                pl.BlockSpec((8, width), lambda i, c: (0, 0)),
            ],
        ),
        out_shape=[
            jax.ShapeDtypeStruct(wide, f32),
            jax.ShapeDtypeStruct(wide, bf16),
            jax.ShapeDtypeStruct((width // 2, width), bf16),
            jax.ShapeDtypeStruct((width // 2, width), bf16),
            jax.ShapeDtypeStruct((8, width), f32),
        ],
        cost_estimate=pl.CostEstimate(flops=0, bytes_accessed=0, transcendentals=0),
        name="ffn_last",
    )(place, acc, xhat, inverse, mixed_t, attention_weights, vectors, dvec)
    return (
        out,
        grad_one,
        gm,
        up_other,
        up_mine,
        down_other,
        down_mine,
        wo_other,
        wo_mine,
        dup_bias,
        dvec,
    )


class Grid:
    def __init__(self, batch, wide):
        self.devices = batch * wide
        self.sizes = dict(z=4, y=batch // 4, x=wide // 2, c=2)
        self.strides = dict(z=batch // 4 * wide, y=wide, x=2, c=1)
        flat = lax.axis_index("batch") * wide + lax.axis_index("wide")
        self.place = {d: lax.rem(flat // self.strides[d], n) for d, n in self.sizes.items()}
        self.vector = jnp.stack([self.place[d] for d in "zyxc"])

    def shift(self, value, **offsets):
        pairs = []
        for i in range(self.devices):
            target = i
            for d, o in offsets.items():
                s, n = self.strides[d], self.sizes[d]
                target += ((i // s + o) % n - i // s % n) * s
            pairs.append((i, target))
        return lax.ppermute(value, ("batch", "wide"), pairs)

    def at(self, d, offset):
        return lax.rem(self.place[d] + (offset + self.sizes[d]), self.sizes[d])

    def block_at(self, d, offset):
        k, n = "zyxc".index(d), self.sizes[d]
        return lambda vector: lax.rem(vector[k] + offset, n)

    def offsets(self, dims):
        ranges = [range(self.sizes[d]) for d in dims]
        return [dict(zip(dims, o)) for o in itertools.product(*ranges)]

    def swap(self, value, dims):
        groups = {}
        for i in range(self.devices):
            key = tuple(i // self.strides[d] % n for d, n in self.sizes.items() if d not in dims)
            groups.setdefault(key, []).append(i)
        return lax.all_to_all(
            value, ("batch", "wide"), 0, 0, axis_index_groups=list(groups.values())
        )

    def gather(self, value, names, dims):
        parts = [(o, self.shift(value, **o) if any(o.values()) else value) for o in self.offsets(dims)]
        if len(parts) == 2:
            (d,) = dims
            own, other = value, parts[1][1]
            first = self.place[d] == 0
            return jnp.concatenate(
                [jnp.where(first, own, other), jnp.where(first, other, own)], axis=names.index(d)
            )
        shape = [self.sizes[d] if d in dims else n for d, n in zip(names, value.shape)]
        out = jnp.zeros(shape + list(value.shape[len(names) :]), value.dtype)
        for o, part in parts:
            start = [self.at(d, -o[d]) if d in dims else 0 for d in names]
            out = lax.dynamic_update_slice(out, part, start + [0] * (value.ndim - len(names)))
        return out

    def send(self, sends, dims):
        return [self.shift(value, **o) for o, value in zip(self.offsets(dims)[1:], sends)]


class Combine:
    def __init__(self, grid, steps):
        self.grid, self.steps = grid, steps
        self.inputs, self.in_specs, self.shapes, self.out_specs, self.terms = [], [], [], [], []

    def spec(self, block, where):
        picks = []
        for w in where:
            if w is None:
                picks.append(lambda i, v: 0)
            elif w == "step":
                picks.append(lambda i, v: i)
            else:
                at = self.grid.block_at(*w)
                picks.append(lambda i, v, at=at: at(v))
        return pl.BlockSpec(block, lambda i, v: tuple(p(i, v) for p in picks))

    def read(self, arrays, where):
        numbers = []
        for a in arrays:
            block = tuple(n if w is None else None for n, w in zip(a.shape, where))
            numbers.append(len(self.inputs))
            self.inputs.append(a)
            self.in_specs.append(self.spec(block, where))
        return numbers

    def add(self, addends, picks):
        numbers = []
        for names, array in addends:
            where = tuple(picks.get(d) for d in names)
            where = tuple((d, w) if isinstance(w, int) else w for d, w in zip(names, where))
            numbers += self.read([array], where + (None,) * (array.ndim - len(names)))
        return numbers

    def write(self, shape, dtype, terms, stepped=None):
        where = tuple("step" if n == stepped else None for n in range(len(shape)))
        block = tuple(n if w is None else None for n, w in zip(shape, where))
        self.shapes.append(jax.ShapeDtypeStruct(shape, dtype))
        self.out_specs.append(self.spec(block, where))
        self.terms.append(terms)

    def run(self, name):
        count = len(self.inputs)

        def kernel(vector_ref, *refs):
            for out_ref, terms in zip(refs[count:], self.terms):
                for target, *rest in terms:
                    total = None
                    for source, numbers in [rest] if len(rest) == 2 else rest[0]:
                        for n in numbers:
                            value = refs[n][source].astype(f32)
                            total = value if total is None else total + value
                    total = total.astype(out_ref.dtype)
                    if len(out_ref.shape) == 1:
                        total = total.reshape(out_ref.shape)
                    out_ref[target] = total

        return pl.pallas_call(
            kernel,
            grid_spec=pltpu.PrefetchScalarGridSpec(
                num_scalar_prefetch=1,
                grid=(self.steps,),
                in_specs=self.in_specs,
                out_specs=self.out_specs,
            ),
            out_shape=self.shapes,
            compiler_params=pltpu.CompilerParams(vmem_limit_bytes=63 * 1024 * 1024 + 900 * 1024),
            cost_estimate=pl.CostEstimate(flops=0, bytes_accessed=0, transcendentals=0),
            name=name,
        )(self.grid.vector, *self.inputs)


everything = (Ellipsis,)


def token_gradient_kernel(d_ref, w_ref, before_ref, out_ref):
    @pl.when(pl.program_id(0) == 0)
    def _():
        out_ref[...] = before_ref[...]

    out_ref[...] += dot_nt(d_ref[...], w_ref[...])


def token_gradient(dqkv, weights, before):
    length, width = before.shape
    parts = 3
    columns = dqkv.shape[1] // parts
    whole = pl.BlockSpec((length, width), lambda k: (0, 0))
    return pl.pallas_call(
        token_gradient_kernel,
        grid=(parts,),
        in_specs=[
            pl.BlockSpec((length, columns), lambda k: (0, k)),
            pl.BlockSpec((width, columns), lambda k: (0, k)),
            whole,
        ],
        out_specs=whole,
        out_shape=jax.ShapeDtypeStruct((length, width), f32),
        cost_estimate=pl.CostEstimate(flops=0, bytes_accessed=0, transcendentals=0),
        name="token_gradient",
    )(dqkv, weights, before)


def hold(value, *others):
    return lax.optimization_barrier((value, others))


def per_device(
    batch,
    wide,
    tokens,
    block_row,
    block_live,
    query_weight,
    key_weight,
    value_weight,
    out_weight,
    position_bias,
    features,
    up_weight,
    up_bias,
    down_weight,
    down_bias,
    gain_one,
    shift_one,
    gain_two,
    shift_two,
    cotangent,
):
    grid = Grid(batch, wide)
    zs, ys, xs, cs = (grid.sizes[d] for d in "zyxc")
    length, width = tokens.shape
    heads, rels = position_bias.shape
    pairs = heads // 2
    own = query_weight.shape[0]
    lanes = width // pairs
    ffn_shard = prepare_ffn(up_weight, down_weight)
    query_weight, (ffn_shard,) = hold(query_weight, ffn_shard)
    shard = prepare(query_weight, key_weight, value_weight, out_weight)
    up_rows, hidden = up_weight.shape
    half = 2 * width
    gathered = grid.gather(shard.reshape(1, 1, 1, 1, own, 4 * width), "zyxc", "z")
    first = grid.gather(gathered[..., :half], "zyxc", "x")
    second = grid.gather(gathered[..., half:], "zyxc", "y")
    inputs = (position_bias, features, block_row, block_live, tokens, down_bias)
    first, (second, *inputs) = hold(first, second, *inputs)
    position_bias, features, block_row, block_live, tokens, down_bias = inputs
    tables = toeplitz_tables(position_bias[:, ::-1])
    feat_forward, feat_back, swap, turn = feature_tables(features)
    offsets = jnp.arange(BLK, dtype=jnp.int32)
    live = (offsets[None, :] < block_live[:, None]).astype(f32).reshape(1, length)
    rows = jnp.broadcast_to(block_row[:, None], (block_row.shape[0], BLK)).reshape(1, length)
    mask = jnp.where(block_row[:, None] == rows, live, 0.0)
    by_core = lambda m: m.reshape(-1, cs, own, length).swapaxes(0, 1).reshape(width, length)
    tokens_t = by_core(tokens.T)
    vectors = jnp.stack([down_bias, gain_one, shift_one, gain_two, shift_two] + [down_bias] * 3)
    live_column = live.reshape(length, 1)

    first = grid.gather(first, "zyxc", "y")
    second = grid.gather(second, "zyxc", "x")
    early = (tables, feat_forward, feat_back, swap, turn, mask, tokens_t, vectors, live_column)
    first, (second, *early) = hold(first, second, *early)
    tables, feat_forward, feat_back, swap, turn, mask, tokens_t, vectors, live_column = early
    first = grid.gather(first, "zyxc", "c").reshape(width, half)
    second = grid.gather(second, "zyxc", "c").reshape(width, half)
    attention_weights = jnp.concatenate([first, second], axis=1)
    ffn_weights = lax.all_gather(ffn_shard, ("wide", "batch"), axis=0, tiled=False)
    ffn_weights = ffn_weights.reshape(wide, batch, 2, up_rows, hidden)
    mixed, mixed32, u, phi, value, inverse = attend(
        tokens, attention_weights, tables, mask, feat_forward, heads
    )
    place = grid.place["c"].reshape(1)
    normed = first_norm(tokens, mixed, attention_weights, vectors)
    normed, (mixed_t, grid.vector) = hold(normed, by_core(mixed.T), grid.vector)
    (
        out_tokens,
        grad_one,
        grad_mixed,
        up_other_grad,
        up_mine_grad,
        down_other,
        down_mine,
        out_other,
        out_mine,
        dup_bias,
        dvec,
    ) = feed_forward(
        place,
        *normed,
        mixed_t,
        attention_weights,
        ffn_weights,
        up_bias.reshape(wide, 1, hidden),
        vectors,
        live_column,
        cotangent,
    )
    ffn_view = lambda m: ("xzy", m.reshape(xs, zs, ys, up_rows, hidden))
    att_view = lambda m: ("zyx", m.reshape(zs, ys, xs, own, -1))
    down_recv = grid.shift(down_other, c=1)
    up = [ffn_view(up_mine_grad), ffn_view(grid.shift(up_other_grad, c=1))]
    out = [att_view(out_mine), att_view(grid.shift(out_other, c=1))]

    columns = 4 * width
    bias_rows = heads * rels // columns
    extra = -(-(3 + bias_rows) // 8) * 8
    first_row = extra - bias_rows
    small_top = jnp.concatenate(
        [dup_bias.reshape(1, columns), dvec.reshape(2, columns), jnp.zeros((extra - 3, columns), f32)]
    )
    down_mine, (small_top,) = hold(down_mine, small_top)
    down = [ffn_view(down_mine), ffn_view(down_recv)]

    step = Combine(grid, zs)
    for y in range(1, ys):
        terms = [(everything, everything, step.add(down, dict(z="step", y=y)))]
        step.write((xs, zs, up_rows, hidden), bf16, terms, stepped=1)
    for x in range(1, xs):
        terms = [(everything, everything, step.add(up, dict(z="step", x=x)))]
        step.write((zs, ys, up_rows, hidden), bf16, terms, stepped=0)
    sends = step.run("ffn_sum_core")
    down_sends, up_sends = sends[: ys - 1], sends[ys - 1 :]
    grad_mixed, (down_sends, up_sends) = hold(grad_mixed, down_sends, up_sends)
    down_new = grid.send(down_sends, "y")
    up_new = grid.send(up_sends, "x")

    dw_mine, dw_other, dqkv, small = attend_back(
        place,
        tokens_t,
        tables,
        mask,
        feat_back,
        swap,
        turn,
        u,
        phi,
        value,
        inverse,
        mixed32,
        grad_mixed,
        small_top,
        heads,
    )
    dw_mine, (dw_other, dqkv, small, down_new, up_new) = hold(
        dw_mine, dw_other, dqkv, small, down_new, up_new
    )
    down += [("xz", v) for v in down_new]
    up += [("zy", v) for v in up_new]
    att = [att_view(dw_mine), att_view(grid.shift(dw_other, c=1))]

    step = Combine(grid, 1)
    block = (zs, up_rows, hidden)
    for x in range(1, xs):
        terms = [(everything, everything, step.add(down, dict(y=0, x=x)))]
        step.write(block, bf16, terms)
    for y in range(1, ys):
        terms = [(everything, everything, step.add(up, dict(x=0, y=y)))]
        step.write(block, bf16, terms)
    sends = step.run("ffn_sum_plane")
    down_new = grid.send(sends[: xs - 1], "x")
    up_new = grid.send(sends[xs - 1 :], "y")
    small = small + grid.shift(small, c=1)
    small_new = grid.send([small.astype(bf16)] * (zs - 1), "z")
    dw_mine, sends = hold(dw_mine, *sends)
    att[0] = att_view(dw_mine)
    step = Combine(grid, 1)
    for o in grid.offsets("yx")[1:]:
        terms = [
            ((..., slice(0, 3 * width)), everything, step.add(att, o)),
            ((..., slice(3 * width, None)), everything, step.add(out, o)),
        ]
        step.write((zs, own, columns), bf16, terms)
    att_sends = step.run("att_sum_core")
    down_new, (up_new, att_sends, small_new) = hold(down_new, up_new, att_sends, small_new)
    down += [("z", v) for v in down_new]
    up += [("z", v) for v in up_new]
    small = (small + sum(v.astype(f32) for v in small_new)).astype(bf16)
    small = jnp.broadcast_to(small[None], (ys * xs,) + small.shape)
    att_new = grid.send(att_sends, "yx")

    here = dict(z=0, y=0, x=0)
    step = Combine(grid, 1)
    for z in range(1, zs):
        terms = [
            ((j,), everything, step.add(addends, dict(z=z, y=0, x=0)))
            for j, addends in enumerate((up, down))
        ]
        step.write((2, up_rows, hidden), bf16, terms)
    sends = step.run("ffn_sum_second")
    dqkv, (small, *sends) = hold(dqkv, small, *sends)
    small = grid.swap(small, "yx")
    ffn_new = grid.send(sends, "z")
    grad_tokens = token_gradient(dqkv, attention_weights, grad_one)
    att_new, (grad_tokens, *sends) = hold(att_new, grad_tokens, *sends)
    att_new = [("z", v) for v in att_new]

    step = Combine(grid, 1)
    for z in range(1, zs):
        picks = dict(z=z, y=0, x=0)
        top = slice(0, own)
        new = step.add(att_new, picks)
        head, tail = slice(0, 3 * width), slice(3 * width, None)
        terms = [
            ((top, head), everything, step.add(att, picks)),
            ((top, tail), everything, step.add(out, picks)),
        ]
        terms = [
            (target, [(everything, numbers), ((slice(None), target[1]), new)])
            for target, _, numbers in terms
        ]
        step.write((own, columns), bf16, terms)
    att_sends = step.run("att_sum_plane")
    last = grid.send(att_sends, "z")

    step = Combine(grid, 1)
    new = step.read(ffn_new, (None, None, None))
    for j, addends in enumerate((up, down)):
        terms = [(everything, [(everything, step.add(addends, here)), ((j,), new)])]
        step.write((up_rows, hidden), f32, terms)
    up_own, down_own = step.run("ffn_sum_last")

    step = Combine(grid, 1)
    new = step.add(att_new, here)
    head = (slice(None), slice(0, 3 * width))
    tail = (slice(None), slice(3 * width, None))
    top = slice(0, own)
    terms = [
        ((top, head[1]), [(everything, step.add(att, here)), (head, new)]),
        ((top, tail[1]), [(everything, step.add(out, here)), (tail, new)]),
    ]
    step.write((own, columns), f32, terms)
    small_in = step.read([small], (None, None, None))

    def small_term(r, cols):
        return [((k, slice(r, r + 1), cols), small_in) for k in range(ys * xs)]

    step.write((columns,), f32, [(everything, small_term(0, slice(None)))])
    for j in range(5):
        at = j % 4 * width
        step.write((width,), f32, [(everything, small_term(1 + j // 4, slice(at, at + width)))])
    per_row = columns // rels
    terms = []
    for h in range(heads):
        at = h % per_row * rels
        term = small_term(first_row + h // per_row, slice(at, at + rels))
        terms.append(((slice(h, h + 1),), term))
    step.write((heads, rels), f32, terms)
    before, dup_bias, *dvec, dbias = step.run("att_sum_own")

    step = Combine(grid, 1)
    last = step.read([before, *last], (None, None))
    for j in range(3):
        terms = []
        for p in range(pairs):
            cols = slice((3 * p + j) * lanes, (3 * p + j + 1) * lanes)
            terms.append(((slice(None), slice(p * lanes, (p + 1) * lanes)), (top, cols), last))
        step.write((own, width), f32, terms)
    step.write((own, width), f32, [(everything, (top, tail[1]), last)])

    dq, dk, dv, out_own = step.run("last_sum")
    return (
        out_tokens,
        grad_tokens,
        dq,
        dk,
        dv,
        out_own,
        dbias,
        up_own,
        dup_bias,
        down_own,
        *dvec,
    )


def solution(mesh):
    both = P(("batch", "wide"), None)
    placed = (
        both,
        P(("batch", "wide")),
        P(("batch", "wide")),
        both,
        both,
        both,
        both,
        P(),
        P(),
        P("batch", "wide"),
        P(),
        P("batch", "wide"),
        P(),
        P(),
        P(),
        P(),
        P(),
        both,
    )
    outs = (
        both,
        both,
        both,
        both,
        both,
        both,
        P(),
        P("batch", "wide"),
        P(),
        P("batch", "wide"),
        P(),
        P(),
        P(),
        P(),
        P(),
    )
    return jax.shard_map(
        partial(per_device, mesh.shape["batch"], mesh.shape["wide"]),
        mesh=mesh,
        in_specs=placed,
        out_specs=outs,
        check_vma=False,
    )
```

```python
import itertools
from functools import partial

import jax
import jax.numpy as jnp
from jax import lax
from jax.experimental import pallas as pl
from jax.experimental.pallas import tpu as pltpu
from jax.sharding import PartitionSpec as P

BLK = 128
f32 = jnp.float32
bf16 = jnp.bfloat16
nt_dims = (((1,), (1,)), ((), ()))


def dot(a, b):
    return jnp.dot(a, b, preferred_element_type=f32)


def dot_nt(a, b):
    return lax.dot_general(a, b, nt_dims, preferred_element_type=f32)


def split_low(x):
    high = x.astype(bf16)
    return high, (x - high.astype(f32)).astype(bf16)


def toeplitz_kernel(bias_ref, out_ref):
    heads = bias_ref.shape[0]
    rels = bias_ref.shape[1]
    for h in range(heads):
        row = jnp.broadcast_to(jnp.exp(bias_ref[h : h + 1, :]), (BLK, rels))
        out_ref[h] = pltpu.roll(row, rels - BLK + 1, 1, stride=1, stride_axis=0)


def toeplitz_tables(flipped_bias):
    heads, rels = flipped_bias.shape
    step = 2
    return pl.pallas_call(
        toeplitz_kernel,
        grid=(heads // step,),
        in_specs=[pl.BlockSpec((None, step, rels), lambda h: (h, 0, 0))],
        out_specs=pl.BlockSpec((step, BLK, rels), lambda h: (h, 0, 0)),
        out_shape=jax.ShapeDtypeStruct((heads, BLK, rels), f32),
        cost_estimate=pl.CostEstimate(
            flops=5_000_000_000, bytes_accessed=8_000_000, transcendentals=0
        ),
        name="toeplitz",
    )(flipped_bias.reshape(heads // step, step, rels))


def lane_half(shape):
    return lax.broadcasted_iota(jnp.int32, shape, 1) < shape[1] // 2


def pair_features(u, feat_ref):
    high, low = split_low(u)
    square = u * u
    s_high, rest = split_low(square)
    rest = square - s_high.astype(f32)
    s_mid, s_low = split_low(rest)
    lhs = jnp.concatenate([high, high, low, s_high, s_mid, s_low], axis=1)
    return jnp.exp(dot(lhs, feat_ref[...]))


def attend_kernel(
    scale,
    tok_ref,
    w_ref,
    table_ref,
    mask_ref,
    feat_ref,
    mixed_ref,
    mixed32_ref,
    u_ref,
    phi_ref,
    val_ref,
    inv_ref,
    weights_ref,
):
    length = tok_ref.shape[0]
    pair = mixed_ref.shape[1]
    size = pair // 2
    blocks = length // BLK
    qkv = dot(tok_ref[...], w_ref[...])
    uq = qkv[:, :pair] * scale
    uk = qkv[:, pair : 2 * pair] * scale
    value = qkv[:, 2 * pair :].astype(bf16)
    pq = pair_features(uq, feat_ref)
    pk = pair_features(uk, feat_ref)
    u_ref[:, :pair] = uq
    u_ref[:, pair:] = uk
    phi_ref[:, :pair] = pq
    phi_ref[:, pair:] = pk
    val_ref[...] = value
    pq = pq.astype(bf16)
    pk = pk.astype(bf16)
    first = lane_half(value.shape)
    zero = jnp.zeros_like(value)
    one = jnp.ones_like(value)
    out = None
    for h in range(2):
        cols = slice(h * size, (h + 1) * size)
        here = first if h == 0 else jnp.logical_not(first)
        for b in range(blocks):
            rows = slice(b * BLK, (b + 1) * BLK)
            start = (blocks - 1 - b) * BLK
            scores = dot_nt(pq[rows, cols], pk[:, cols])
            coupling = table_ref[h, :, start : start + length] * mask_ref[b : b + 1, :]
            weights_ref[rows, :] = (coupling * scores).astype(bf16)
        rhs = jnp.concatenate([jnp.where(here, value, zero), jnp.where(here, one, zero)], axis=1)
        part = dot(weights_ref[...], rhs)
        out = part if out is None else out + part
    inverse = 1.0 / out[:, pair:]
    mixed = out[:, :pair] * inverse
    inv_ref[...] = inverse
    mixed32_ref[...] = mixed
    mixed_ref[...] = mixed.astype(bf16)


def attend(tokens, weights, tables, mask, feat_split, heads):
    length, width = tokens.shape
    pair = 2 * width // heads
    pairs = heads // 2
    rels = tables.shape[2]
    scale = float((pair // 2) ** (-0.25))
    whole = lambda shape: pl.BlockSpec(shape, lambda h: (0,) * len(shape))
    column = lambda cols: pl.BlockSpec((length, cols), lambda h: (0, h))
    return pl.pallas_call(
        partial(attend_kernel, scale),
        grid=(pairs,),
        in_specs=[
            whole((length, width)),
            pl.BlockSpec((width, 3 * pair), lambda h: (0, h)),
            pl.BlockSpec((2, BLK, rels), lambda h: (h, 0, 0)),
            whole(mask.shape),
            whole(feat_split.shape),
        ],
        out_specs=[
            column(pair),
            column(pair),
            column(2 * pair),
            column(2 * pair),
            column(pair),
            column(pair),
        ],
        out_shape=[
            jax.ShapeDtypeStruct((length, width), bf16),
            jax.ShapeDtypeStruct((length, width), f32),
            jax.ShapeDtypeStruct((length, 2 * width), f32),
            jax.ShapeDtypeStruct((length, 2 * width), f32),
            jax.ShapeDtypeStruct((length, width), bf16),
            jax.ShapeDtypeStruct((length, width), f32),
        ],
        scratch_shapes=[pltpu.VMEM((length, length), bf16)],
        cost_estimate=pl.CostEstimate(flops=0, bytes_accessed=0, transcendentals=0),
        name="attend",
    )(tokens, weights, tables, mask, feat_split)


def pair_backward(scale, grad_phi, phi, u, feat_ref):
    pair = u.shape[1]
    high, low = split_low(grad_phi * phi)
    back = dot(jnp.concatenate([high, high, low], axis=1), feat_ref[...])
    return (scale * (back[:, :pair] - u * back[:, pair:])).astype(bf16)


def attend_back_kernel(
    scale,
    place_ref,
    tok_t_ref,
    table_ref,
    mask_ref,
    feat_ref,
    swap_ref,
    turn_ref,
    u_ref,
    phi_ref,
    val_ref,
    inv_ref,
    mixed_ref,
    gm_ref,
    top_ref,
    dw_mine_ref,
    dw_other_ref,
    dqkv_ref,
    small_ref,
    probs_ref,
    gs_ref,
    diag_ref,
):
    length, pair = val_ref.shape
    size = pair // 2
    blocks = length // BLK

    @pl.when(pl.program_id(0) == 0)
    def _():
        small_ref[...] = top_ref[...]

    gm = gm_ref[...].astype(f32)
    scaled = gm * inv_ref[...]
    g_high, g_low = split_low(scaled)
    gt = scaled.T
    gt_high, gt_low = split_low(gt)
    d_high, d_low = split_low(scaled * mixed_ref[...])
    inner = dot(jnp.concatenate([d_high, d_low], axis=1), swap_ref[...])
    i_high, i_low = split_low(inner)
    phi = phi_ref[...]
    pq32, pk32 = phi[:, :pair], phi[:, pair:]
    pq = pq32.astype(bf16)
    pk = pk32.astype(bf16)
    pq_t = pq32.T.astype(bf16)
    value = val_ref[...]
    first = lane_half(value.shape)
    unit = jnp.full_like(value, 1.0 / size)
    zero = jnp.zeros_like(value)
    gq = None
    gk_heads = []
    gv_heads = []
    for h in range(2):
        cols = slice(h * size, (h + 1) * size)
        here = first if h == 0 else jnp.logical_not(first)
        lhs = jnp.concatenate(
            [jnp.where(here, g_high, i_high), jnp.where(here, g_low, i_low)], axis=1
        )
        rhs = jnp.where(here, value, unit)
        rhs = jnp.concatenate([rhs, rhs], axis=1)
        diag_ref[...] = jnp.zeros_like(diag_ref)
        for b in range(blocks):
            rows = slice(b * BLK, (b + 1) * BLK)
            start = (blocks - 1 - b) * BLK
            window = slice(start, start + length)
            mask = mask_ref[b : b + 1, :]
            scores = dot_nt(pq[rows, cols], pk[:, cols])
            coupling = table_ref[h, :, window] * mask
            probs_ref[rows, :] = (coupling * scores).astype(bf16)
            grad_scores = dot_nt(lhs[rows], rhs) * coupling
            gs_ref[rows, :] = grad_scores.astype(bf16)
            diag_ref[:, window] += grad_scores * scores
        part = dot(gs_ref[...], jnp.where(here, pk, zero))
        gq = part if gq is None else gq + part
        gk_heads.append(dot(pq_t[cols, :], gs_ref[...]))
        both = dot(jnp.concatenate([gt_high[cols], gt_low[cols]], axis=0), probs_ref[...])
        gv_heads.append(both[:size] + both[size:])
        folded = diag_ref[...]
        half = BLK // 2
        while half >= 1:
            folded = pltpu.roll(folded[:half], half, 1) + folded[half:]
            half //= 2
        split = [folded[:, n : n + BLK] for n in range(0, folded.shape[1], BLK)]
        f_high, rest = split_low(jnp.concatenate(split, axis=0))
        f_mid, f_low = split_low(jnp.concatenate(split, axis=0) - f_high.astype(f32))
        turned = dot(jnp.concatenate([f_high, f_mid, f_low], axis=1), turn_ref[...])
        turned = [turned[n : n + 1] for n in reversed(range(len(split)))]
        head = 2 * pl.program_id(0) + h
        rels = table_ref.shape[2]
        per_row = small_ref.shape[1] // rels
        column = pl.multiple_of(lax.rem(head, per_row) * rels, rels)
        row = small_ref.shape[0] - pl.num_programs(0) * 2 // per_row + head // per_row
        small_ref[pl.ds(row, 1), pl.ds(column, rels)] = jnp.concatenate(turned, axis=1)
    gk = jnp.concatenate(gk_heads, axis=0).T
    gv = jnp.concatenate(gv_heads, axis=0).T.astype(bf16)
    u = u_ref[...]
    dq = pair_backward(scale, gq, pq32, u[:, :pair], feat_ref)
    dk = pair_backward(scale, gk, pk32, u[:, pair:], feat_ref)
    dqkv_ref[:, :pair] = dq
    dqkv_ref[:, pair : 2 * pair] = dk
    dqkv_ref[:, 2 * pair :] = gv
    half = tok_t_ref.shape[0] // 2
    place = place_ref[0]
    mine = pl.ds(pl.multiple_of(place * half, half), half)
    other = pl.ds(pl.multiple_of((1 - place) * half, half), half)
    dw_mine_ref[...] = dot(tok_t_ref[mine, :], dqkv_ref[...]).astype(bf16)
    dw_other_ref[...] = dot(tok_t_ref[other, :], dqkv_ref[...]).astype(bf16)


def attend_back(
    place,
    tokens_t,
    tables,
    mask,
    feat_back,
    swap,
    turn,
    u,
    phi,
    value,
    inverse,
    mixed,
    grad_mixed,
    small_top,
    heads,
):
    width, length = tokens_t.shape
    pair = 2 * width // heads
    rels = tables.shape[2]
    scale = float((pair // 2) ** (-0.25))
    whole = lambda shape: pl.BlockSpec(shape, lambda h, p: (0,) * len(shape))
    column = lambda cols: pl.BlockSpec((length, cols), lambda h, p: (0, h))
    own_column = lambda rows: pl.BlockSpec((rows, 3 * pair), lambda h, p: (0, h))
    return pl.pallas_call(
        partial(attend_back_kernel, scale),
        grid_spec=pltpu.PrefetchScalarGridSpec(
            num_scalar_prefetch=1,
            grid=(heads // 2,),
            in_specs=[
                whole((width, length)),
                pl.BlockSpec((2, BLK, rels), lambda h, p: (h, 0, 0)),
                whole(mask.shape),
                whole(feat_back.shape),
                whole(swap.shape),
                whole(turn.shape),
                column(2 * pair),
                column(2 * pair),
                column(pair),
                column(pair),
                column(pair),
                column(pair),
                whole(small_top.shape),
            ],
            out_specs=[
                own_column(width // 2),
                own_column(width // 2),
                own_column(length),
                whole(small_top.shape),
            ],
            scratch_shapes=[
                pltpu.VMEM((length, length), bf16),
                pltpu.VMEM((length, length), bf16),
                pltpu.VMEM((BLK, rels), f32),
            ],
        ),
        out_shape=[
            jax.ShapeDtypeStruct((width // 2, 3 * width), bf16),
            jax.ShapeDtypeStruct((width // 2, 3 * width), bf16),
            jax.ShapeDtypeStruct((length, 3 * width), bf16),
            jax.ShapeDtypeStruct(small_top.shape, f32),
        ],
        cost_estimate=pl.CostEstimate(flops=0, bytes_accessed=0, transcendentals=0),
        name="attend_back",
    )(place, tokens_t, tables, mask, feat_back, swap, turn, u, phi, value, inverse, mixed, grad_mixed, small_top)


def block_diagonal(matrix):
    zero = jnp.zeros_like(matrix)
    return jnp.concatenate(
        [jnp.concatenate([matrix, zero], axis=1), jnp.concatenate([zero, matrix], axis=1)], axis=0
    )


def feature_tables(features):
    size = features.shape[0]
    ones = block_diagonal(jnp.ones((size, size), f32)).astype(bf16)
    high, low = split_low(block_diagonal(features))
    half = ones * -0.5
    forward = jnp.concatenate([high, low, high, half, half, half], axis=0)
    high, low = split_low(block_diagonal(features.T))
    none = jnp.zeros_like(ones)
    backward = jnp.concatenate(
        [jnp.concatenate([high, low, high], axis=0), jnp.concatenate([ones, none, ones], axis=0)],
        axis=1,
    )
    swap = jnp.concatenate([-ones[:, size:], -ones[:, :size]], axis=1)
    turn = jnp.eye(BLK, dtype=bf16)[::-1]
    return forward, backward, jnp.concatenate([swap, swap], axis=0), jnp.tile(turn, (3, 1))


def prepare_ffn_kernel(up_ref, down_ref, ffn_ref):
    rows = up_ref.shape[0]
    ffn_ref[:rows] = up_ref[...].astype(bf16)
    ffn_ref[rows:] = down_ref[...].astype(bf16)


def prepare_ffn(up, down):
    return pl.pallas_call(
        prepare_ffn_kernel,
        out_shape=jax.ShapeDtypeStruct((2 * up.shape[0], up.shape[1]), bf16),
        name="prepare_ffn",
    )(up, down)


def prepare_kernel(q_ref, k_ref, v_ref, o_ref, att_ref):
    width = o_ref.shape[1]
    lanes = att_ref.shape[1] // 4 // (width // 128)
    for j, ref in enumerate((q_ref, k_ref, v_ref)):
        for p in range(width // lanes):
            to = (3 * p + j) * lanes
            att_ref[:, to : to + lanes] = ref[:, p * lanes : (p + 1) * lanes].astype(bf16)
    att_ref[:, 3 * width :] = o_ref[...].astype(bf16)


def prepare(query, key, value, out):
    own, width = query.shape
    return pl.pallas_call(
        prepare_kernel,
        out_shape=jax.ShapeDtypeStruct((own, 4 * width), bf16),
        name="prepare",
    )(query, key, value, out)


root_half = 0.7071067811865476
inv_root_two_pi = 0.3989422804014327
eps = 1e-05


def norm_stats(residual):
    centered = residual - jnp.mean(residual, axis=1, keepdims=True)
    inverse = lax.rsqrt(jnp.mean(centered * centered, axis=1, keepdims=True) + eps)
    return centered * inverse, inverse


def norm_back(grad, xhat, inverse, gain):
    scaled = grad * gain
    mean_grad = jnp.mean(scaled, axis=1, keepdims=True)
    mean_dot = jnp.mean(scaled * xhat, axis=1, keepdims=True)
    return (scaled - mean_grad - xhat * mean_dot) * inverse


def column_sum(x):
    return jnp.sum(x, axis=0, keepdims=True)


def ffn_kernel(
    place_ref,
    low_ref,
    low_t_ref,
    xhat_ref,
    up_ref,
    down_ref,
    up_bias_ref,
    vec_ref,
    live_ref,
    cot_ref,
    out_ref,
    acc_ref,
    up_other_ref,
    up_mine_ref,
    down_other_ref,
    down_mine_ref,
    dup_bias_ref,
    dvec_ref,
    act_ref,
    slope_ref,
    gb_ref,
    gb_t_ref,
):
    phase = pl.program_id(0)
    part = pl.program_id(1)
    parts = pl.num_programs(1)
    length, width = low_ref.shape
    rows, hidden = up_ref.shape[1:]
    vec = vec_ref[...]
    down_bias, gain_one, shift_one, gain_two, shift_two = (vec[i : i + 1] for i in range(5))

    @pl.when((phase == 0) & (part == 0))
    def _():
        acc_ref[...] = jnp.zeros_like(acc_ref)

    @pl.when(phase == 0)
    def _():
        up = up_ref[...].reshape(width, hidden)
        down = down_ref[...].reshape(width, hidden)
        v = dot(low_ref[...], up) + up_bias_ref[...]
        half = 0.5 + 0.5 * lax.erf(v * root_half)
        act = (v * half).astype(bf16)
        act_ref[part] = act
        slope_ref[part] = half + v * (jnp.exp(-0.5 * v * v) * inv_root_two_pi)
        acc_ref[...] += dot_nt(act, down)

    @pl.when((phase == 0) & (part == parts - 1))
    def _():
        live = live_ref[...]
        normed = xhat_ref[...] * gain_one + shift_one
        xhat, inverse = norm_stats(normed + (acc_ref[...] + down_bias))
        out_ref[...] = ((xhat * gain_two + shift_two) * live).astype(bf16)
        grad = cot_ref[...].astype(f32) * live
        grad_two = norm_back(grad, xhat, inverse, gain_two)
        low = grad_two.astype(bf16)
        gb_ref[...] = low
        gb_t_ref[...] = grad_two.T.astype(bf16)
        dvec_ref[0:1, :] = column_sum(low.astype(f32))
        dvec_ref[3:4, :] = column_sum(grad * xhat)
        dvec_ref[4:5, :] = column_sum(grad)
        dvec_ref[1:3, :] = jnp.zeros((2, width), f32)
        dvec_ref[5:8, :] = jnp.zeros((3, width), f32)
        acc_ref[...] = grad_two

    def backward(d_up_ref, d_down_ref):
        up = up_ref[...].reshape(width, hidden)
        down = down_ref[...].reshape(width, hidden)
        grad_act = dot(gb_ref[...], down)
        grad_hidden = (grad_act * slope_ref[part]).astype(bf16)
        dup_bias_ref[...] = column_sum(grad_hidden.astype(f32))
        d_up = dot(low_t_ref[...], grad_hidden).astype(bf16)
        d_down = dot(gb_t_ref[...], act_ref[part]).astype(bf16)
        d_up_ref[...] = d_up.reshape(-1, rows, hidden)
        d_down_ref[...] = d_down.reshape(-1, rows, hidden)
        acc_ref[...] += dot_nt(grad_hidden, up)

    @pl.when((phase == 1) & (part < parts // 2))
    def _():
        backward(up_other_ref, down_other_ref)

    @pl.when((phase == 1) & (part >= parts // 2))
    def _():
        backward(up_mine_ref, down_mine_ref)


def ffn_last_kernel(
    place_ref,
    acc_ref,
    xhat_ref,
    inv_ref,
    mixed_t_ref,
    wo_ref,
    vec_ref,
    dvec_in_ref,
    grad_one_ref,
    gm_ref,
    wo_other_ref,
    wo_mine_ref,
    dvec_ref,
):
    width = acc_ref.shape[1]
    grad = acc_ref[...]
    xhat = xhat_ref[...]
    grad_one = norm_back(grad, xhat, inv_ref[...], vec_ref[1:2, :])
    grad_one_ref[...] = grad_one
    grad_att = grad_one.astype(bf16)
    gm_ref[...] = dot_nt(grad_att, wo_ref[...]).astype(bf16)
    half = width // 2
    place = place_ref[0]
    mine = pl.ds(pl.multiple_of(place * half, half), half)
    other = pl.ds(pl.multiple_of((1 - place) * half, half), half)
    wo_mine_ref[...] = dot(mixed_t_ref[mine, :], grad_att).astype(bf16)
    wo_other_ref[...] = dot(mixed_t_ref[other, :], grad_att).astype(bf16)
    dvec_ref[...] = dvec_in_ref[...]
    dvec_ref[1:2, :] = column_sum(grad * xhat)
    dvec_ref[2:3, :] = column_sum(grad)


def first_norm_kernel(tok_ref, mixed_ref, wo_ref, vec_ref, low_ref, low_t_ref, xhat_ref, inv_ref):
    residual = tok_ref[...].astype(f32) + dot(mixed_ref[...], wo_ref[...])
    xhat, inverse = norm_stats(residual)
    normed = xhat * vec_ref[1:2, :] + vec_ref[2:3, :]
    xhat_ref[...] = xhat
    inv_ref[...] = inverse
    low_ref[...] = normed.astype(bf16)
    low_t_ref[...] = normed.T.astype(bf16)


def first_norm(tokens, mixed, attention_weights, vectors):
    length, width = tokens.shape
    wo_column = attention_weights.shape[1] // width - 1
    whole = lambda shape: pl.BlockSpec(shape, lambda i: (0,) * len(shape))
    return pl.pallas_call(
        first_norm_kernel,
        grid=(1,),
        in_specs=[
            whole((length, width)),
            whole((length, width)),
            pl.BlockSpec((width, width), lambda i: (0, wo_column)),
            whole(vectors.shape),
        ],
        out_specs=[
            whole((length, width)),
            whole((width, length)),
            whole((length, width)),
            whole((length, 1)),
        ],
        out_shape=[
            jax.ShapeDtypeStruct((length, width), bf16),
            jax.ShapeDtypeStruct((width, length), bf16),
            jax.ShapeDtypeStruct((length, width), f32),
            jax.ShapeDtypeStruct((length, 1), f32),
        ],
        cost_estimate=pl.CostEstimate(flops=0, bytes_accessed=0, transcendentals=0),
        name="first_norm",
    )(tokens, mixed, attention_weights, vectors)


def feed_forward(
    place,
    low,
    low_t,
    xhat,
    inverse,
    mixed_t,
    attention_weights,
    weights,
    up_bias,
    vectors,
    live,
    cotangent,
):
    length, width = low.shape
    parts, shards, _, rows, hidden = weights.shape
    xs = parts // 2
    whole = lambda shape: pl.BlockSpec(shape, lambda p, w, c: (0,) * len(shape))
    once = lambda shape: pl.BlockSpec(
        shape, lambda p, w, c: (0,) * len(shape), pipeline_mode=pl.Buffered(1)
    )
    wo_column = attention_weights.shape[1] // width - 1
    wide = (length, width)
    part_of = lambda w, c: 2 * lax.rem(w, xs) + jnp.where(w < xs, 1 - c[0], c[0])
    weight_spec = lambda which: pl.BlockSpec(
        (None, shards, None, rows, hidden), lambda p, w, c: (part_of(w, c), 0, which, 0, 0)
    )
    other_spec = pl.BlockSpec(
        (None, shards, rows, hidden), lambda p, w, c: (p * jnp.minimum(w, xs - 1), 0, 0, 0)
    )
    mine_spec = pl.BlockSpec(
        (None, shards, rows, hidden), lambda p, w, c: (p * jnp.maximum(w - xs, 0), 0, 0, 0)
    )
    grads = jax.ShapeDtypeStruct((xs, shards, rows, hidden), bf16)
    out, acc, up_other, up_mine, down_other, down_mine, dup_bias, dvec = pl.pallas_call(
        ffn_kernel,
        grid_spec=pltpu.PrefetchScalarGridSpec(
            num_scalar_prefetch=1,
            grid=(2, parts),
            in_specs=[
                once(wide),
                once((width, length)),
                once(wide),
                weight_spec(0),
                weight_spec(1),
                pl.BlockSpec((None, 1, hidden), lambda p, w, c: (part_of(w, c), 0, 0)),
                whole(vectors.shape),
                once((length, 1)),
                once(wide),
            ],
            out_specs=[
                whole(wide),
                whole(wide),
                other_spec,
                mine_spec,
                other_spec,
                mine_spec,
                pl.BlockSpec(
                    (None, 1, hidden), lambda p, w, c: (part_of(w * p, c), 0, 0)
                ),
                whole((8, width)),
            ],
            scratch_shapes=[
                pltpu.VMEM((parts, length, hidden), bf16),
                pltpu.VMEM((parts, length, hidden), f32),
                pltpu.VMEM(wide, bf16),
                pltpu.VMEM((width, length), bf16),
            ],
        ),
        out_shape=[
            jax.ShapeDtypeStruct(wide, bf16),
            jax.ShapeDtypeStruct(wide, f32),
            grads,
            grads,
            grads,
            grads,
            jax.ShapeDtypeStruct((parts, 1, hidden), f32),
            jax.ShapeDtypeStruct((8, width), f32),
        ],
        compiler_params=pltpu.CompilerParams(vmem_limit_bytes=58 * 1024 * 1024),
        cost_estimate=pl.CostEstimate(flops=0, bytes_accessed=0, transcendentals=0),
        name="feed_forward",
    )(
        place,
        low,
        low_t,
        xhat,
        weights,
        weights,
        up_bias,
        vectors,
        live,
        cotangent,
    )
    grad_one, gm, wo_other, wo_mine, dvec = pl.pallas_call(
        ffn_last_kernel,
        grid_spec=pltpu.PrefetchScalarGridSpec(
            num_scalar_prefetch=1,
            grid=(1,),
            in_specs=[
                pl.BlockSpec(wide, lambda i, c: (0, 0)),
                pl.BlockSpec(wide, lambda i, c: (0, 0)),
                pl.BlockSpec((length, 1), lambda i, c: (0, 0)),
                pl.BlockSpec((width, length), lambda i, c: (0, 0)),
                pl.BlockSpec((width, width), lambda i, c: (0, wo_column)),
                pl.BlockSpec(vectors.shape, lambda i, c: (0, 0)),
                pl.BlockSpec((8, width), lambda i, c: (0, 0)),
            ],
            out_specs=[
                pl.BlockSpec(wide, lambda i, c: (0, 0)),
                pl.BlockSpec(wide, lambda i, c: (0, 0)),
                pl.BlockSpec((width // 2, width), lambda i, c: (0, 0)),
                pl.BlockSpec((width // 2, width), lambda i, c: (0, 0)),
                pl.BlockSpec((8, width), lambda i, c: (0, 0)),
            ],
        ),
        out_shape=[
            jax.ShapeDtypeStruct(wide, f32),
            jax.ShapeDtypeStruct(wide, bf16),
            jax.ShapeDtypeStruct((width // 2, width), bf16),
            jax.ShapeDtypeStruct((width // 2, width), bf16),
            jax.ShapeDtypeStruct((8, width), f32),
        ],
        cost_estimate=pl.CostEstimate(flops=0, bytes_accessed=0, transcendentals=0),
        name="ffn_last",
    )(place, acc, xhat, inverse, mixed_t, attention_weights, vectors, dvec)
    return (
        out,
        grad_one,
        gm,
        up_other,
        up_mine,
        down_other,
        down_mine,
        wo_other,
        wo_mine,
        dup_bias,
        dvec,
    )


class Grid:
    def __init__(self, batch, wide):
        self.devices = batch * wide
        self.sizes = dict(z=4, y=batch // 4, x=wide // 2, c=2)
        self.strides = dict(z=batch // 4 * wide, y=wide, x=2, c=1)
        flat = lax.axis_index("batch") * wide + lax.axis_index("wide")
        self.place = {d: lax.rem(flat // self.strides[d], n) for d, n in self.sizes.items()}
        self.vector = jnp.stack([self.place[d] for d in "zyxc"])

    def shift(self, value, **offsets):
        pairs = []
        for i in range(self.devices):
            target = i
            for d, o in offsets.items():
                s, n = self.strides[d], self.sizes[d]
                target += ((i // s + o) % n - i // s % n) * s
            pairs.append((i, target))
        return lax.ppermute(value, ("batch", "wide"), pairs)

    def at(self, d, offset):
        return lax.rem(self.place[d] + (offset + self.sizes[d]), self.sizes[d])

    def block_at(self, d, offset):
        k, n = "zyxc".index(d), self.sizes[d]
        return lambda vector: lax.rem(vector[k] + offset, n)

    def offsets(self, dims):
        ranges = [range(self.sizes[d]) for d in dims]
        return [dict(zip(dims, o)) for o in itertools.product(*ranges)]

    def swap(self, value, dims):
        groups = {}
        for i in range(self.devices):
            key = tuple(i // self.strides[d] % n for d, n in self.sizes.items() if d not in dims)
            groups.setdefault(key, []).append(i)
        return lax.all_to_all(
            value, ("batch", "wide"), 0, 0, axis_index_groups=list(groups.values())
        )

    def gather(self, value, names, dims):
        parts = [(o, self.shift(value, **o) if any(o.values()) else value) for o in self.offsets(dims)]
        if len(parts) == 2:
            (d,) = dims
            own, other = value, parts[1][1]
            first = self.place[d] == 0
            return jnp.concatenate(
                [jnp.where(first, own, other), jnp.where(first, other, own)], axis=names.index(d)
            )
        shape = [self.sizes[d] if d in dims else n for d, n in zip(names, value.shape)]
        out = jnp.zeros(shape + list(value.shape[len(names) :]), value.dtype)
        for o, part in parts:
            start = [self.at(d, -o[d]) if d in dims else 0 for d in names]
            out = lax.dynamic_update_slice(out, part, start + [0] * (value.ndim - len(names)))
        return out

    def send(self, sends, dims):
        return [self.shift(value, **o) for o, value in zip(self.offsets(dims)[1:], sends)]


class Combine:
    def __init__(self, grid, steps):
        self.grid, self.steps = grid, steps
        self.inputs, self.in_specs, self.shapes, self.out_specs, self.terms = [], [], [], [], []

    def spec(self, block, where):
        picks = []
        for w in where:
            if w is None:
                picks.append(lambda i, v: 0)
            elif w == "step":
                picks.append(lambda i, v: i)
            else:
                at = self.grid.block_at(*w)
                picks.append(lambda i, v, at=at: at(v))
        return pl.BlockSpec(block, lambda i, v: tuple(p(i, v) for p in picks))

    def read(self, arrays, where):
        numbers = []
        for a in arrays:
            block = tuple(n if w is None else None for n, w in zip(a.shape, where))
            numbers.append(len(self.inputs))
            self.inputs.append(a)
            self.in_specs.append(self.spec(block, where))
        return numbers

    def add(self, addends, picks):
        numbers = []
        for names, array in addends:
            where = tuple(picks.get(d) for d in names)
            where = tuple((d, w) if isinstance(w, int) else w for d, w in zip(names, where))
            numbers += self.read([array], where + (None,) * (array.ndim - len(names)))
        return numbers

    def write(self, shape, dtype, terms, stepped=None):
        where = tuple("step" if n == stepped else None for n in range(len(shape)))
        block = tuple(n if w is None else None for n, w in zip(shape, where))
        self.shapes.append(jax.ShapeDtypeStruct(shape, dtype))
        self.out_specs.append(self.spec(block, where))
        self.terms.append(terms)

    def run(self, name):
        count = len(self.inputs)

        def kernel(vector_ref, *refs):
            for out_ref, terms in zip(refs[count:], self.terms):
                for target, *rest in terms:
                    total = None
                    for source, numbers in [rest] if len(rest) == 2 else rest[0]:
                        for n in numbers:
                            value = refs[n][source].astype(f32)
                            total = value if total is None else total + value
                    total = total.astype(out_ref.dtype)
                    if len(out_ref.shape) == 1:
                        total = total.reshape(out_ref.shape)
                    out_ref[target] = total

        return pl.pallas_call(
            kernel,
            grid_spec=pltpu.PrefetchScalarGridSpec(
                num_scalar_prefetch=1,
                grid=(self.steps,),
                in_specs=self.in_specs,
                out_specs=self.out_specs,
            ),
            out_shape=self.shapes,
            compiler_params=pltpu.CompilerParams(vmem_limit_bytes=63 * 1024 * 1024 + 900 * 1024),
            cost_estimate=pl.CostEstimate(flops=0, bytes_accessed=0, transcendentals=0),
            name=name,
        )(self.grid.vector, *self.inputs)


everything = (Ellipsis,)


def token_gradient_kernel(d_ref, w_ref, before_ref, out_ref):
    @pl.when(pl.program_id(0) == 0)
    def _():
        out_ref[...] = before_ref[...]

    out_ref[...] += dot_nt(d_ref[...], w_ref[...])


def token_gradient(dqkv, weights, before):
    length, width = before.shape
    parts = 3
    columns = dqkv.shape[1] // parts
    whole = pl.BlockSpec((length, width), lambda k: (0, 0))
    return pl.pallas_call(
        token_gradient_kernel,
        grid=(parts,),
        in_specs=[
            pl.BlockSpec((length, columns), lambda k: (0, k)),
            pl.BlockSpec((width, columns), lambda k: (0, k)),
            whole,
        ],
        out_specs=whole,
        out_shape=jax.ShapeDtypeStruct((length, width), f32),
        cost_estimate=pl.CostEstimate(flops=0, bytes_accessed=0, transcendentals=0),
        name="token_gradient",
    )(dqkv, weights, before)


def hold(value, *others):
    return lax.optimization_barrier((value, others))


def per_device(
    batch,
    wide,
    tokens,
    block_row,
    block_live,
    query_weight,
    key_weight,
    value_weight,
    out_weight,
    position_bias,
    features,
    up_weight,
    up_bias,
    down_weight,
    down_bias,
    gain_one,
    shift_one,
    gain_two,
    shift_two,
    cotangent,
):
    grid = Grid(batch, wide)
    zs, ys, xs, cs = (grid.sizes[d] for d in "zyxc")
    length, width = tokens.shape
    heads, rels = position_bias.shape
    pairs = heads // 2
    own = query_weight.shape[0]
    lanes = width // pairs
    ffn_shard = prepare_ffn(up_weight, down_weight)
    query_weight, (ffn_shard,) = hold(query_weight, ffn_shard)
    shard = prepare(query_weight, key_weight, value_weight, out_weight)
    up_rows, hidden = up_weight.shape
    half = 2 * width
    gathered = grid.gather(shard.reshape(1, 1, 1, 1, own, 4 * width), "zyxc", "z")
    first = grid.gather(gathered[..., :half], "zyxc", "x")
    second = grid.gather(gathered[..., half:], "zyxc", "y")
    inputs = (position_bias, features, block_row, block_live, tokens, down_bias)
    first, (second, *inputs) = hold(first, second, *inputs)
    position_bias, features, block_row, block_live, tokens, down_bias = inputs
    tables = toeplitz_tables(position_bias[:, ::-1])
    feat_forward, feat_back, swap, turn = feature_tables(features)
    offsets = jnp.arange(BLK, dtype=jnp.int32)
    live = (offsets[None, :] < block_live[:, None]).astype(f32).reshape(1, length)
    rows = jnp.broadcast_to(block_row[:, None], (block_row.shape[0], BLK)).reshape(1, length)
    mask = jnp.where(block_row[:, None] == rows, live, 0.0)
    by_core = lambda m: m.reshape(-1, cs, own, length).swapaxes(0, 1).reshape(width, length)
    tokens_t = by_core(tokens.T)
    vectors = jnp.stack([down_bias, gain_one, shift_one, gain_two, shift_two] + [down_bias] * 3)
    live_column = live.reshape(length, 1)

    first = grid.gather(first, "zyxc", "y")
    second = grid.gather(second, "zyxc", "x")
    early = (tables, feat_forward, feat_back, swap, turn, mask, tokens_t, vectors, live_column)
    first, (second, *early) = hold(first, second, *early)
    tables, feat_forward, feat_back, swap, turn, mask, tokens_t, vectors, live_column = early
    first = grid.gather(first, "zyxc", "c").reshape(width, half)
    second = grid.gather(second, "zyxc", "c").reshape(width, half)
    attention_weights = jnp.concatenate([first, second], axis=1)
    ffn_weights = lax.all_gather(ffn_shard, ("wide", "batch"), axis=0, tiled=False)
    ffn_weights = ffn_weights.reshape(wide, batch, 2, up_rows, hidden)
    mixed, mixed32, u, phi, value, inverse = attend(
        tokens, attention_weights, tables, mask, feat_forward, heads
    )
    place = grid.place["c"].reshape(1)
    normed = first_norm(tokens, mixed, attention_weights, vectors)
    normed, (mixed_t, grid.vector) = hold(normed, by_core(mixed.T), grid.vector)
    (
        out_tokens,
        grad_one,
        grad_mixed,
        up_other_grad,
        up_mine_grad,
        down_other,
        down_mine,
        out_other,
        out_mine,
        dup_bias,
        dvec,
    ) = feed_forward(
        place,
        *normed,
        mixed_t,
        attention_weights,
        ffn_weights,
        up_bias.reshape(wide, 1, hidden),
        vectors,
        live_column,
        cotangent,
    )
    ffn_view = lambda m: ("xzy", m.reshape(xs, zs, ys, up_rows, hidden))
    att_view = lambda m: ("zyx", m.reshape(zs, ys, xs, own, -1))
    down_recv = grid.shift(down_other, c=1)
    up = [ffn_view(up_mine_grad), ffn_view(grid.shift(up_other_grad, c=1))]
    out = [att_view(out_mine), att_view(grid.shift(out_other, c=1))]

    columns = 4 * width
    bias_rows = heads * rels // columns
    extra = -(-(3 + bias_rows) // 8) * 8
    first_row = extra - bias_rows
    down_mine, (grad_mixed,) = hold(down_mine, grad_mixed)
    down = [ffn_view(down_mine), ffn_view(down_recv)]

    step = Combine(grid, zs)
    for y in range(1, ys):
        terms = [(everything, everything, step.add(down, dict(z="step", y=y)))]
        step.write((xs, zs, up_rows, hidden), bf16, terms, stepped=1)
    for x in range(1, xs):
        terms = [(everything, everything, step.add(up, dict(z="step", x=x)))]
        step.write((zs, ys, up_rows, hidden), bf16, terms, stepped=0)
    sends = step.run("ffn_sum_core")
    down_sends, up_sends = sends[: ys - 1], sends[ys - 1 :]
    grad_mixed, (down_sends, up_sends, dup_bias, dvec) = hold(
        grad_mixed, down_sends, up_sends, dup_bias, dvec
    )
    small_top = jnp.concatenate(
        [dup_bias.reshape(1, columns), dvec.reshape(2, columns), jnp.zeros((extra - 3, columns), f32)]
    )
    down_new = grid.send(down_sends, "y")
    up_new = grid.send(up_sends, "x")

    dw_mine, dw_other, dqkv, small = attend_back(
        place,
        tokens_t,
        tables,
        mask,
        feat_back,
        swap,
        turn,
        u,
        phi,
        value,
        inverse,
        mixed32,
        grad_mixed,
        small_top,
        heads,
    )
    dw_mine, (dw_other, dqkv, small, down_new, up_new) = hold(
        dw_mine, dw_other, dqkv, small, down_new, up_new
    )
    down += [("xz", v) for v in down_new]
    up += [("zy", v) for v in up_new]
    att = [att_view(dw_mine), att_view(grid.shift(dw_other, c=1))]

    step = Combine(grid, 1)
    block = (zs, up_rows, hidden)
    for x in range(1, xs):
        terms = [(everything, everything, step.add(down, dict(y=0, x=x)))]
        step.write(block, bf16, terms)
    for y in range(1, ys):
        terms = [(everything, everything, step.add(up, dict(x=0, y=y)))]
        step.write(block, bf16, terms)
    sends = step.run("ffn_sum_plane")
    down_new = grid.send(sends[: xs - 1], "x")
    up_new = grid.send(sends[xs - 1 :], "y")
    small = small + grid.shift(small, c=1)
    small_new = grid.send([small.astype(bf16)] * (zs - 1), "z")
    dw_mine, sends = hold(dw_mine, *sends)
    att[0] = att_view(dw_mine)
    step = Combine(grid, 1)
    for o in grid.offsets("yx")[1:]:
        terms = [
            ((..., slice(0, 3 * width)), everything, step.add(att, o)),
            ((..., slice(3 * width, None)), everything, step.add(out, o)),
        ]
        step.write((zs, own, columns), bf16, terms)
    att_sends = step.run("att_sum_core")
    down_new, (up_new, att_sends, small_new) = hold(down_new, up_new, att_sends, small_new)
    down += [("z", v) for v in down_new]
    up += [("z", v) for v in up_new]
    small = (small + sum(v.astype(f32) for v in small_new)).astype(bf16)
    small = jnp.broadcast_to(small[None], (ys * xs,) + small.shape)
    att_new = grid.send(att_sends, "yx")

    here = dict(z=0, y=0, x=0)
    step = Combine(grid, 1)
    for z in range(1, zs):
        terms = [
            ((j,), everything, step.add(addends, dict(z=z, y=0, x=0)))
            for j, addends in enumerate((up, down))
        ]
        step.write((2, up_rows, hidden), bf16, terms)
    sends = step.run("ffn_sum_second")
    dqkv, (small, *sends) = hold(dqkv, small, *sends)
    small = grid.swap(small, "yx")
    ffn_new = grid.send(sends, "z")
    grad_tokens = token_gradient(dqkv, attention_weights, grad_one)
    att_new, (grad_tokens, *sends) = hold(att_new, grad_tokens, *sends)
    att_new = [("z", v) for v in att_new]

    step = Combine(grid, 1)
    for z in range(1, zs):
        picks = dict(z=z, y=0, x=0)
        top = slice(0, own)
        new = step.add(att_new, picks)
        head, tail = slice(0, 3 * width), slice(3 * width, None)
        terms = [
            ((top, head), everything, step.add(att, picks)),
            ((top, tail), everything, step.add(out, picks)),
        ]
        terms = [
            (target, [(everything, numbers), ((slice(None), target[1]), new)])
            for target, _, numbers in terms
        ]
        step.write((own, columns), bf16, terms)
    att_sends = step.run("att_sum_plane")
    last = grid.send(att_sends, "z")

    step = Combine(grid, 1)
    new = step.read(ffn_new, (None, None, None))
    for j, addends in enumerate((up, down)):
        terms = [(everything, [(everything, step.add(addends, here)), ((j,), new)])]
        step.write((up_rows, hidden), f32, terms)
    up_own, down_own = step.run("ffn_sum_last")

    step = Combine(grid, 1)
    new = step.add(att_new, here)
    head = (slice(None), slice(0, 3 * width))
    tail = (slice(None), slice(3 * width, None))
    top = slice(0, own)
    terms = [
        ((top, head[1]), [(everything, step.add(att, here)), (head, new)]),
        ((top, tail[1]), [(everything, step.add(out, here)), (tail, new)]),
    ]
    step.write((own, columns), f32, terms)
    small_in = step.read([small], (None, None, None))

    def small_term(r, cols):
        return [((k, slice(r, r + 1), cols), small_in) for k in range(ys * xs)]

    step.write((columns,), f32, [(everything, small_term(0, slice(None)))])
    for j in range(5):
        at = j % 4 * width
        step.write((width,), f32, [(everything, small_term(1 + j // 4, slice(at, at + width)))])
    per_row = columns // rels
    terms = []
    for h in range(heads):
        at = h % per_row * rels
        term = small_term(first_row + h // per_row, slice(at, at + rels))
        terms.append(((slice(h, h + 1),), term))
    step.write((heads, rels), f32, terms)
    before, dup_bias, *dvec, dbias = step.run("att_sum_own")

    step = Combine(grid, 1)
    last = step.read([before, *last], (None, None))
    for j in range(3):
        terms = []
        for p in range(pairs):
            cols = slice((3 * p + j) * lanes, (3 * p + j + 1) * lanes)
            terms.append(((slice(None), slice(p * lanes, (p + 1) * lanes)), (top, cols), last))
        step.write((own, width), f32, terms)
    step.write((own, width), f32, [(everything, (top, tail[1]), last)])

    dq, dk, dv, out_own = step.run("last_sum")
    return (
        out_tokens,
        grad_tokens,
        dq,
        dk,
        dv,
        out_own,
        dbias,
        up_own,
        dup_bias,
        down_own,
        *dvec,
    )


def solution(mesh):
    both = P(("batch", "wide"), None)
    placed = (
        both,
        P(("batch", "wide")),
        P(("batch", "wide")),
        both,
        both,
        both,
        both,
        P(),
        P(),
        P("batch", "wide"),
        P(),
        P("batch", "wide"),
        P(),
        P(),
        P(),
        P(),
        P(),
        both,
    )
    outs = (
        both,
        both,
        both,
        both,
        both,
        both,
        P(),
        P("batch", "wide"),
        P(),
        P("batch", "wide"),
        P(),
        P(),
        P(),
        P(),
        P(),
    )
    return jax.shard_map(
        partial(per_device, mesh.shape["batch"], mesh.shape["wide"]),
        mesh=mesh,
        in_specs=placed,
        out_specs=outs,
        check_vma=False,
    )
```
